256 devices in a mesh: blk: 128 (over x, z, y), pipe: 2 (over core).
Axes of the slice: x: 4, y: 4, z: 8, core: 2. Of those that a mesh axis runs over, the one named last changes fastest.
Arguments:
- endpoints: bfloat16 [2, 2, 12, 16384, 128], P('pipe', None, None, 'blk'), may hold values from -6 to 6
- row_counts: int32 [2], replicated, may hold values from 1 to 12, as said below
- layer_order: int32 [4], replicated, may hold values from 0 to 3, each once
- depth_weight: float32 [4, 3, 3, 128], replicated, may hold values from -2 to 2
- point_weight: bfloat16 [4, 128, 128], replicated, may hold values from -0.5 to 0.5
- point_bias: float32 [4, 128], replicated, may hold values from -3 to 3
Outputs:
- endpoints_out: bfloat16 [2, 2, 12, 16384, 128], P('pipe', None, None, 'blk')
- grad_depth: float32 [4, 3, 3, 128], replicated
- grad_point: float32 [4, 128, 128], replicated
- grad_bias: float32 [4, 128], replicated
The draws below stay inside these ranges and needn't reach their ends.
Inputs may be any that keep to these rules, and one draw needn't show every extreme that they name: `row_counts`: one of the two counts is 12. `layer_order`: a permutation of the layers.
All inputs are finite; a program needn't handle non-finite values.
Results may differ from the reference program's by a relative error of at most 0.013.
Values may be sent and summed in bfloat16 or wider, within the bound.
A program may use at most 64 MiB of HBM per device.

```python
import math
import jax
import jax.numpy as jnp
from jax import lax

C = 128
MICRO = 2
ROWS_MAX = 12
LAYERS = 4
ANGLES = 16384
N_PIPE = 2


def draw_row_counts(key, part):
    first_key, second_key = jax.random.split(jax.random.fold_in(key, 7))
    shorter = jax.random.randint(first_key, (), 1, ROWS_MAX)
    fullest = jax.random.randint(second_key, (), 0, MICRO)
    slots = jnp.arange(MICRO)
    return jnp.where(slots == fullest, ROWS_MAX, shorter).astype(jnp.int32)


def levels(stream_key, dims, cuts, low, largest):
    loudness, own = 1.0, jax.random.fold_in(stream_key, 6)
    for axis_at, shards_of in cuts:
        steps = jnp.exp(jax.random.uniform(jax.random.fold_in(own, axis_at), (shards_of,), jnp.float32, low / len(cuts), largest / len(cuts)))
        loudness = loudness * jnp.repeat(steps, dims[axis_at] // shards_of).reshape([-1 if axis == axis_at else 1 for axis in range(len(dims))])
    return loudness


def centred(key, extent, scale, limit, shards=(), dtype=jnp.bfloat16):
    result = scale * jax.random.normal(key, extent, jnp.float32)
    if shards:
        result = result * levels(key, extent, shards, -0.22, 0.18)
    return jnp.clip(result, -limit, limit).astype(dtype)


def setup_inputs(seed: int = 0) -> dict:
    seeds = jax.random.split(jax.random.key(seed), 7)
    return {
        "endpoints": centred(seeds[0], (N_PIPE, MICRO, ROWS_MAX, ANGLES, C), 1.0, 6.0, ((0, 2), (3, 128))),
        "row_counts": draw_row_counts(jax.random.fold_in(seeds[6], 71), 0),
        "layer_order": jax.random.permutation(seeds[2], LAYERS).astype(jnp.int32),
        "depth_weight": centred(seeds[3], (LAYERS, 3, 3, C), 9 ** -0.5, 2.0, (), jnp.float32),
        "point_weight": centred(seeds[4], (LAYERS, C, C), C ** -0.5, 0.5),
        "point_bias": centred(seeds[5], (LAYERS, C), 0.5, 3.0, (), jnp.float32),
    }


root_half = 0.7071067811865476
density_norm = 0.3989422804014327

def gelu_pair(preact):
    normal_cdf = 0.5 * (1.0 + lax.erf(preact * root_half))
    normal_pdf = density_norm * jnp.exp(-0.5 * preact * preact)
    return (preact * normal_cdf, normal_cdf + preact * normal_pdf)

def widen(activation):
    wrapped = jnp.concatenate([activation[:, -1:], activation, activation[:, :1]], axis=1)
    return jnp.pad(wrapped, ((1, 1), (0, 0), (0, 0)))

def mixing(padded, depth, point, offset_vec):
    height = padded.shape[0] - 2
    breadth = padded.shape[1] - 2
    channels = padded.shape[2]
    depthwise = jnp.zeros((height, breadth, channels), jnp.float32)
    for row_off in range(3):
        for col_off in range(3):
            depthwise = depthwise + depth[row_off, col_off] * padded[row_off:row_off + height, col_off:col_off + breadth].astype(jnp.float32)
    mixed_bf = depthwise.astype(jnp.bfloat16)
    preact = jnp.dot(mixed_bf.reshape(height * breadth, channels), point, preferred_element_type=jnp.float32)
    preact = preact.reshape(height, breadth, channels) + offset_vec
    return (mixed_bf, preact)

def retreat(cotangent, live_rows, depth, point, padded, mixed_bf, preact):
    height = padded.shape[0] - 2
    breadth = padded.shape[1] - 2
    channels = padded.shape[2]
    masked_grad = cotangent.astype(jnp.float32) * live_rows
    gated = (masked_grad * gelu_pair(preact)[1]).astype(jnp.bfloat16)
    flat_mix = mixed_bf.reshape(height * breadth, channels)
    flat_gate = gated.reshape(height * breadth, channels)
    point_term = lax.dot_general(flat_mix, flat_gate, (((0,), (0,)), ((), ())), preferred_element_type=jnp.float32)
    bias_term = lax.optimization_barrier(jnp.sum(gated.astype(jnp.float32), axis=(0, 1)))
    back_mix = lax.dot_general(flat_gate, point, (((1,), (1,)), ((), ())), preferred_element_type=jnp.float32)
    back_mix = back_mix.reshape(height, breadth, channels).astype(jnp.bfloat16)
    spread = widen(back_mix)
    back_float = back_mix.astype(jnp.float32)
    earlier = jnp.zeros((height, breadth, channels), jnp.float32)
    kernel_rows = []
    for row_off in range(3):
        kernel_row = []
        for col_off in range(3):
            kernel_row.append(lax.optimization_barrier(jnp.sum(back_float * padded[row_off:row_off + height, col_off:col_off + breadth].astype(jnp.float32), axis=(0, 1))))
            earlier = earlier + depth[row_off, col_off] * spread[2 - row_off:2 - row_off + height, 2 - col_off:2 - col_off + breadth].astype(jnp.float32)
        kernel_rows.append(jnp.stack(kernel_row))
    depth_term = jnp.stack(kernel_rows)
    previous = ((masked_grad + earlier) * live_rows).astype(jnp.bfloat16)
    return (previous, depth_term, point_term, bias_term)

def reference(endpoints, row_counts, layer_order, depth_weight, point_weight, point_bias):
    grad_depth = jnp.zeros(depth_weight.shape, jnp.float32)
    grad_point = jnp.zeros(point_weight.shape, jnp.float32)
    grad_bias = jnp.zeros(point_bias.shape, jnp.float32)
    outcomes = []
    input_grads = []
    for batch in range(MICRO):
        live_rows = (jnp.arange(ROWS_MAX)[:, None, None] < row_counts[batch]).astype(jnp.float32)
        activation = (endpoints[0, batch].astype(jnp.float32) * live_rows).astype(jnp.bfloat16)
        kept = []
        for position in range(LAYERS):
            layer_id = layer_order[position]
            depth = lax.dynamic_index_in_dim(depth_weight, layer_id, 0, keepdims=False)
            point = lax.dynamic_index_in_dim(point_weight, layer_id, 0, keepdims=False)
            offset_vec = lax.dynamic_index_in_dim(point_bias, layer_id, 0, keepdims=False)
            kept.append(activation)
            padded = widen(activation)
            mixed_bf, preact = mixing(padded, depth, point, offset_vec)
            activation = ((activation.astype(jnp.float32) + gelu_pair(preact)[0]) * live_rows).astype(jnp.bfloat16)
        outcomes.append(activation)
        cotangent = endpoints[1, batch]
        for position in range(LAYERS - 1, -1, -1):
            layer_id = layer_order[position]
            depth = lax.dynamic_index_in_dim(depth_weight, layer_id, 0, keepdims=False)
            point = lax.dynamic_index_in_dim(point_weight, layer_id, 0, keepdims=False)
            offset_vec = lax.dynamic_index_in_dim(point_bias, layer_id, 0, keepdims=False)
            padded = widen(kept[position])
            mixed_bf, preact = mixing(padded, depth, point, offset_vec)
            cotangent, depth_term, point_term, bias_term = retreat(cotangent, live_rows, depth, point, padded, mixed_bf, preact)
            grad_depth = grad_depth.at[layer_id].add(depth_term)
            grad_point = grad_point.at[layer_id].add(point_term)
            grad_bias = grad_bias.at[layer_id].add(bias_term)
        input_grads.append(cotangent)
    factor = 1.0 / math.sqrt(MICRO * ROWS_MAX * ANGLES)
    endpoints_out = jnp.stack([jnp.stack(input_grads), jnp.stack(outcomes)])
    return (endpoints_out, grad_depth * factor, grad_point * factor, grad_bias * factor)
```

```python
import math

import jax
import jax.numpy as jnp
from jax import lax
from jax.sharding import PartitionSpec as P

root_half = 0.7071067811865476
density_norm = 0.3989422804014327

X_HALO = 8
G_HALO = 4


def gelu_pair(preact):
    normal_cdf = 0.5 * (1.0 + lax.erf(preact * root_half))
    normal_pdf = density_norm * jnp.exp(-0.5 * preact * preact)
    return (preact * normal_cdf, normal_cdf + preact * normal_pdf)


def select_row(table, chosen):
    return lax.dynamic_index_in_dim(table, chosen, 0, keepdims=False)


def pad_rows(x):
    return jnp.pad(x, ((1, 1), (0, 0), (0, 0)))


def conv_forward(padded, depth):
    height = padded.shape[0] - 2
    breadth = padded.shape[1] - 2
    acc = jnp.zeros((height, breadth, padded.shape[2]), jnp.float32)
    for i in range(3):
        for j in range(3):
            acc = acc + depth[i, j] * padded[i : i + height, j : j + breadth].astype(jnp.float32)
    return acc


def conv_backward(spread, depth):
    height = spread.shape[0] - 2
    breadth = spread.shape[1] - 2
    acc = jnp.zeros((height, breadth, spread.shape[2]), jnp.float32)
    for i in range(3):
        for j in range(3):
            acc = acc + depth[i, j] * spread[
                2 - i : 2 - i + height, 2 - j : 2 - j + breadth
            ].astype(jnp.float32)
    return acc


def shards(endpoints, row_counts, layer_order, depth_weight, point_weight, point_bias):
    held = endpoints[0]
    height = held.shape[1]
    breadth = held.shape[2]
    channels = held.shape[3]
    layers = layer_order.shape[0]
    core = lax.axis_index("pipe")

    swap = [(0, 1), (1, 0)]
    sent = select_row(held, 1 - core)
    received = lax.ppermute(sent, "pipe", swap)
    mine = select_row(held, core)
    x_in = jnp.where(core == 0, mine, received)
    g_in = jnp.where(core == 0, received, mine)

    edge_x_hi = x_in[:, breadth - X_HALO :]
    edge_x_lo = x_in[:, :X_HALO]
    edge_g_hi = g_in[:, breadth - G_HALO :]
    edge_g_lo = g_in[:, :G_HALO]
    size = lax.axis_size("blk")
    up = [(i, (i + 1) % size) for i in range(size)]
    down = [(j, i) for i, j in up]
    from_left = lax.ppermute(jnp.concatenate([edge_x_hi, edge_g_hi], axis=1), "blk", up)
    from_right = lax.ppermute(jnp.concatenate([edge_x_lo, edge_g_lo], axis=1), "blk", down)
    x_wide = jnp.concatenate([from_left[:, :X_HALO], x_in, from_right[:, :X_HALO]], axis=1)
    g_wide = jnp.concatenate([from_left[:, X_HALO:], g_in, from_right[:, X_HALO:]], axis=1)

    live = (jnp.arange(height)[:, None, None] < select_row(row_counts, core)).astype(jnp.float32)

    weights = []
    for p in range(layers):
        w = layer_order[p]
        weights.append(
            (select_row(depth_weight, w), select_row(point_weight, w), select_row(point_bias, w))
        )

    activation = (x_wide.astype(jnp.float32) * live).astype(jnp.bfloat16)
    acts, mixes, preacts = [], [], []
    for p in range(layers):
        depth, point, offset_vec = weights[p]
        acts.append(activation)
        mixed = conv_forward(pad_rows(activation), depth).astype(jnp.bfloat16)
        rows, span = mixed.shape[0], mixed.shape[1]
        preact = jnp.dot(
            mixed.reshape(rows * span, channels), point, preferred_element_type=jnp.float32
        ).reshape(rows, span, channels) + offset_vec
        mixes.append(mixed)
        preacts.append(preact)
        activation = (
            (activation[:, 1:-1].astype(jnp.float32) + gelu_pair(preact)[0]) * live
        ).astype(jnp.bfloat16)
    final_halo = X_HALO - layers
    outcome = activation[:, final_halo : final_halo + breadth]

    cotangent = g_wide
    depth_terms, point_terms, bias_terms = [None] * layers, [None] * layers, [None] * layers
    for p in range(layers - 1, -1, -1):
        depth, point, _ = weights[p]
        halo_c = (cotangent.shape[1] - breadth) // 2
        halo_p = (preacts[p].shape[1] - breadth) // 2
        shift = halo_p - halo_c
        span = cotangent.shape[1]
        preact = preacts[p][:, shift : shift + span]
        masked = cotangent.astype(jnp.float32) * live
        gated = (masked * gelu_pair(preact)[1]).astype(jnp.bfloat16)
        back_mix = lax.dot_general(
            gated.reshape(height * span, channels),
            point,
            (((1,), (1,)), ((), ())),
            preferred_element_type=jnp.float32,
        ).reshape(height, span, channels).astype(jnp.bfloat16)

        gate_in = gated[:, halo_c : halo_c + breadth].reshape(height * breadth, channels)
        mix_in = mixes[p][:, halo_p : halo_p + breadth].reshape(height * breadth, channels)
        point_terms[p] = lax.dot_general(
            mix_in, gate_in, (((0,), (0,)), ((), ())), preferred_element_type=jnp.float32
        )
        bias_terms[p] = jnp.sum(gate_in.astype(jnp.float32), axis=0)
        back_in = back_mix[:, halo_c : halo_c + breadth].astype(jnp.float32)
        padded = pad_rows(acts[p])
        halo_a = (acts[p].shape[1] - breadth) // 2
        rows_k = []
        for i in range(3):
            row_k = []
            for j in range(3):
                start = halo_a - 1 + j
                row_k.append(
                    jnp.sum(
                        back_in * padded[i : i + height, start : start + breadth].astype(jnp.float32),
                        axis=(0, 1),
                    )
                )
            rows_k.append(jnp.stack(row_k))
        depth_terms[p] = jnp.stack(rows_k)

        earlier = conv_backward(pad_rows(back_mix), depth)
        cotangent = ((masked[:, 1:-1] + earlier) * live).astype(jnp.bfloat16)
    input_grad = cotangent

    got_outcome = lax.ppermute(outcome, "pipe", [(0, 1)])
    got_grad = lax.ppermute(input_grad, "pipe", [(1, 0)])
    first = jnp.where(core == 0, input_grad, got_outcome)
    second = jnp.where(core == 0, got_grad, outcome)
    result = jnp.stack([first, second])[None]

    totals = (jnp.stack(depth_terms), jnp.stack(point_terms), jnp.stack(bias_terms))
    summed = lax.psum(totals, ("blk", "pipe"))
    inverse = jnp.zeros((layers,), jnp.int32).at[layer_order].set(jnp.arange(layers, dtype=jnp.int32))
    factor = 1.0 / math.sqrt(held.shape[0] * height * breadth * lax.axis_size("blk"))
    ordered = tuple(jnp.take(s, inverse, axis=0) * factor for s in summed)
    return (result, ordered[0], ordered[1], ordered[2])


def solution(mesh):
    in_specs = (P("pipe", None, None, "blk", None), P(), P(), P(), P(), P())
    out_specs = (P("pipe", None, None, "blk", None), P(), P(), P())
    return jax.shard_map(shards, mesh=mesh, in_specs=in_specs, out_specs=out_specs, check_vma=False)
```

```python
import math

import jax
import jax.numpy as jnp
from jax import lax
from jax.sharding import Mesh, PartitionSpec as P

root_half = 0.7071067811865476
density_norm = 0.3989422804014327

X_HALO = 8
G_HALO = 4


BLK_AXES = ("x", "z", "y")


def blk_count():
    count = 1
    for axis in BLK_AXES:
        count *= lax.axis_size(axis)
    return count


def gelu_pair(preact):
    normal_cdf = 0.5 * (1.0 + lax.erf(preact * root_half))
    normal_pdf = density_norm * jnp.exp(-0.5 * preact * preact)
    return (preact * normal_cdf, normal_cdf + preact * normal_pdf)


def select_row(table, chosen):
    return lax.dynamic_index_in_dim(table, chosen, 0, keepdims=False)


def pad_rows(x):
    return jnp.pad(x, ((1, 1), (0, 0), (0, 0)))


def conv_forward(padded, depth):
    height = padded.shape[0] - 2
    breadth = padded.shape[1] - 2
    acc = jnp.zeros((height, breadth, padded.shape[2]), jnp.float32)
    for i in range(3):
        for j in range(3):
            acc = acc + depth[i, j] * padded[i : i + height, j : j + breadth].astype(jnp.float32)
    return acc


def conv_backward(spread, depth):
    height = spread.shape[0] - 2
    breadth = spread.shape[1] - 2
    acc = jnp.zeros((height, breadth, spread.shape[2]), jnp.float32)
    for i in range(3):
        for j in range(3):
            acc = acc + depth[i, j] * spread[
                2 - i : 2 - i + height, 2 - j : 2 - j + breadth
            ].astype(jnp.float32)
    return acc


def shards(endpoints, row_counts, layer_order, depth_weight, point_weight, point_bias):
    held = endpoints[0]
    height = held.shape[1]
    breadth = held.shape[2]
    channels = held.shape[3]
    layers = layer_order.shape[0]
    core = lax.axis_index("pipe")

    swap = [(0, 1), (1, 0)]
    sent = select_row(held, 1 - core)
    received = lax.ppermute(sent, "pipe", swap)
    mine = select_row(held, core)
    x_in = jnp.where(core == 0, mine, received)
    g_in = jnp.where(core == 0, received, mine)

    edge_x_hi = x_in[:, breadth - X_HALO :]
    edge_x_lo = x_in[:, :X_HALO]
    edge_g_hi = g_in[:, breadth - G_HALO :]
    edge_g_lo = g_in[:, :G_HALO]
    size = blk_count()
    up = [(i, (i + 1) % size) for i in range(size)]
    down = [(j, i) for i, j in up]
    from_left = lax.ppermute(jnp.concatenate([edge_x_hi, edge_g_hi], axis=1), BLK_AXES, up)
    from_right = lax.ppermute(jnp.concatenate([edge_x_lo, edge_g_lo], axis=1), BLK_AXES, down)
    x_wide = jnp.concatenate([from_left[:, :X_HALO], x_in, from_right[:, :X_HALO]], axis=1)
    g_wide = jnp.concatenate([from_left[:, X_HALO:], g_in, from_right[:, X_HALO:]], axis=1)

    live = (jnp.arange(height)[:, None, None] < select_row(row_counts, core)).astype(jnp.float32)

    weights = []
    for p in range(layers):
        w = layer_order[p]
        weights.append(
            (select_row(depth_weight, w), select_row(point_weight, w), select_row(point_bias, w))
        )

    activation = (x_wide.astype(jnp.float32) * live).astype(jnp.bfloat16)
    acts, mixes, preacts = [], [], []
    for p in range(layers):
        depth, point, offset_vec = weights[p]
        acts.append(activation)
        mixed = conv_forward(pad_rows(activation), depth).astype(jnp.bfloat16)
        rows, span = mixed.shape[0], mixed.shape[1]
        preact = jnp.dot(
            mixed.reshape(rows * span, channels), point, preferred_element_type=jnp.float32
        ).reshape(rows, span, channels) + offset_vec
        mixes.append(mixed)
        preacts.append(preact)
        activation = (
            (activation[:, 1:-1].astype(jnp.float32) + gelu_pair(preact)[0]) * live
        ).astype(jnp.bfloat16)
    final_halo = X_HALO - layers
    outcome = activation[:, final_halo : final_halo + breadth]

    cotangent = g_wide
    depth_terms, point_terms, bias_terms = [None] * layers, [None] * layers, [None] * layers
    for p in range(layers - 1, -1, -1):
        depth, point, _ = weights[p]
        halo_c = (cotangent.shape[1] - breadth) // 2
        halo_p = (preacts[p].shape[1] - breadth) // 2
        shift = halo_p - halo_c
        span = cotangent.shape[1]
        preact = preacts[p][:, shift : shift + span]
        masked = cotangent.astype(jnp.float32) * live
        gated = (masked * gelu_pair(preact)[1]).astype(jnp.bfloat16)
        back_mix = lax.dot_general(
            gated.reshape(height * span, channels),
            point,
            (((1,), (1,)), ((), ())),
            preferred_element_type=jnp.float32,
        ).reshape(height, span, channels).astype(jnp.bfloat16)

        gate_in = gated[:, halo_c : halo_c + breadth].reshape(height * breadth, channels)
        mix_in = mixes[p][:, halo_p : halo_p + breadth].reshape(height * breadth, channels)
        point_terms[p] = lax.dot_general(
            mix_in, gate_in, (((0,), (0,)), ((), ())), preferred_element_type=jnp.float32
        )
        bias_terms[p] = jnp.sum(gate_in.astype(jnp.float32), axis=0)
        back_in = back_mix[:, halo_c : halo_c + breadth].astype(jnp.float32)
        padded = pad_rows(acts[p])
        halo_a = (acts[p].shape[1] - breadth) // 2
        rows_k = []
        for i in range(3):
            row_k = []
            for j in range(3):
                start = halo_a - 1 + j
                row_k.append(
                    jnp.sum(
                        back_in * padded[i : i + height, start : start + breadth].astype(jnp.float32),
                        axis=(0, 1),
                    )
                )
            rows_k.append(jnp.stack(row_k))
        depth_terms[p] = jnp.stack(rows_k)

        earlier = conv_backward(pad_rows(back_mix), depth)
        cotangent = ((masked[:, 1:-1] + earlier) * live).astype(jnp.bfloat16)
    input_grad = cotangent

    got_outcome = lax.ppermute(outcome, "pipe", [(0, 1)])
    got_grad = lax.ppermute(input_grad, "pipe", [(1, 0)])
    first = jnp.where(core == 0, input_grad, got_outcome)
    second = jnp.where(core == 0, got_grad, outcome)
    result = jnp.stack([first, second])[None]

    pieces = (jnp.stack(depth_terms), jnp.stack(point_terms), jnp.stack(bias_terms))
    flat = jnp.concatenate([piece.reshape(layers, -1) for piece in pieces], axis=1)
    for axis in ("pipe",) + BLK_AXES:
        flat = lax.psum(flat, axis)
    inverse = jnp.zeros((layers,), jnp.int32).at[layer_order].set(jnp.arange(layers, dtype=jnp.int32))
    factor = 1.0 / math.sqrt(held.shape[0] * height * breadth * blk_count())
    flat = jnp.take(flat, inverse, axis=0) * factor
    ordered, at = [], 0
    for piece in pieces:
        width = piece[0].size
        ordered.append(flat[:, at : at + width].reshape(piece.shape))
        at += width
    return (result, ordered[0], ordered[1], ordered[2])


def solution(mesh):
    devices = mesh.devices
    blk = devices.shape[0]
    y_size = 4 if blk % 4 == 0 else 1
    rest = blk // y_size
    z_size = 8 if rest % 8 == 0 else rest
    x_size = rest // z_size
    torus = Mesh(devices.reshape(x_size, z_size, y_size, devices.shape[1]), BLK_AXES + ("pipe",))
    spec = P("pipe", None, None, BLK_AXES, None)
    in_specs = (spec, P(), P(), P(), P(), P())
    out_specs = (spec, P(), P(), P())
    return jax.shard_map(shards, mesh=torus, in_specs=in_specs, out_specs=out_specs, check_vma=False)
```

```python
import math

import jax
import jax.numpy as jnp
from jax import lax
from jax.sharding import Mesh, PartitionSpec as P

root_half = 0.7071067811865476
density_norm = 0.3989422804014327

X_HALO = 8
G_HALO = 4


BLK_AXES = ("x", "z", "y")


def blk_count():
    count = 1
    for axis in BLK_AXES:
        count *= lax.axis_size(axis)
    return count


def gelu_pair(preact):
    normal_cdf = 0.5 * (1.0 + lax.erf(preact * root_half))
    normal_pdf = density_norm * jnp.exp(-0.5 * preact * preact)
    return (preact * normal_cdf, normal_cdf + preact * normal_pdf)


def select_row(table, chosen):
    return lax.dynamic_index_in_dim(table, chosen, 0, keepdims=False)


def pad_rows(x):
    return jnp.pad(x, ((1, 1), (0, 0), (0, 0)))


def conv_forward(padded, depth):
    height = padded.shape[0] - 2
    breadth = padded.shape[1] - 2
    acc = jnp.zeros((height, breadth, padded.shape[2]), jnp.float32)
    for i in range(3):
        for j in range(3):
            acc = acc + depth[i, j] * padded[i : i + height, j : j + breadth].astype(jnp.float32)
    return acc


def conv_backward(spread, depth):
    height = spread.shape[0] - 2
    breadth = spread.shape[1] - 2
    acc = jnp.zeros((height, breadth, spread.shape[2]), jnp.float32)
    for i in range(3):
        for j in range(3):
            acc = acc + depth[i, j] * spread[
                2 - i : 2 - i + height, 2 - j : 2 - j + breadth
            ].astype(jnp.float32)
    return acc


def all_reduce(flat, core):
    half = flat.shape[1] // 2
    swap = [(0, 1), (1, 0)]
    mine = lax.dynamic_slice_in_dim(flat, core * half, half, axis=1)
    other = lax.dynamic_slice_in_dim(flat, (1 - core) * half, half, axis=1)
    acc = mine + lax.ppermute(other, "pipe", swap)
    for axis in ("y", "z", "x"):
        size = lax.axis_size(axis)
        bit = 1
        while bit < size:
            pairs = [(i, i ^ bit) for i in range(size)]
            acc = acc + lax.ppermute(acc, axis, pairs)
            bit *= 2
    theirs = lax.ppermute(acc, "pipe", swap)
    low = jnp.where(core == 0, acc, theirs)
    high = jnp.where(core == 0, theirs, acc)
    return jnp.concatenate([low, high], axis=1)


def shards(endpoints, row_counts, layer_order, depth_weight, point_weight, point_bias):
    held = endpoints[0]
    height = held.shape[1]
    breadth = held.shape[2]
    channels = held.shape[3]
    layers = layer_order.shape[0]
    core = lax.axis_index("pipe")

    swap = [(0, 1), (1, 0)]
    sent = select_row(held, 1 - core)
    received = lax.ppermute(sent, "pipe", swap)
    mine = select_row(held, core)
    x_in = jnp.where(core == 0, mine, received)
    g_in = jnp.where(core == 0, received, mine)

    edge_x_hi = x_in[:, breadth - X_HALO :]
    edge_x_lo = x_in[:, :X_HALO]
    edge_g_hi = g_in[:, breadth - G_HALO :]
    edge_g_lo = g_in[:, :G_HALO]
    size = blk_count()
    up = [(i, (i + 1) % size) for i in range(size)]
    down = [(j, i) for i, j in up]
    from_left = lax.ppermute(jnp.concatenate([edge_x_hi, edge_g_hi], axis=1), BLK_AXES, up)
    from_right = lax.ppermute(jnp.concatenate([edge_x_lo, edge_g_lo], axis=1), BLK_AXES, down)
    x_wide = jnp.concatenate([from_left[:, :X_HALO], x_in, from_right[:, :X_HALO]], axis=1)
    g_wide = jnp.concatenate([from_left[:, X_HALO:], g_in, from_right[:, X_HALO:]], axis=1)

    live = (jnp.arange(height)[:, None, None] < select_row(row_counts, core)).astype(jnp.float32)

    weights = []
    for p in range(layers):
        w = layer_order[p]
        weights.append(
            (select_row(depth_weight, w), select_row(point_weight, w), select_row(point_bias, w))
        )

    activation = (x_wide.astype(jnp.float32) * live).astype(jnp.bfloat16)
    acts, mixes, preacts = [], [], []
    for p in range(layers):
        depth, point, offset_vec = weights[p]
        acts.append(activation)
        mixed = conv_forward(pad_rows(activation), depth).astype(jnp.bfloat16)
        rows, span = mixed.shape[0], mixed.shape[1]
        preact = jnp.dot(
            mixed.reshape(rows * span, channels), point, preferred_element_type=jnp.float32
        ).reshape(rows, span, channels) + offset_vec
        mixes.append(mixed)
        preacts.append(preact)
        activation = (
            (activation[:, 1:-1].astype(jnp.float32) + gelu_pair(preact)[0]) * live
        ).astype(jnp.bfloat16)
    final_halo = X_HALO - layers
    outcome = activation[:, final_halo : final_halo + breadth]

    cotangent = g_wide
    depth_terms, point_terms, bias_terms = [None] * layers, [None] * layers, [None] * layers
    for p in range(layers - 1, -1, -1):
        depth, point, _ = weights[p]
        halo_c = (cotangent.shape[1] - breadth) // 2
        halo_p = (preacts[p].shape[1] - breadth) // 2
        shift = halo_p - halo_c
        span = cotangent.shape[1]
        preact = preacts[p][:, shift : shift + span]
        masked = cotangent.astype(jnp.float32) * live
        gated = (masked * gelu_pair(preact)[1]).astype(jnp.bfloat16)
        back_mix = lax.dot_general(
            gated.reshape(height * span, channels),
            point,
            (((1,), (1,)), ((), ())),
            preferred_element_type=jnp.float32,
        ).reshape(height, span, channels).astype(jnp.bfloat16)

        gate_in = gated[:, halo_c : halo_c + breadth].reshape(height * breadth, channels)
        mix_in = mixes[p][:, halo_p : halo_p + breadth].reshape(height * breadth, channels)
        point_terms[p] = lax.dot_general(
            mix_in, gate_in, (((0,), (0,)), ((), ())), preferred_element_type=jnp.float32
        )
        bias_terms[p] = jnp.sum(gate_in.astype(jnp.float32), axis=0)
        back_in = back_mix[:, halo_c : halo_c + breadth].astype(jnp.float32)
        padded = pad_rows(acts[p])
        halo_a = (acts[p].shape[1] - breadth) // 2
        rows_k = []
        for i in range(3):
            row_k = []
            for j in range(3):
                start = halo_a - 1 + j
                row_k.append(
                    jnp.sum(
                        back_in * padded[i : i + height, start : start + breadth].astype(jnp.float32),
                        axis=(0, 1),
                    )
                )
            rows_k.append(jnp.stack(row_k))
        depth_terms[p] = jnp.stack(rows_k)

        earlier = conv_backward(pad_rows(back_mix), depth)
        cotangent = ((masked[:, 1:-1] + earlier) * live).astype(jnp.bfloat16)
    input_grad = cotangent

    got_outcome = lax.ppermute(outcome, "pipe", [(0, 1)])
    got_grad = lax.ppermute(input_grad, "pipe", [(1, 0)])
    first = jnp.where(core == 0, input_grad, got_outcome)
    second = jnp.where(core == 0, got_grad, outcome)
    result = jnp.stack([first, second])[None]

    pieces = (jnp.stack(depth_terms), jnp.stack(point_terms), jnp.stack(bias_terms))
    flat = jnp.concatenate([piece.reshape(layers, -1) for piece in pieces], axis=1)
    flat = all_reduce(flat, core)
    inverse = jnp.zeros((layers,), jnp.int32).at[layer_order].set(jnp.arange(layers, dtype=jnp.int32))
    factor = 1.0 / math.sqrt(held.shape[0] * height * breadth * blk_count())
    flat = jnp.take(flat, inverse, axis=0) * factor
    ordered, at = [], 0
    for piece in pieces:
        width = piece[0].size
        ordered.append(flat[:, at : at + width].reshape(piece.shape))
        at += width
    return (result, ordered[0], ordered[1], ordered[2])


def solution(mesh):
    devices = mesh.devices
    blk = devices.shape[0]
    y_size = 4 if blk % 4 == 0 else 1
    rest = blk // y_size
    z_size = 8 if rest % 8 == 0 else rest
    x_size = rest // z_size
    torus = Mesh(devices.reshape(x_size, z_size, y_size, devices.shape[1]), BLK_AXES + ("pipe",))
    spec = P("pipe", None, None, BLK_AXES, None)
    in_specs = (spec, P(), P(), P(), P(), P())
    out_specs = (spec, P(), P(), P())
    return jax.shard_map(shards, mesh=torus, in_specs=in_specs, out_specs=out_specs, check_vma=False)
```

```python
import math

import jax
import jax.numpy as jnp
from jax import lax
from jax.experimental import pallas as pl
from jax.experimental.pallas import tpu as pltpu
from jax.sharding import Mesh, PartitionSpec as P

MESH_ID = pl.DeviceIdType.MESH

root_half = 0.7071067811865476
density_norm = 0.3989422804014327

X_HALO = 8
G_HALO = 4


BLK_AXES = ("x", "z", "y")


def blk_count():
    count = 1
    for axis in BLK_AXES:
        count *= lax.axis_size(axis)
    return count


def gelu_pair(preact):
    normal_cdf = 0.5 * (1.0 + lax.erf(preact * root_half))
    normal_pdf = density_norm * jnp.exp(-0.5 * preact * preact)
    return (preact * normal_cdf, normal_cdf + preact * normal_pdf)


def select_row(table, chosen):
    return lax.dynamic_index_in_dim(table, chosen, 0, keepdims=False)


def pad_rows(x):
    return jnp.pad(x, ((1, 1), (0, 0), (0, 0)))


def conv_forward(padded, depth):
    height = padded.shape[0] - 2
    breadth = padded.shape[1] - 2
    acc = jnp.zeros((height, breadth, padded.shape[2]), jnp.float32)
    for i in range(3):
        for j in range(3):
            acc = acc + depth[i, j] * padded[i : i + height, j : j + breadth].astype(jnp.float32)
    return acc


def conv_backward(spread, depth):
    height = spread.shape[0] - 2
    breadth = spread.shape[1] - 2
    acc = jnp.zeros((height, breadth, spread.shape[2]), jnp.float32)
    for i in range(3):
        for j in range(3):
            acc = acc + depth[i, j] * spread[
                2 - i : 2 - i + height, 2 - j : 2 - j + breadth
            ].astype(jnp.float32)
    return acc


def torus_coords(b):
    y_size, z_size = lax.axis_size("y"), lax.axis_size("z")
    return (b // (y_size * z_size), lax.rem(b // y_size, z_size), lax.rem(b, y_size))


def exchange_kernel(held_ref, edges_ref, body_out, lo_out, hi_out, body, lo, hi, send_sem, recv_sem):
    core = lax.axis_index("pipe")
    count = blk_count()
    here = (lax.axis_index("x") * lax.axis_size("z") + lax.axis_index("z")) * lax.axis_size("y") + lax.axis_index("y")
    right = torus_coords(lax.rem(here + 1, count))
    left = torus_coords(lax.rem(here + count - 1, count))
    mine = torus_coords(here)
    partner = mine + (1 - core,)
    targets = [partner] + [right + (m,) for m in range(2)] + [left + (m,) for m in range(2)]

    barrier = pltpu.get_barrier_semaphore()
    for target in targets:
        pl.semaphore_signal(barrier, inc=1, device_id=target, device_id_type=MESH_ID)
    pl.semaphore_wait(barrier, len(targets))

    copies = [
        pltpu.make_async_remote_copy(
            src_ref=held_ref.at[1 - core], dst_ref=body,
            send_sem=send_sem.at[0], recv_sem=recv_sem.at[0],
            device_id=partner, device_id_type=MESH_ID,
        )
    ]
    for m in range(2):
        copies.append(pltpu.make_async_remote_copy(
            src_ref=edges_ref.at[1, m], dst_ref=lo.at[core],
            send_sem=send_sem.at[1 + m], recv_sem=recv_sem.at[1 + core],
            device_id=right + (m,), device_id_type=MESH_ID,
        ))
        copies.append(pltpu.make_async_remote_copy(
            src_ref=edges_ref.at[0, m], dst_ref=hi.at[core],
            send_sem=send_sem.at[3 + m], recv_sem=recv_sem.at[3 + core],
            device_id=left + (m,), device_id_type=MESH_ID,
        ))
    for copy in copies:
        copy.start()
    copies[0].wait_recv()
    for k in range(2):
        pltpu.make_async_remote_copy(
            src_ref=edges_ref.at[1, k], dst_ref=lo.at[k],
            send_sem=send_sem.at[1 + k], recv_sem=recv_sem.at[1 + k],
            device_id=right + (k,), device_id_type=MESH_ID,
        ).wait_recv()
        pltpu.make_async_remote_copy(
            src_ref=edges_ref.at[0, k], dst_ref=hi.at[k],
            send_sem=send_sem.at[3 + k], recv_sem=recv_sem.at[3 + k],
            device_id=left + (k,), device_id_type=MESH_ID,
        ).wait_recv()
    for copy in copies:
        copy.wait_send()
    body_out[...] = body[...]
    lo_out[...] = lo[...]
    hi_out[...] = hi[...]


def exchange(held, edges):
    grid_shape = held.shape[1:]
    strip_shape = edges.shape[2:]
    vmem = pl.BlockSpec(memory_space=pltpu.VMEM)
    return pl.pallas_call(
        exchange_kernel,
        out_shape=(
            jax.ShapeDtypeStruct(grid_shape, held.dtype),
            jax.ShapeDtypeStruct((2,) + strip_shape, held.dtype),
            jax.ShapeDtypeStruct((2,) + strip_shape, held.dtype),
        ),
        in_specs=[vmem, vmem],
        out_specs=(vmem, vmem, vmem),
        scratch_shapes=[
            pltpu.VMEM(grid_shape, held.dtype),
            pltpu.VMEM((2,) + strip_shape, held.dtype),
            pltpu.VMEM((2,) + strip_shape, held.dtype),
            pltpu.SemaphoreType.DMA((5,)),
            pltpu.SemaphoreType.DMA((5,)),
        ],
        compiler_params=pltpu.CompilerParams(collective_id=0, has_side_effects=True),
    )(held, edges)


def all_reduce(flat, core):
    half = flat.shape[1] // 2
    swap = [(0, 1), (1, 0)]
    mine = lax.dynamic_slice_in_dim(flat, core * half, half, axis=1)
    other = lax.dynamic_slice_in_dim(flat, (1 - core) * half, half, axis=1)
    acc = mine + lax.ppermute(other, "pipe", swap)
    for axis in ("y", "z", "x"):
        size = lax.axis_size(axis)
        bit = 1
        while bit < size:
            pairs = [(i, i ^ bit) for i in range(size)]
            acc = acc + lax.ppermute(acc, axis, pairs)
            bit *= 2
    theirs = lax.ppermute(acc, "pipe", swap)
    low = jnp.where(core == 0, acc, theirs)
    high = jnp.where(core == 0, theirs, acc)
    return jnp.concatenate([low, high], axis=1)


def shards(endpoints, row_counts, layer_order, depth_weight, point_weight, point_bias):
    held = endpoints[0]
    height = held.shape[1]
    breadth = held.shape[2]
    channels = held.shape[3]
    layers = layer_order.shape[0]
    core = lax.axis_index("pipe")

    edges = jnp.stack([held[:, :, :X_HALO], held[:, :, breadth - X_HALO :]])
    body, lo, hi = exchange(held, edges)
    mine = select_row(held, core)
    x_in = jnp.where(core == 0, mine, body)
    g_in = jnp.where(core == 0, body, mine)
    x_wide = jnp.concatenate([lo[0], x_in, hi[0]], axis=1)
    g_wide = jnp.concatenate([lo[1][:, X_HALO - G_HALO :], g_in, hi[1][:, :G_HALO]], axis=1)

    live = (jnp.arange(height)[:, None, None] < select_row(row_counts, core)).astype(jnp.float32)

    weights = []
    for p in range(layers):
        w = layer_order[p]
        weights.append(
            (select_row(depth_weight, w), select_row(point_weight, w), select_row(point_bias, w))
        )

    activation = (x_wide.astype(jnp.float32) * live).astype(jnp.bfloat16)
    acts, mixes, preacts = [], [], []
    for p in range(layers):
        depth, point, offset_vec = weights[p]
        acts.append(activation)
        mixed = conv_forward(pad_rows(activation), depth).astype(jnp.bfloat16)
        rows, span = mixed.shape[0], mixed.shape[1]
        preact = jnp.dot(
            mixed.reshape(rows * span, channels), point, preferred_element_type=jnp.float32
        ).reshape(rows, span, channels) + offset_vec
        mixes.append(mixed)
        preacts.append(preact)
        activation = (
            (activation[:, 1:-1].astype(jnp.float32) + gelu_pair(preact)[0]) * live
        ).astype(jnp.bfloat16)
    final_halo = X_HALO - layers
    outcome = activation[:, final_halo : final_halo + breadth]

    cotangent = g_wide
    depth_terms, point_terms, bias_terms = [None] * layers, [None] * layers, [None] * layers
    for p in range(layers - 1, -1, -1):
        depth, point, _ = weights[p]
        halo_c = (cotangent.shape[1] - breadth) // 2
        halo_p = (preacts[p].shape[1] - breadth) // 2
        shift = halo_p - halo_c
        span = cotangent.shape[1]
        preact = preacts[p][:, shift : shift + span]
        masked = cotangent.astype(jnp.float32) * live
        gated = (masked * gelu_pair(preact)[1]).astype(jnp.bfloat16)
        back_mix = lax.dot_general(
            gated.reshape(height * span, channels),
            point,
            (((1,), (1,)), ((), ())),
            preferred_element_type=jnp.float32,
        ).reshape(height, span, channels).astype(jnp.bfloat16)

        gate_in = gated[:, halo_c : halo_c + breadth].reshape(height * breadth, channels)
        mix_in = mixes[p][:, halo_p : halo_p + breadth].reshape(height * breadth, channels)
        point_terms[p] = lax.dot_general(
            mix_in, gate_in, (((0,), (0,)), ((), ())), preferred_element_type=jnp.float32
        )
        bias_terms[p] = jnp.sum(gate_in.astype(jnp.float32), axis=0)
        back_in = back_mix[:, halo_c : halo_c + breadth].astype(jnp.float32)
        padded = pad_rows(acts[p])
        halo_a = (acts[p].shape[1] - breadth) // 2
        rows_k = []
        for i in range(3):
            row_k = []
            for j in range(3):
                start = halo_a - 1 + j
                row_k.append(
                    jnp.sum(
                        back_in * padded[i : i + height, start : start + breadth].astype(jnp.float32),
                        axis=(0, 1),
                    )
                )
            rows_k.append(jnp.stack(row_k))
        depth_terms[p] = jnp.stack(rows_k)

        earlier = conv_backward(pad_rows(back_mix), depth)
        cotangent = ((masked[:, 1:-1] + earlier) * live).astype(jnp.bfloat16)
    input_grad = cotangent

    got_outcome = lax.ppermute(outcome, "pipe", [(0, 1)])
    got_grad = lax.ppermute(input_grad, "pipe", [(1, 0)])
    first = jnp.where(core == 0, input_grad, got_outcome)
    second = jnp.where(core == 0, got_grad, outcome)
    result = jnp.stack([first, second])[None]

    pieces = (jnp.stack(depth_terms), jnp.stack(point_terms), jnp.stack(bias_terms))
    flat = jnp.concatenate([piece.reshape(layers, -1) for piece in pieces], axis=1)
    flat = all_reduce(flat, core)
    inverse = jnp.zeros((layers,), jnp.int32).at[layer_order].set(jnp.arange(layers, dtype=jnp.int32))
    factor = 1.0 / math.sqrt(held.shape[0] * height * breadth * blk_count())
    flat = jnp.take(flat, inverse, axis=0) * factor
    ordered, at = [], 0
    for piece in pieces:
        width = piece[0].size
        ordered.append(flat[:, at : at + width].reshape(piece.shape))
        at += width
    return (result, ordered[0], ordered[1], ordered[2])


def solution(mesh):
    devices = mesh.devices
    blk = devices.shape[0]
    y_size = 4 if blk % 4 == 0 else 1
    rest = blk // y_size
    z_size = 8 if rest % 8 == 0 else rest
    x_size = rest // z_size
    torus = Mesh(devices.reshape(x_size, z_size, y_size, devices.shape[1]), BLK_AXES + ("pipe",))
    spec = P("pipe", None, None, BLK_AXES, None)
    in_specs = (spec, P(), P(), P(), P(), P())
    out_specs = (spec, P(), P(), P())
    return jax.shard_map(shards, mesh=torus, in_specs=in_specs, out_specs=out_specs, check_vma=False)
```

```python
import math

import jax
import jax.numpy as jnp
from jax import lax
from jax.experimental import pallas as pl
from jax.experimental.pallas import tpu as pltpu
from jax.sharding import Mesh, PartitionSpec as P

MESH_ID = pl.DeviceIdType.MESH

root_half = 0.7071067811865476
density_norm = 0.3989422804014327

X_HALO = 8
G_HALO = 4


BLK_AXES = ("x", "z", "y")


def blk_count():
    count = 1
    for axis in BLK_AXES:
        count *= lax.axis_size(axis)
    return count


def gelu_pair(preact):
    normal_cdf = 0.5 * (1.0 + lax.erf(preact * root_half))
    normal_pdf = density_norm * jnp.exp(-0.5 * preact * preact)
    return (preact * normal_cdf, normal_cdf + preact * normal_pdf)


def select_row(table, chosen):
    return lax.dynamic_index_in_dim(table, chosen, 0, keepdims=False)


def pad_rows(x):
    return jnp.pad(x, ((1, 1), (0, 0), (0, 0)))


def conv_forward(padded, depth):
    height = padded.shape[0] - 2
    breadth = padded.shape[1] - 2
    acc = jnp.zeros((height, breadth, padded.shape[2]), jnp.float32)
    for i in range(3):
        for j in range(3):
            acc = acc + depth[i, j] * padded[i : i + height, j : j + breadth].astype(jnp.float32)
    return acc


def conv_backward(spread, depth):
    height = spread.shape[0] - 2
    breadth = spread.shape[1] - 2
    acc = jnp.zeros((height, breadth, spread.shape[2]), jnp.float32)
    for i in range(3):
        for j in range(3):
            acc = acc + depth[i, j] * spread[
                2 - i : 2 - i + height, 2 - j : 2 - j + breadth
            ].astype(jnp.float32)
    return acc


def torus_coords(b):
    y_size, z_size = lax.axis_size("y"), lax.axis_size("z")
    return (b // (y_size * z_size), lax.rem(b // y_size, z_size), lax.rem(b, y_size))


def exchange_kernel(held_ref, edges_ref, body_out, lo_out, hi_out, body, lo, hi, send_sem, recv_sem):
    core = lax.axis_index("pipe")
    count = blk_count()
    here = (lax.axis_index("x") * lax.axis_size("z") + lax.axis_index("z")) * lax.axis_size("y") + lax.axis_index("y")
    right = torus_coords(lax.rem(here + 1, count))
    left = torus_coords(lax.rem(here + count - 1, count))
    mine = torus_coords(here)
    partner = mine + (1 - core,)
    targets = [partner] + [right + (m,) for m in range(2)] + [left + (m,) for m in range(2)]

    barrier = pltpu.get_barrier_semaphore()
    for target in targets:
        pl.semaphore_signal(barrier, inc=1, device_id=target, device_id_type=MESH_ID)
    pl.semaphore_wait(barrier, len(targets))

    copies = [
        pltpu.make_async_remote_copy(
            src_ref=held_ref.at[1 - core], dst_ref=body,
            send_sem=send_sem.at[0], recv_sem=recv_sem.at[0],
            device_id=partner, device_id_type=MESH_ID,
        )
    ]
    for m in range(2):
        copies.append(pltpu.make_async_remote_copy(
            src_ref=edges_ref.at[1, m], dst_ref=lo.at[core],
            send_sem=send_sem.at[1 + m], recv_sem=recv_sem.at[1 + core],
            device_id=right + (m,), device_id_type=MESH_ID,
        ))
        copies.append(pltpu.make_async_remote_copy(
            src_ref=edges_ref.at[0, m], dst_ref=hi.at[core],
            send_sem=send_sem.at[3 + m], recv_sem=recv_sem.at[3 + core],
            device_id=left + (m,), device_id_type=MESH_ID,
        ))
    for copy in copies:
        copy.start()
    copies[0].wait_recv()
    for k in range(2):
        pltpu.make_async_remote_copy(
            src_ref=edges_ref.at[1, k], dst_ref=lo.at[k],
            send_sem=send_sem.at[1 + k], recv_sem=recv_sem.at[1 + k],
            device_id=right + (k,), device_id_type=MESH_ID,
        ).wait_recv()
        pltpu.make_async_remote_copy(
            src_ref=edges_ref.at[0, k], dst_ref=hi.at[k],
            send_sem=send_sem.at[3 + k], recv_sem=recv_sem.at[3 + k],
            device_id=left + (k,), device_id_type=MESH_ID,
        ).wait_recv()
    for copy in copies:
        copy.wait_send()
    body_out[...] = body[...]
    lo_out[...] = lo[...]
    hi_out[...] = hi[...]


def exchange(held, edges):
    grid_shape = held.shape[1:]
    strip_shape = edges.shape[2:]
    vmem = pl.BlockSpec(memory_space=pltpu.VMEM)
    return pl.pallas_call(
        exchange_kernel,
        out_shape=(
            jax.ShapeDtypeStruct(grid_shape, held.dtype),
            jax.ShapeDtypeStruct((2,) + strip_shape, held.dtype),
            jax.ShapeDtypeStruct((2,) + strip_shape, held.dtype),
        ),
        in_specs=[vmem, vmem],
        out_specs=(vmem, vmem, vmem),
        scratch_shapes=[
            pltpu.VMEM(grid_shape, held.dtype),
            pltpu.VMEM((2,) + strip_shape, held.dtype),
            pltpu.VMEM((2,) + strip_shape, held.dtype),
            pltpu.SemaphoreType.DMA((5,)),
            pltpu.SemaphoreType.DMA((5,)),
        ],
        compiler_params=pltpu.CompilerParams(collective_id=0, has_side_effects=True),
    )(held, edges)


def flip(index, bit):
    return index + bit - 2 * bit * lax.rem(index // bit, 2)


def reduce_kernel(flat_ref, out_ref, acc, recv, send_sem, recv_sem):
    core = lax.axis_index("pipe")
    half = flat_ref.shape[1] // 2
    coords = {axis: lax.axis_index(axis) for axis in BLK_AXES}
    order_a, order_b = [], []
    for axis in ("z", "y", "x"):
        bit = 1
        while bit < lax.axis_size(axis):
            order_a.append((axis, bit))
            bit *= 2
    for axis in ("y", "x", "z"):
        bit = 1
        while bit < lax.axis_size(axis):
            order_b.append((axis, bit))
            bit *= 2
    partner = tuple(coords[axis] for axis in BLK_AXES) + (1 - core,)
    peers = []
    for (axis_a, bit_a), (axis_b, bit_b) in zip(order_a, order_b):
        peer = []
        for axis in BLK_AXES:
            flip_a = flip(coords[axis], bit_a) if axis == axis_a else coords[axis]
            flip_b = flip(coords[axis], bit_b) if axis == axis_b else coords[axis]
            peer.append(flip_a * (1 - core) + flip_b * core)
        peers.append(tuple(peer) + (core,))

    barrier = pltpu.get_barrier_semaphore()
    for target in [partner] + peers:
        pl.semaphore_signal(barrier, inc=1, device_id=target, device_id_type=MESH_ID)
    pl.semaphore_wait(barrier, 1 + len(peers))

    own = pl.ds(pl.multiple_of(core * half, 128), half)
    other = pl.ds(pl.multiple_of((1 - core) * half, 128), half)
    first = pltpu.make_async_remote_copy(
        src_ref=flat_ref.at[:, other], dst_ref=recv.at[0],
        send_sem=send_sem.at[0], recv_sem=recv_sem.at[0],
        device_id=partner, device_id_type=MESH_ID,
    )
    first.start()
    first.wait()
    acc[0] = flat_ref[:, own] + recv[0]
    for step, peer in enumerate(peers):
        copy = pltpu.make_async_remote_copy(
            src_ref=acc.at[step], dst_ref=recv.at[step + 1],
            send_sem=send_sem.at[step + 1], recv_sem=recv_sem.at[step + 1],
            device_id=peer, device_id_type=MESH_ID,
        )
        copy.start()
        copy.wait()
        acc[step + 1] = acc[step] + recv[step + 1]
    last = len(peers)
    final = pltpu.make_async_remote_copy(
        src_ref=acc.at[last], dst_ref=recv.at[last + 1],
        send_sem=send_sem.at[last + 1], recv_sem=recv_sem.at[last + 1],
        device_id=partner, device_id_type=MESH_ID,
    )
    final.start()
    final.wait()
    out_ref[:, own] = acc[last]
    out_ref[:, other] = recv[last + 1]


def all_reduce(flat):
    rows, width = flat.shape
    steps = 0
    for axis in BLK_AXES:
        steps += max(lax.axis_size(axis) - 1, 0).bit_length()
    vmem = pl.BlockSpec(memory_space=pltpu.VMEM)
    return pl.pallas_call(
        reduce_kernel,
        out_shape=jax.ShapeDtypeStruct(flat.shape, flat.dtype),
        in_specs=[vmem],
        out_specs=vmem,
        scratch_shapes=[
            pltpu.VMEM((steps + 1, rows, width // 2), flat.dtype),
            pltpu.VMEM((steps + 2, rows, width // 2), flat.dtype),
            pltpu.SemaphoreType.DMA((steps + 2,)),
            pltpu.SemaphoreType.DMA((steps + 2,)),
        ],
        compiler_params=pltpu.CompilerParams(collective_id=1, has_side_effects=True),
    )(flat)


def shards(endpoints, row_counts, layer_order, depth_weight, point_weight, point_bias):
    held = endpoints[0]
    height = held.shape[1]
    breadth = held.shape[2]
    channels = held.shape[3]
    layers = layer_order.shape[0]
    core = lax.axis_index("pipe")

    edges = jnp.stack([held[:, :, :X_HALO], held[:, :, breadth - X_HALO :]])
    body, lo, hi = exchange(held, edges)
    mine = select_row(held, core)
    x_in = jnp.where(core == 0, mine, body)
    g_in = jnp.where(core == 0, body, mine)
    x_wide = jnp.concatenate([lo[0], x_in, hi[0]], axis=1)
    g_wide = jnp.concatenate([lo[1][:, X_HALO - G_HALO :], g_in, hi[1][:, :G_HALO]], axis=1)

    live = (jnp.arange(height)[:, None, None] < select_row(row_counts, core)).astype(jnp.float32)

    weights = []
    for p in range(layers):
        w = layer_order[p]
        weights.append(
            (select_row(depth_weight, w), select_row(point_weight, w), select_row(point_bias, w))
        )

    activation = (x_wide.astype(jnp.float32) * live).astype(jnp.bfloat16)
    acts, mixes, preacts = [], [], []
    for p in range(layers):
        depth, point, offset_vec = weights[p]
        acts.append(activation)
        mixed = conv_forward(pad_rows(activation), depth).astype(jnp.bfloat16)
        rows, span = mixed.shape[0], mixed.shape[1]
        preact = jnp.dot(
            mixed.reshape(rows * span, channels), point, preferred_element_type=jnp.float32
        ).reshape(rows, span, channels) + offset_vec
        mixes.append(mixed)
        preacts.append(preact)
        activation = (
            (activation[:, 1:-1].astype(jnp.float32) + gelu_pair(preact)[0]) * live
        ).astype(jnp.bfloat16)
    final_halo = X_HALO - layers
    outcome = activation[:, final_halo : final_halo + breadth]

    cotangent = g_wide
    depth_terms, point_terms, bias_terms = [None] * layers, [None] * layers, [None] * layers
    for p in range(layers - 1, -1, -1):
        depth, point, _ = weights[p]
        halo_c = (cotangent.shape[1] - breadth) // 2
        halo_p = (preacts[p].shape[1] - breadth) // 2
        shift = halo_p - halo_c
        span = cotangent.shape[1]
        preact = preacts[p][:, shift : shift + span]
        masked = cotangent.astype(jnp.float32) * live
        gated = (masked * gelu_pair(preact)[1]).astype(jnp.bfloat16)
        back_mix = lax.dot_general(
            gated.reshape(height * span, channels),
            point,
            (((1,), (1,)), ((), ())),
            preferred_element_type=jnp.float32,
        ).reshape(height, span, channels).astype(jnp.bfloat16)

        gate_in = gated[:, halo_c : halo_c + breadth].reshape(height * breadth, channels)
        mix_in = mixes[p][:, halo_p : halo_p + breadth].reshape(height * breadth, channels)
        point_terms[p] = lax.dot_general(
            mix_in, gate_in, (((0,), (0,)), ((), ())), preferred_element_type=jnp.float32
        )
        bias_terms[p] = jnp.sum(gate_in.astype(jnp.float32), axis=0)
        back_in = back_mix[:, halo_c : halo_c + breadth].astype(jnp.float32)
        padded = pad_rows(acts[p])
        halo_a = (acts[p].shape[1] - breadth) // 2
        rows_k = []
        for i in range(3):
            row_k = []
            for j in range(3):
                start = halo_a - 1 + j
                row_k.append(
                    jnp.sum(
                        back_in * padded[i : i + height, start : start + breadth].astype(jnp.float32),
                        axis=(0, 1),
                    )
                )
            rows_k.append(jnp.stack(row_k))
        depth_terms[p] = jnp.stack(rows_k)

        earlier = conv_backward(pad_rows(back_mix), depth)
        cotangent = ((masked[:, 1:-1] + earlier) * live).astype(jnp.bfloat16)
    input_grad = cotangent

    got_outcome = lax.ppermute(outcome, "pipe", [(0, 1)])
    got_grad = lax.ppermute(input_grad, "pipe", [(1, 0)])
    first = jnp.where(core == 0, input_grad, got_outcome)
    second = jnp.where(core == 0, got_grad, outcome)
    result = jnp.stack([first, second])[None]

    pieces = (jnp.stack(depth_terms), jnp.stack(point_terms), jnp.stack(bias_terms))
    flat = jnp.concatenate([piece.reshape(layers, -1) for piece in pieces], axis=1)
    flat = all_reduce(flat)
    inverse = jnp.zeros((layers,), jnp.int32).at[layer_order].set(jnp.arange(layers, dtype=jnp.int32))
    factor = 1.0 / math.sqrt(held.shape[0] * height * breadth * blk_count())
    flat = jnp.take(flat, inverse, axis=0) * factor
    ordered, at = [], 0
    for piece in pieces:
        width = piece[0].size
        ordered.append(flat[:, at : at + width].reshape(piece.shape))
        at += width
    return (result, ordered[0], ordered[1], ordered[2])


def solution(mesh):
    devices = mesh.devices
    blk = devices.shape[0]
    y_size = 4 if blk % 4 == 0 else 1
    rest = blk // y_size
    z_size = 8 if rest % 8 == 0 else rest
    x_size = rest // z_size
    torus = Mesh(devices.reshape(x_size, z_size, y_size, devices.shape[1]), BLK_AXES + ("pipe",))
    spec = P("pipe", None, None, BLK_AXES, None)
    in_specs = (spec, P(), P(), P(), P(), P())
    out_specs = (spec, P(), P(), P())
    return jax.shard_map(shards, mesh=torus, in_specs=in_specs, out_specs=out_specs, check_vma=False)
```

```python
import math

import jax
import jax.numpy as jnp
from jax import lax
from jax.experimental import pallas as pl
from jax.experimental.pallas import tpu as pltpu
from jax.sharding import Mesh, PartitionSpec as P

MESH_ID = pl.DeviceIdType.MESH

root_half = 0.7071067811865476
density_norm = 0.3989422804014327

X_HALO = 8
G_HALO = 4


BLK_AXES = ("x", "z", "y")


def blk_count():
    count = 1
    for axis in BLK_AXES:
        count *= lax.axis_size(axis)
    return count


def gelu_pair(preact):
    normal_cdf = 0.5 * (1.0 + lax.erf(preact * root_half))
    normal_pdf = density_norm * jnp.exp(-0.5 * preact * preact)
    return (preact * normal_cdf, normal_cdf + preact * normal_pdf)


def select_row(table, chosen):
    return lax.dynamic_index_in_dim(table, chosen, 0, keepdims=False)


def pad_rows(x):
    return jnp.pad(x, ((1, 1), (0, 0), (0, 0)))


def conv_forward(padded, depth):
    height = padded.shape[0] - 2
    breadth = padded.shape[1] - 2
    acc = jnp.zeros((height, breadth, padded.shape[2]), jnp.float32)
    for i in range(3):
        for j in range(3):
            acc = acc + depth[i, j] * padded[i : i + height, j : j + breadth].astype(jnp.float32)
    return acc


def conv_backward(spread, depth):
    height = spread.shape[0] - 2
    breadth = spread.shape[1] - 2
    acc = jnp.zeros((height, breadth, spread.shape[2]), jnp.float32)
    for i in range(3):
        for j in range(3):
            acc = acc + depth[i, j] * spread[
                2 - i : 2 - i + height, 2 - j : 2 - j + breadth
            ].astype(jnp.float32)
    return acc


def torus_coords(b):
    y_size, z_size = lax.axis_size("y"), lax.axis_size("z")
    return (b // (y_size * z_size), lax.rem(b // y_size, z_size), lax.rem(b, y_size))


def exchange_kernel(held_ref, edges_ref, body_out, lo_out, hi_out, body, lo, hi, send_sem, recv_sem):
    core = lax.axis_index("pipe")
    count = blk_count()
    here = (lax.axis_index("x") * lax.axis_size("z") + lax.axis_index("z")) * lax.axis_size("y") + lax.axis_index("y")
    right = torus_coords(lax.rem(here + 1, count))
    left = torus_coords(lax.rem(here + count - 1, count))
    mine = torus_coords(here)
    partner = mine + (1 - core,)
    targets = [partner] + [right + (m,) for m in range(2)] + [left + (m,) for m in range(2)]

    barrier = pltpu.get_barrier_semaphore()
    for target in targets:
        pl.semaphore_signal(barrier, inc=1, device_id=target, device_id_type=MESH_ID)
    pl.semaphore_wait(barrier, len(targets))

    copies = [
        pltpu.make_async_remote_copy(
            src_ref=held_ref.at[1 - core], dst_ref=body,
            send_sem=send_sem.at[0], recv_sem=recv_sem.at[0],
            device_id=partner, device_id_type=MESH_ID,
        )
    ]
    for m in range(2):
        copies.append(pltpu.make_async_remote_copy(
            src_ref=edges_ref.at[1, m], dst_ref=lo.at[core],
            send_sem=send_sem.at[1 + m], recv_sem=recv_sem.at[1 + core],
            device_id=right + (m,), device_id_type=MESH_ID,
        ))
        copies.append(pltpu.make_async_remote_copy(
            src_ref=edges_ref.at[0, m], dst_ref=hi.at[core],
            send_sem=send_sem.at[3 + m], recv_sem=recv_sem.at[3 + core],
            device_id=left + (m,), device_id_type=MESH_ID,
        ))
    for copy in copies:
        copy.start()
    copies[0].wait_recv()
    for k in range(2):
        pltpu.make_async_remote_copy(
            src_ref=edges_ref.at[1, k], dst_ref=lo.at[k],
            send_sem=send_sem.at[1 + k], recv_sem=recv_sem.at[1 + k],
            device_id=right + (k,), device_id_type=MESH_ID,
        ).wait_recv()
        pltpu.make_async_remote_copy(
            src_ref=edges_ref.at[0, k], dst_ref=hi.at[k],
            send_sem=send_sem.at[3 + k], recv_sem=recv_sem.at[3 + k],
            device_id=left + (k,), device_id_type=MESH_ID,
        ).wait_recv()
    for copy in copies:
        copy.wait_send()
    body_out[...] = body[...]
    lo_out[...] = lo[...]
    hi_out[...] = hi[...]


def exchange(held, edges):
    grid_shape = held.shape[1:]
    strip_shape = edges.shape[2:]
    vmem = pl.BlockSpec(memory_space=pltpu.VMEM)
    return pl.pallas_call(
        exchange_kernel,
        out_shape=(
            jax.ShapeDtypeStruct(grid_shape, held.dtype),
            jax.ShapeDtypeStruct((2,) + strip_shape, held.dtype),
            jax.ShapeDtypeStruct((2,) + strip_shape, held.dtype),
        ),
        in_specs=[vmem, vmem],
        out_specs=(vmem, vmem, vmem),
        scratch_shapes=[
            pltpu.VMEM(grid_shape, held.dtype),
            pltpu.VMEM((2,) + strip_shape, held.dtype),
            pltpu.VMEM((2,) + strip_shape, held.dtype),
            pltpu.SemaphoreType.DMA((5,)),
            pltpu.SemaphoreType.DMA((5,)),
        ],
        compiler_params=pltpu.CompilerParams(collective_id=0, has_side_effects=True),
    )(held, edges)


def flip(index, bit):
    return index + bit - 2 * bit * lax.rem(index // bit, 2)


def reduce_kernel(flat_ref, out_ref, acc, recv, send_sem, recv_sem):
    core = lax.axis_index("pipe")
    half = flat_ref.shape[0] // 2
    coords = {axis: lax.axis_index(axis) for axis in BLK_AXES}
    order_a, order_b = [], []
    for axis in ("z", "y", "x"):
        bit = 1
        while bit < lax.axis_size(axis):
            order_a.append((axis, bit))
            bit *= 2
    for axis in ("y", "x", "z"):
        bit = 1
        while bit < lax.axis_size(axis):
            order_b.append((axis, bit))
            bit *= 2
    partner = tuple(coords[axis] for axis in BLK_AXES) + (1 - core,)
    peers = []
    for (axis_a, bit_a), (axis_b, bit_b) in zip(order_a, order_b):
        peer = []
        for axis in BLK_AXES:
            flip_a = flip(coords[axis], bit_a) if axis == axis_a else coords[axis]
            flip_b = flip(coords[axis], bit_b) if axis == axis_b else coords[axis]
            peer.append(flip_a * (1 - core) + flip_b * core)
        peers.append(tuple(peer) + (core,))

    barrier = pltpu.get_barrier_semaphore()
    for target in [partner] + peers:
        pl.semaphore_signal(barrier, inc=1, device_id=target, device_id_type=MESH_ID)
    pl.semaphore_wait(barrier, 1 + len(peers))

    own = pl.ds(pl.multiple_of(core * half, 8), half)
    other = pl.ds(pl.multiple_of((1 - core) * half, 8), half)
    first = pltpu.make_async_remote_copy(
        src_ref=flat_ref.at[other], dst_ref=recv.at[0],
        send_sem=send_sem.at[0], recv_sem=recv_sem.at[0],
        device_id=partner, device_id_type=MESH_ID,
    )
    first.start()
    first.wait()
    acc[0] = flat_ref[own] + recv[0]
    for step, peer in enumerate(peers):
        copy = pltpu.make_async_remote_copy(
            src_ref=acc.at[step], dst_ref=recv.at[step + 1],
            send_sem=send_sem.at[step + 1], recv_sem=recv_sem.at[step + 1],
            device_id=peer, device_id_type=MESH_ID,
        )
        copy.start()
        copy.wait()
        acc[step + 1] = acc[step] + recv[step + 1]
    last = len(peers)
    final = pltpu.make_async_remote_copy(
        src_ref=acc.at[last], dst_ref=recv.at[last + 1],
        send_sem=send_sem.at[last + 1], recv_sem=recv_sem.at[last + 1],
        device_id=partner, device_id_type=MESH_ID,
    )
    final.start()
    final.wait()
    out_ref[own] = acc[last]
    out_ref[other] = recv[last + 1]


def all_reduce(flat):
    rows, width = flat.shape
    steps = 0
    for axis in BLK_AXES:
        steps += max(lax.axis_size(axis) - 1, 0).bit_length()
    vmem = pl.BlockSpec(memory_space=pltpu.VMEM)
    return pl.pallas_call(
        reduce_kernel,
        out_shape=jax.ShapeDtypeStruct(flat.shape, flat.dtype),
        in_specs=[vmem],
        out_specs=vmem,
        scratch_shapes=[
            pltpu.VMEM((steps + 1, rows // 2, width), flat.dtype),
            pltpu.VMEM((steps + 2, rows // 2, width), flat.dtype),
            pltpu.SemaphoreType.DMA((steps + 2,)),
            pltpu.SemaphoreType.DMA((steps + 2,)),
        ],
        compiler_params=pltpu.CompilerParams(collective_id=1, has_side_effects=True),
    )(flat)


def shards(endpoints, row_counts, layer_order, depth_weight, point_weight, point_bias):
    held = endpoints[0]
    height = held.shape[1]
    breadth = held.shape[2]
    channels = held.shape[3]
    layers = layer_order.shape[0]
    core = lax.axis_index("pipe")

    edges = jnp.stack([held[:, :, :X_HALO], held[:, :, breadth - X_HALO :]])
    body, lo, hi = exchange(held, edges)
    mine = select_row(held, core)
    x_in = jnp.where(core == 0, mine, body)
    g_in = jnp.where(core == 0, body, mine)
    x_wide = jnp.concatenate([lo[0], x_in, hi[0]], axis=1)
    g_wide = jnp.concatenate([lo[1][:, X_HALO - G_HALO :], g_in, hi[1][:, :G_HALO]], axis=1)

    live = (jnp.arange(height)[:, None, None] < select_row(row_counts, core)).astype(jnp.float32)

    weights = []
    for p in range(layers):
        w = layer_order[p]
        weights.append(
            (select_row(depth_weight, w), select_row(point_weight, w), select_row(point_bias, w))
        )

    activation = (x_wide.astype(jnp.float32) * live).astype(jnp.bfloat16)
    acts, mixes, preacts = [], [], []
    for p in range(layers):
        depth, point, offset_vec = weights[p]
        acts.append(activation)
        mixed = conv_forward(pad_rows(activation), depth).astype(jnp.bfloat16)
        rows, span = mixed.shape[0], mixed.shape[1]
        preact = jnp.dot(
            mixed.reshape(rows * span, channels), point, preferred_element_type=jnp.float32
        ).reshape(rows, span, channels) + offset_vec
        mixes.append(mixed)
        preacts.append(preact)
        activation = (
            (activation[:, 1:-1].astype(jnp.float32) + gelu_pair(preact)[0]) * live
        ).astype(jnp.bfloat16)
    final_halo = X_HALO - layers
    outcome = activation[:, final_halo : final_halo + breadth]

    cotangent = g_wide
    depth_terms, point_terms, bias_terms = [None] * layers, [None] * layers, [None] * layers
    for p in range(layers - 1, -1, -1):
        depth, point, _ = weights[p]
        halo_c = (cotangent.shape[1] - breadth) // 2
        halo_p = (preacts[p].shape[1] - breadth) // 2
        shift = halo_p - halo_c
        span = cotangent.shape[1]
        preact = preacts[p][:, shift : shift + span]
        masked = cotangent.astype(jnp.float32) * live
        gated = (masked * gelu_pair(preact)[1]).astype(jnp.bfloat16)
        back_mix = lax.dot_general(
            gated.reshape(height * span, channels),
            point,
            (((1,), (1,)), ((), ())),
            preferred_element_type=jnp.float32,
        ).reshape(height, span, channels).astype(jnp.bfloat16)

        gate_in = gated[:, halo_c : halo_c + breadth].reshape(height * breadth, channels)
        mix_in = mixes[p][:, halo_p : halo_p + breadth].reshape(height * breadth, channels)
        point_terms[p] = lax.dot_general(
            mix_in, gate_in, (((0,), (0,)), ((), ())), preferred_element_type=jnp.float32
        )
        bias_terms[p] = jnp.sum(gate_in.astype(jnp.float32), axis=0)
        back_in = back_mix[:, halo_c : halo_c + breadth].astype(jnp.float32)
        padded = pad_rows(acts[p])
        halo_a = (acts[p].shape[1] - breadth) // 2
        rows_k = []
        for i in range(3):
            row_k = []
            for j in range(3):
                start = halo_a - 1 + j
                row_k.append(
                    jnp.sum(
                        back_in * padded[i : i + height, start : start + breadth].astype(jnp.float32),
                        axis=(0, 1),
                    )
                )
            rows_k.append(jnp.stack(row_k))
        depth_terms[p] = jnp.stack(rows_k)

        earlier = conv_backward(pad_rows(back_mix), depth)
        cotangent = ((masked[:, 1:-1] + earlier) * live).astype(jnp.bfloat16)
    input_grad = cotangent

    got_outcome = lax.ppermute(outcome, "pipe", [(0, 1)])
    got_grad = lax.ppermute(input_grad, "pipe", [(1, 0)])
    first = jnp.where(core == 0, input_grad, got_outcome)
    second = jnp.where(core == 0, got_grad, outcome)
    result = jnp.stack([first, second])[None]

    pieces = []
    for terms in (depth_terms, point_terms, bias_terms):
        by_layer = []
        for w in range(layers):
            picked = jnp.zeros_like(terms[0])
            for p in range(layers):
                picked = picked + jnp.where(layer_order[p] == w, terms[p], 0.0)
            by_layer.append(picked)
        pieces.append(jnp.stack(by_layer))
    flat = jnp.concatenate([piece.reshape(-1) for piece in pieces])
    lanes = 128
    rows = -(-flat.shape[0] // lanes)
    rows = -(-rows // 16) * 16
    flat = jnp.pad(flat, (0, rows * lanes - flat.shape[0])).reshape(rows, lanes)
    factor = 1.0 / math.sqrt(held.shape[0] * height * breadth * blk_count())
    flat = (all_reduce(flat) * factor).reshape(-1)
    ordered, at = [], 0
    for piece in pieces:
        ordered.append(flat[at : at + piece.size].reshape(piece.shape))
        at += piece.size
    return (result, ordered[0], ordered[1], ordered[2])


def solution(mesh):
    devices = mesh.devices
    blk = devices.shape[0]
    y_size = 4 if blk % 4 == 0 else 1
    rest = blk // y_size
    z_size = 8 if rest % 8 == 0 else rest
    x_size = rest // z_size
    torus = Mesh(devices.reshape(x_size, z_size, y_size, devices.shape[1]), BLK_AXES + ("pipe",))
    spec = P("pipe", None, None, BLK_AXES, None)
    in_specs = (spec, P(), P(), P(), P(), P())
    out_specs = (spec, P(), P(), P())
    return jax.shard_map(shards, mesh=torus, in_specs=in_specs, out_specs=out_specs, check_vma=False)
```

```python
import math

import jax
import jax.numpy as jnp
from jax import lax
from jax.experimental import pallas as pl
from jax.experimental.pallas import tpu as pltpu
from jax.sharding import Mesh, PartitionSpec as P

MESH_ID = pl.DeviceIdType.MESH

root_half = 0.7071067811865476
density_norm = 0.3989422804014327

X_HALO = 8
G_HALO = 4


BLK_AXES = ("x", "z", "y")


def blk_count():
    count = 1
    for axis in BLK_AXES:
        count *= lax.axis_size(axis)
    return count


def gelu_pair(preact):
    normal_cdf = 0.5 * (1.0 + lax.erf(preact * root_half))
    normal_pdf = density_norm * jnp.exp(-0.5 * preact * preact)
    return (preact * normal_cdf, normal_cdf + preact * normal_pdf)


def select_row(table, chosen):
    return lax.dynamic_index_in_dim(table, chosen, 0, keepdims=False)


def pad_rows(x):
    return jnp.pad(x, ((1, 1), (0, 0), (0, 0)))


def conv_forward(padded, depth):
    height = padded.shape[0] - 2
    breadth = padded.shape[1] - 2
    acc = jnp.zeros((height, breadth, padded.shape[2]), jnp.float32)
    for i in range(3):
        for j in range(3):
            acc = acc + depth[i, j] * padded[i : i + height, j : j + breadth].astype(jnp.float32)
    return acc


def conv_backward(spread, depth):
    height = spread.shape[0] - 2
    breadth = spread.shape[1] - 2
    acc = jnp.zeros((height, breadth, spread.shape[2]), jnp.float32)
    for i in range(3):
        for j in range(3):
            acc = acc + depth[i, j] * spread[
                2 - i : 2 - i + height, 2 - j : 2 - j + breadth
            ].astype(jnp.float32)
    return acc


def torus_coords(b):
    y_size, z_size = lax.axis_size("y"), lax.axis_size("z")
    return (b // (y_size * z_size), lax.rem(b // y_size, z_size), lax.rem(b, y_size))


def exchange_kernel(held_ref, edges_ref, body_out, lo_out, hi_out, body, lo, hi, send_sem, recv_sem):
    core = lax.axis_index("pipe")
    count = blk_count()
    here = (lax.axis_index("x") * lax.axis_size("z") + lax.axis_index("z")) * lax.axis_size("y") + lax.axis_index("y")
    right = torus_coords(lax.rem(here + 1, count))
    left = torus_coords(lax.rem(here + count - 1, count))
    mine = torus_coords(here)
    partner = mine + (1 - core,)
    targets = [partner] + [right + (m,) for m in range(2)] + [left + (m,) for m in range(2)]

    barrier = pltpu.get_barrier_semaphore()
    for target in targets:
        pl.semaphore_signal(barrier, inc=1, device_id=target, device_id_type=MESH_ID)
    pl.semaphore_wait(barrier, len(targets))

    copies = [
        pltpu.make_async_remote_copy(
            src_ref=held_ref.at[1 - core], dst_ref=body,
            send_sem=send_sem.at[0], recv_sem=recv_sem.at[0],
            device_id=partner, device_id_type=MESH_ID,
        )
    ]
    for m in range(2):
        copies.append(pltpu.make_async_remote_copy(
            src_ref=edges_ref.at[1, m], dst_ref=lo.at[core],
            send_sem=send_sem.at[1 + m], recv_sem=recv_sem.at[1 + core],
            device_id=right + (m,), device_id_type=MESH_ID,
        ))
        copies.append(pltpu.make_async_remote_copy(
            src_ref=edges_ref.at[0, m], dst_ref=hi.at[core],
            send_sem=send_sem.at[3 + m], recv_sem=recv_sem.at[3 + core],
            device_id=left + (m,), device_id_type=MESH_ID,
        ))
    for copy in copies:
        copy.start()
    copies[0].wait_recv()
    for k in range(2):
        pltpu.make_async_remote_copy(
            src_ref=edges_ref.at[1, k], dst_ref=lo.at[k],
            send_sem=send_sem.at[1 + k], recv_sem=recv_sem.at[1 + k],
            device_id=right + (k,), device_id_type=MESH_ID,
        ).wait_recv()
        pltpu.make_async_remote_copy(
            src_ref=edges_ref.at[0, k], dst_ref=hi.at[k],
            send_sem=send_sem.at[3 + k], recv_sem=recv_sem.at[3 + k],
            device_id=left + (k,), device_id_type=MESH_ID,
        ).wait_recv()
    for copy in copies:
        copy.wait_send()
    body_out[...] = body[...]
    lo_out[...] = lo[...]
    hi_out[...] = hi[...]


def exchange(held, edges):
    grid_shape = held.shape[1:]
    strip_shape = edges.shape[2:]
    vmem = pl.BlockSpec(memory_space=pltpu.VMEM)
    return pl.pallas_call(
        exchange_kernel,
        out_shape=(
            jax.ShapeDtypeStruct(grid_shape, held.dtype),
            jax.ShapeDtypeStruct((2,) + strip_shape, held.dtype),
            jax.ShapeDtypeStruct((2,) + strip_shape, held.dtype),
        ),
        in_specs=[vmem, vmem],
        out_specs=(vmem, vmem, vmem),
        scratch_shapes=[
            pltpu.VMEM(grid_shape, held.dtype),
            pltpu.VMEM((2,) + strip_shape, held.dtype),
            pltpu.VMEM((2,) + strip_shape, held.dtype),
            pltpu.SemaphoreType.DMA((5,)),
            pltpu.SemaphoreType.DMA((5,)),
        ],
        compiler_params=pltpu.CompilerParams(collective_id=0, has_side_effects=True),
    )(held, edges)


def gather_sum(acc, axis):
    size = lax.axis_size(axis)
    index = lax.axis_index(axis)
    shifted = [acc] + [
        lax.ppermute(acc, axis, [(j, (j + k) % size) for j in range(size)])
        for k in range(1, size)
    ]
    stacked = jnp.stack(shifted)
    values = [select_row(stacked, lax.rem(index - j + size, size)) for j in range(size)]
    while len(values) > 1:
        values = [values[k] + values[k + 1] for k in range(0, len(values), 2)]
    return values[0]


def all_reduce(flat, core):
    half = flat.shape[1] // 2
    swap = [(0, 1), (1, 0)]
    mine = lax.dynamic_slice_in_dim(flat, core * half, half, axis=1)
    other = lax.dynamic_slice_in_dim(flat, (1 - core) * half, half, axis=1)
    acc = mine + lax.ppermute(other, "pipe", swap)
    for axis in ("y", "z", "x"):
        size = lax.axis_size(axis)
        if size == 4:
            acc = gather_sum(acc, axis)
            continue
        bit = 1
        while bit < size:
            pairs = [(i, i ^ bit) for i in range(size)]
            acc = acc + lax.ppermute(acc, axis, pairs)
            bit *= 2
    theirs = lax.ppermute(acc, "pipe", swap)
    low = jnp.where(core == 0, acc, theirs)
    high = jnp.where(core == 0, theirs, acc)
    return jnp.concatenate([low, high], axis=1)


def shards(endpoints, row_counts, layer_order, depth_weight, point_weight, point_bias):
    held = endpoints[0]
    height = held.shape[1]
    breadth = held.shape[2]
    channels = held.shape[3]
    layers = layer_order.shape[0]
    core = lax.axis_index("pipe")

    edges = jnp.stack([held[:, :, :X_HALO], held[:, :, breadth - X_HALO :]])
    body, lo, hi = exchange(held, edges)
    mine = select_row(held, core)
    x_in = jnp.where(core == 0, mine, body)
    g_in = jnp.where(core == 0, body, mine)
    x_wide = jnp.concatenate([lo[0], x_in, hi[0]], axis=1)
    g_wide = jnp.concatenate([lo[1][:, X_HALO - G_HALO :], g_in, hi[1][:, :G_HALO]], axis=1)

    live = (jnp.arange(height)[:, None, None] < select_row(row_counts, core)).astype(jnp.float32)

    weights = []
    for p in range(layers):
        w = layer_order[p]
        weights.append(
            (select_row(depth_weight, w), select_row(point_weight, w), select_row(point_bias, w))
        )

    activation = (x_wide.astype(jnp.float32) * live).astype(jnp.bfloat16)
    acts, mixes, preacts = [], [], []
    for p in range(layers):
        depth, point, offset_vec = weights[p]
        acts.append(activation)
        mixed = conv_forward(pad_rows(activation), depth).astype(jnp.bfloat16)
        rows, span = mixed.shape[0], mixed.shape[1]
        preact = jnp.dot(
            mixed.reshape(rows * span, channels), point, preferred_element_type=jnp.float32
        ).reshape(rows, span, channels) + offset_vec
        mixes.append(mixed)
        preacts.append(preact)
        activation = (
            (activation[:, 1:-1].astype(jnp.float32) + gelu_pair(preact)[0]) * live
        ).astype(jnp.bfloat16)
    final_halo = X_HALO - layers
    outcome = activation[:, final_halo : final_halo + breadth]

    cotangent = g_wide
    depth_terms, point_terms, bias_terms = [None] * layers, [None] * layers, [None] * layers
    for p in range(layers - 1, -1, -1):
        depth, point, _ = weights[p]
        halo_c = (cotangent.shape[1] - breadth) // 2
        halo_p = (preacts[p].shape[1] - breadth) // 2
        shift = halo_p - halo_c
        span = cotangent.shape[1]
        preact = preacts[p][:, shift : shift + span]
        masked = cotangent.astype(jnp.float32) * live
        gated = (masked * gelu_pair(preact)[1]).astype(jnp.bfloat16)
        back_mix = lax.dot_general(
            gated.reshape(height * span, channels),
            point,
            (((1,), (1,)), ((), ())),
            preferred_element_type=jnp.float32,
        ).reshape(height, span, channels).astype(jnp.bfloat16)

        gate_in = gated[:, halo_c : halo_c + breadth].reshape(height * breadth, channels)
        mix_in = mixes[p][:, halo_p : halo_p + breadth].reshape(height * breadth, channels)
        point_terms[p] = lax.dot_general(
            mix_in, gate_in, (((0,), (0,)), ((), ())), preferred_element_type=jnp.float32
        )
        bias_terms[p] = jnp.sum(gate_in.astype(jnp.float32), axis=0)
        back_in = back_mix[:, halo_c : halo_c + breadth].astype(jnp.float32)
        padded = pad_rows(acts[p])
        halo_a = (acts[p].shape[1] - breadth) // 2
        rows_k = []
        for i in range(3):
            row_k = []
            for j in range(3):
                start = halo_a - 1 + j
                row_k.append(
                    jnp.sum(
                        back_in * padded[i : i + height, start : start + breadth].astype(jnp.float32),
                        axis=(0, 1),
                    )
                )
            rows_k.append(jnp.stack(row_k))
        depth_terms[p] = jnp.stack(rows_k)

        earlier = conv_backward(pad_rows(back_mix), depth)
        cotangent = ((masked[:, 1:-1] + earlier) * live).astype(jnp.bfloat16)
    input_grad = cotangent

    got_outcome = lax.ppermute(outcome, "pipe", [(0, 1)])
    got_grad = lax.ppermute(input_grad, "pipe", [(1, 0)])
    first = jnp.where(core == 0, input_grad, got_outcome)
    second = jnp.where(core == 0, got_grad, outcome)
    result = jnp.stack([first, second])[None]

    pieces = (jnp.stack(depth_terms), jnp.stack(point_terms), jnp.stack(bias_terms))
    flat = jnp.concatenate([piece.reshape(layers, -1) for piece in pieces], axis=1)
    flat = all_reduce(flat, core)
    factor = 1.0 / math.sqrt(held.shape[0] * height * breadth * blk_count())
    by_layer = []
    for w in range(layers):
        picked = jnp.zeros_like(flat[0])
        for p in range(layers):
            picked = picked + jnp.where(layer_order[p] == w, flat[p], 0.0)
        by_layer.append(picked)
    flat = jnp.stack(by_layer) * factor
    ordered, at = [], 0
    for piece in pieces:
        width = piece[0].size
        ordered.append(flat[:, at : at + width].reshape(piece.shape))
        at += width
    return (result, ordered[0], ordered[1], ordered[2])


def solution(mesh):
    devices = mesh.devices
    blk = devices.shape[0]
    y_size = 4 if blk % 4 == 0 else 1
    rest = blk // y_size
    z_size = 8 if rest % 8 == 0 else rest
    x_size = rest // z_size
    torus = Mesh(devices.reshape(x_size, z_size, y_size, devices.shape[1]), BLK_AXES + ("pipe",))
    spec = P("pipe", None, None, BLK_AXES, None)
    in_specs = (spec, P(), P(), P(), P(), P())
    out_specs = (spec, P(), P(), P())
    return jax.shard_map(shards, mesh=torus, in_specs=in_specs, out_specs=out_specs, check_vma=False)
```

```python
import math

import jax
import jax.numpy as jnp
from jax import lax
from jax.experimental import pallas as pl
from jax.experimental.pallas import tpu as pltpu
from jax.sharding import Mesh, PartitionSpec as P

MESH_ID = pl.DeviceIdType.MESH

root_half = 0.7071067811865476
density_norm = 0.3989422804014327

X_HALO = 8
G_HALO = 4


BLK_AXES = ("x", "z", "y")


def blk_count():
    count = 1
    for axis in BLK_AXES:
        count *= lax.axis_size(axis)
    return count


def gelu_pair(preact):
    normal_cdf = 0.5 * (1.0 + lax.erf(preact * root_half))
    normal_pdf = density_norm * jnp.exp(-0.5 * preact * preact)
    return (preact * normal_cdf, normal_cdf + preact * normal_pdf)


def select_row(table, chosen):
    return lax.dynamic_index_in_dim(table, chosen, 0, keepdims=False)


def pad_rows(x):
    return jnp.pad(x, ((1, 1), (0, 0), (0, 0)))


def conv_forward(padded, depth):
    height = padded.shape[0] - 2
    breadth = padded.shape[1] - 2
    acc = jnp.zeros((height, breadth, padded.shape[2]), jnp.float32)
    for i in range(3):
        for j in range(3):
            acc = acc + depth[i, j] * padded[i : i + height, j : j + breadth].astype(jnp.float32)
    return acc


def conv_backward(spread, depth):
    height = spread.shape[0] - 2
    breadth = spread.shape[1] - 2
    acc = jnp.zeros((height, breadth, spread.shape[2]), jnp.float32)
    for i in range(3):
        for j in range(3):
            acc = acc + depth[i, j] * spread[
                2 - i : 2 - i + height, 2 - j : 2 - j + breadth
            ].astype(jnp.float32)
    return acc


def torus_coords(b):
    y_size, z_size = lax.axis_size("y"), lax.axis_size("z")
    return (b // (y_size * z_size), lax.rem(b // y_size, z_size), lax.rem(b, y_size))


def exchange_kernel(held_ref, edges_ref, body_out, lo_out, hi_out, body, lo, hi, send_sem, recv_sem):
    core = lax.axis_index("pipe")
    count = blk_count()
    here = (lax.axis_index("x") * lax.axis_size("z") + lax.axis_index("z")) * lax.axis_size("y") + lax.axis_index("y")
    right = torus_coords(lax.rem(here + 1, count))
    left = torus_coords(lax.rem(here + count - 1, count))
    mine = torus_coords(here)
    partner = mine + (1 - core,)
    targets = [partner] + [right + (m,) for m in range(2)] + [left + (m,) for m in range(2)]

    barrier = pltpu.get_barrier_semaphore()
    for target in targets:
        pl.semaphore_signal(barrier, inc=1, device_id=target, device_id_type=MESH_ID)
    pl.semaphore_wait(barrier, len(targets))

    copies = [
        pltpu.make_async_remote_copy(
            src_ref=held_ref.at[1 - core], dst_ref=body,
            send_sem=send_sem.at[0], recv_sem=recv_sem.at[0],
            device_id=partner, device_id_type=MESH_ID,
        )
    ]
    for m in range(2):
        copies.append(pltpu.make_async_remote_copy(
            src_ref=edges_ref.at[1, m], dst_ref=lo.at[core],
            send_sem=send_sem.at[1 + m], recv_sem=recv_sem.at[1 + core],
            device_id=right + (m,), device_id_type=MESH_ID,
        ))
        copies.append(pltpu.make_async_remote_copy(
            src_ref=edges_ref.at[0, m], dst_ref=hi.at[core],
            send_sem=send_sem.at[3 + m], recv_sem=recv_sem.at[3 + core],
            device_id=left + (m,), device_id_type=MESH_ID,
        ))
    for copy in copies:
        copy.start()
    copies[0].wait_recv()
    for k in range(2):
        pltpu.make_async_remote_copy(
            src_ref=edges_ref.at[1, k], dst_ref=lo.at[k],
            send_sem=send_sem.at[1 + k], recv_sem=recv_sem.at[1 + k],
            device_id=right + (k,), device_id_type=MESH_ID,
        ).wait_recv()
        pltpu.make_async_remote_copy(
            src_ref=edges_ref.at[0, k], dst_ref=hi.at[k],
            send_sem=send_sem.at[3 + k], recv_sem=recv_sem.at[3 + k],
            device_id=left + (k,), device_id_type=MESH_ID,
        ).wait_recv()
    for copy in copies:
        copy.wait_send()
    body_out[...] = body[...]
    lo_out[...] = lo[...]
    hi_out[...] = hi[...]


def exchange(held, edges):
    grid_shape = held.shape[1:]
    strip_shape = edges.shape[2:]
    vmem = pl.BlockSpec(memory_space=pltpu.VMEM)
    return pl.pallas_call(
        exchange_kernel,
        out_shape=(
            jax.ShapeDtypeStruct(grid_shape, held.dtype),
            jax.ShapeDtypeStruct((2,) + strip_shape, held.dtype),
            jax.ShapeDtypeStruct((2,) + strip_shape, held.dtype),
        ),
        in_specs=[vmem, vmem],
        out_specs=(vmem, vmem, vmem),
        scratch_shapes=[
            pltpu.VMEM(grid_shape, held.dtype),
            pltpu.VMEM((2,) + strip_shape, held.dtype),
            pltpu.VMEM((2,) + strip_shape, held.dtype),
            pltpu.SemaphoreType.DMA((5,)),
            pltpu.SemaphoreType.DMA((5,)),
        ],
        compiler_params=pltpu.CompilerParams(collective_id=0, has_side_effects=True),
    )(held, edges)


def xor_pairs(size, bit):
    return [(i, i ^ bit) for i in range(size)]


def all_reduce(flat, core):
    half = flat.shape[1] // 2
    swap = [(0, 1), (1, 0)]
    mine = lax.dynamic_slice_in_dim(flat, core * half, half, axis=1)
    other = lax.dynamic_slice_in_dim(flat, (1 - core) * half, half, axis=1)
    acc = (mine + lax.ppermute(other, "pipe", swap)).reshape(-1)
    block = 128 * 8 * 8
    padded = -(-acc.shape[0] // block) * block
    acc = jnp.pad(acc, (0, padded - acc.shape[0])).reshape(padded // 128, 128)

    halving, doubling = [], []
    for axis in ("y", "z", "x"):
        bit = 1
        while bit < lax.axis_size(axis):
            (halving if bit == 1 else doubling).append((axis, bit))
            bit *= 2
    for axis, bit in halving:
        side = lax.rem(lax.axis_index(axis) // bit, 2)
        rows = acc.shape[0] // 2
        kept = lax.dynamic_slice_in_dim(acc, side * rows, rows, axis=0)
        sent = lax.dynamic_slice_in_dim(acc, (1 - side) * rows, rows, axis=0)
        acc = kept + lax.ppermute(sent, axis, xor_pairs(lax.axis_size(axis), bit))
    for axis, bit in doubling:
        acc = acc + lax.ppermute(acc, axis, xor_pairs(lax.axis_size(axis), bit))
    for axis, bit in reversed(halving):
        side = lax.rem(lax.axis_index(axis) // bit, 2)
        got = lax.ppermute(acc, axis, xor_pairs(lax.axis_size(axis), bit))
        acc = jnp.concatenate([jnp.where(side == 0, acc, got), jnp.where(side == 0, got, acc)], axis=0)
    acc = acc.reshape(-1)[: half * flat.shape[0]].reshape(flat.shape[0], half)

    theirs = lax.ppermute(acc, "pipe", swap)
    low = jnp.where(core == 0, acc, theirs)
    high = jnp.where(core == 0, theirs, acc)
    return jnp.concatenate([low, high], axis=1)


def shards(endpoints, row_counts, layer_order, depth_weight, point_weight, point_bias):
    held = endpoints[0]
    height = held.shape[1]
    breadth = held.shape[2]
    channels = held.shape[3]
    layers = layer_order.shape[0]
    core = lax.axis_index("pipe")

    edges = jnp.stack([held[:, :, :X_HALO], held[:, :, breadth - X_HALO :]])
    body, lo, hi = exchange(held, edges)
    mine = select_row(held, core)
    x_in = jnp.where(core == 0, mine, body)
    g_in = jnp.where(core == 0, body, mine)
    x_wide = jnp.concatenate([lo[0], x_in, hi[0]], axis=1)
    g_wide = jnp.concatenate([lo[1][:, X_HALO - G_HALO :], g_in, hi[1][:, :G_HALO]], axis=1)

    live = (jnp.arange(height)[:, None, None] < select_row(row_counts, core)).astype(jnp.float32)

    weights = []
    for p in range(layers):
        w = layer_order[p]
        weights.append(
            (select_row(depth_weight, w), select_row(point_weight, w), select_row(point_bias, w))
        )

    activation = (x_wide.astype(jnp.float32) * live).astype(jnp.bfloat16)
    acts, mixes, preacts = [], [], []
    for p in range(layers):
        depth, point, offset_vec = weights[p]
        acts.append(activation)
        mixed = conv_forward(pad_rows(activation), depth).astype(jnp.bfloat16)
        rows, span = mixed.shape[0], mixed.shape[1]
        preact = jnp.dot(
            mixed.reshape(rows * span, channels), point, preferred_element_type=jnp.float32
        ).reshape(rows, span, channels) + offset_vec
        mixes.append(mixed)
        preacts.append(preact)
        activation = (
            (activation[:, 1:-1].astype(jnp.float32) + gelu_pair(preact)[0]) * live
        ).astype(jnp.bfloat16)
    final_halo = X_HALO - layers
    outcome = activation[:, final_halo : final_halo + breadth]

    cotangent = g_wide
    depth_terms, point_terms, bias_terms = [None] * layers, [None] * layers, [None] * layers
    for p in range(layers - 1, -1, -1):
        depth, point, _ = weights[p]
        halo_c = (cotangent.shape[1] - breadth) // 2
        halo_p = (preacts[p].shape[1] - breadth) // 2
        shift = halo_p - halo_c
        span = cotangent.shape[1]
        preact = preacts[p][:, shift : shift + span]
        masked = cotangent.astype(jnp.float32) * live
        gated = (masked * gelu_pair(preact)[1]).astype(jnp.bfloat16)
        back_mix = lax.dot_general(
            gated.reshape(height * span, channels),
            point,
            (((1,), (1,)), ((), ())),
            preferred_element_type=jnp.float32,
        ).reshape(height, span, channels).astype(jnp.bfloat16)

        gate_in = gated[:, halo_c : halo_c + breadth].reshape(height * breadth, channels)
        mix_in = mixes[p][:, halo_p : halo_p + breadth].reshape(height * breadth, channels)
        point_terms[p] = lax.dot_general(
            mix_in, gate_in, (((0,), (0,)), ((), ())), preferred_element_type=jnp.float32
        )
        bias_terms[p] = jnp.sum(gate_in.astype(jnp.float32), axis=0)
        back_in = back_mix[:, halo_c : halo_c + breadth].astype(jnp.float32)
        padded = pad_rows(acts[p])
        halo_a = (acts[p].shape[1] - breadth) // 2
        rows_k = []
        for i in range(3):
            row_k = []
            for j in range(3):
                start = halo_a - 1 + j
                row_k.append(
                    jnp.sum(
                        back_in * padded[i : i + height, start : start + breadth].astype(jnp.float32),
                        axis=(0, 1),
                    )
                )
            rows_k.append(jnp.stack(row_k))
        depth_terms[p] = jnp.stack(rows_k)

        earlier = conv_backward(pad_rows(back_mix), depth)
        cotangent = ((masked[:, 1:-1] + earlier) * live).astype(jnp.bfloat16)
    input_grad = cotangent

    got_outcome = lax.ppermute(outcome, "pipe", [(0, 1)])
    got_grad = lax.ppermute(input_grad, "pipe", [(1, 0)])
    first = jnp.where(core == 0, input_grad, got_outcome)
    second = jnp.where(core == 0, got_grad, outcome)
    result = jnp.stack([first, second])[None]

    pieces = (jnp.stack(depth_terms), jnp.stack(point_terms), jnp.stack(bias_terms))
    flat = jnp.concatenate([piece.reshape(layers, -1) for piece in pieces], axis=1)
    flat = all_reduce(flat, core)
    factor = 1.0 / math.sqrt(held.shape[0] * height * breadth * blk_count())
    by_layer = []
    for w in range(layers):
        picked = jnp.zeros_like(flat[0])
        for p in range(layers):
            picked = picked + jnp.where(layer_order[p] == w, flat[p], 0.0)
        by_layer.append(picked)
    flat = jnp.stack(by_layer) * factor
    ordered, at = [], 0
    for piece in pieces:
        width = piece[0].size
        ordered.append(flat[:, at : at + width].reshape(piece.shape))
        at += width
    return (result, ordered[0], ordered[1], ordered[2])


def solution(mesh):
    devices = mesh.devices
    blk = devices.shape[0]
    y_size = 4 if blk % 4 == 0 else 1
    rest = blk // y_size
    z_size = 8 if rest % 8 == 0 else rest
    x_size = rest // z_size
    torus = Mesh(devices.reshape(x_size, z_size, y_size, devices.shape[1]), BLK_AXES + ("pipe",))
    spec = P("pipe", None, None, BLK_AXES, None)
    in_specs = (spec, P(), P(), P(), P(), P())
    out_specs = (spec, P(), P(), P())
    return jax.shard_map(shards, mesh=torus, in_specs=in_specs, out_specs=out_specs, check_vma=False)
```

```python
import math

import jax
import jax.numpy as jnp
from jax import lax
from jax.experimental import pallas as pl
from jax.experimental.pallas import tpu as pltpu
from jax.sharding import Mesh, PartitionSpec as P

MESH_ID = pl.DeviceIdType.MESH

root_half = 0.7071067811865476
density_norm = 0.3989422804014327

X_HALO = 8
G_HALO = 4


BLK_AXES = ("x", "z", "y")


def blk_count():
    count = 1
    for axis in BLK_AXES:
        count *= lax.axis_size(axis)
    return count


def gelu_pair(preact):
    normal_cdf = 0.5 * (1.0 + lax.erf(preact * root_half))
    normal_pdf = density_norm * jnp.exp(-0.5 * preact * preact)
    return (preact * normal_cdf, normal_cdf + preact * normal_pdf)


def select_row(table, chosen):
    return lax.dynamic_index_in_dim(table, chosen, 0, keepdims=False)


def pad_rows(x):
    return jnp.pad(x, ((1, 1), (0, 0), (0, 0)))


def conv_forward(padded, depth):
    height = padded.shape[0] - 2
    breadth = padded.shape[1] - 2
    acc = jnp.zeros((height, breadth, padded.shape[2]), jnp.float32)
    for i in range(3):
        for j in range(3):
            acc = acc + depth[i, j] * padded[i : i + height, j : j + breadth].astype(jnp.float32)
    return acc


def conv_backward(spread, depth):
    height = spread.shape[0] - 2
    breadth = spread.shape[1] - 2
    acc = jnp.zeros((height, breadth, spread.shape[2]), jnp.float32)
    for i in range(3):
        for j in range(3):
            acc = acc + depth[i, j] * spread[
                2 - i : 2 - i + height, 2 - j : 2 - j + breadth
            ].astype(jnp.float32)
    return acc


def torus_coords(b):
    y_size, z_size = lax.axis_size("y"), lax.axis_size("z")
    return (b // (y_size * z_size), lax.rem(b // y_size, z_size), lax.rem(b, y_size))


def exchange_kernel(held_ref, edges_ref, body_out, lo_out, hi_out, body, lo, hi, send_sem, recv_sem):
    core = lax.axis_index("pipe")
    count = blk_count()
    here = (lax.axis_index("x") * lax.axis_size("z") + lax.axis_index("z")) * lax.axis_size("y") + lax.axis_index("y")
    right = torus_coords(lax.rem(here + 1, count))
    left = torus_coords(lax.rem(here + count - 1, count))
    mine = torus_coords(here)
    partner = mine + (1 - core,)
    targets = [partner] + [right + (m,) for m in range(2)] + [left + (m,) for m in range(2)]

    barrier = pltpu.get_barrier_semaphore()
    for target in targets:
        pl.semaphore_signal(barrier, inc=1, device_id=target, device_id_type=MESH_ID)
    pl.semaphore_wait(barrier, len(targets))

    copies = [
        pltpu.make_async_remote_copy(
            src_ref=held_ref.at[1 - core], dst_ref=body,
            send_sem=send_sem.at[0], recv_sem=recv_sem.at[0],
            device_id=partner, device_id_type=MESH_ID,
        )
    ]
    for m in range(2):
        copies.append(pltpu.make_async_remote_copy(
            src_ref=edges_ref.at[1, m], dst_ref=lo.at[core],
            send_sem=send_sem.at[1 + m], recv_sem=recv_sem.at[1 + core],
            device_id=right + (m,), device_id_type=MESH_ID,
        ))
        copies.append(pltpu.make_async_remote_copy(
            src_ref=edges_ref.at[0, m], dst_ref=hi.at[core],
            send_sem=send_sem.at[3 + m], recv_sem=recv_sem.at[3 + core],
            device_id=left + (m,), device_id_type=MESH_ID,
        ))
    for copy in copies:
        copy.start()
    copies[0].wait_recv()
    for k in range(2):
        pltpu.make_async_remote_copy(
            src_ref=edges_ref.at[1, k], dst_ref=lo.at[k],
            send_sem=send_sem.at[1 + k], recv_sem=recv_sem.at[1 + k],
            device_id=right + (k,), device_id_type=MESH_ID,
        ).wait_recv()
        pltpu.make_async_remote_copy(
            src_ref=edges_ref.at[0, k], dst_ref=hi.at[k],
            send_sem=send_sem.at[3 + k], recv_sem=recv_sem.at[3 + k],
            device_id=left + (k,), device_id_type=MESH_ID,
        ).wait_recv()
    for copy in copies:
        copy.wait_send()
    body_out[...] = body[...]
    lo_out[...] = lo[...]
    hi_out[...] = hi[...]


def exchange(held, edges):
    grid_shape = held.shape[1:]
    strip_shape = edges.shape[2:]
    vmem = pl.BlockSpec(memory_space=pltpu.VMEM)
    return pl.pallas_call(
        exchange_kernel,
        out_shape=(
            jax.ShapeDtypeStruct(grid_shape, held.dtype),
            jax.ShapeDtypeStruct((2,) + strip_shape, held.dtype),
            jax.ShapeDtypeStruct((2,) + strip_shape, held.dtype),
        ),
        in_specs=[vmem, vmem],
        out_specs=(vmem, vmem, vmem),
        scratch_shapes=[
            pltpu.VMEM(grid_shape, held.dtype),
            pltpu.VMEM((2,) + strip_shape, held.dtype),
            pltpu.VMEM((2,) + strip_shape, held.dtype),
            pltpu.SemaphoreType.DMA((5,)),
            pltpu.SemaphoreType.DMA((5,)),
        ],
        compiler_params=pltpu.CompilerParams(collective_id=0, has_side_effects=True),
    )(held, edges)


def group_members(axis):
    here = [lax.axis_index(name) for name in BLK_AXES] + [lax.axis_index("pipe")]
    slot = BLK_AXES.index(axis)
    return [tuple(here[:slot]) + (j,) + tuple(here[slot + 1 :]) for j in range(lax.axis_size(axis))]


def tree_sum(values):
    while len(values) > 1:
        values = [values[k] + values[k + 1] for k in range(0, len(values), 2)]
    return values[0]


def reduce_kernel(flat_ref, out_ref, own, part, whole, got_pipe, got_y, got_z, got_x, got_back, got_end,
                  send_sem, recv_pipe, recv_y, recv_z, recv_x, recv_back, recv_end):
    core = lax.axis_index("pipe")
    here = tuple(lax.axis_index(name) for name in BLK_AXES)
    partner = here + (1 - core,)
    my_y, my_z, my_x = (lax.axis_index(name) for name in ("y", "z", "x"))
    groups = {axis: group_members(axis) for axis in ("y", "z", "x")}

    barrier = pltpu.get_barrier_semaphore()
    pl.semaphore_signal(barrier, inc=1, device_id=partner, device_id_type=MESH_ID)
    count = 1
    for axis, mine in (("y", my_y), ("z", my_z), ("x", my_x)):
        for j, member in enumerate(groups[axis]):
            @pl.when(j != mine)
            def _():
                pl.semaphore_signal(barrier, inc=1, device_id=member, device_id_type=MESH_ID)
        count += len(groups[axis]) - 1
    pl.semaphore_wait(barrier, count)

    sends = iter(range(send_sem.shape[0]))

    def one(src, dst, sem, target):
        copy = pltpu.make_async_remote_copy(
            src_ref=src, dst_ref=dst, send_sem=send_sem.at[next(sends)], recv_sem=sem,
            device_id=target, device_id_type=MESH_ID,
        )
        copy.start()
        copy.wait()

    def spread(axis, mine, src_of, dst, sems):
        copies = []
        for j, member in enumerate(groups[axis]):
            copy = pltpu.make_async_remote_copy(
                src_ref=src_of(j), dst_ref=dst.at[mine], send_sem=send_sem.at[next(sends)],
                recv_sem=sems.at[mine], device_id=member, device_id_type=MESH_ID,
            )
            copies.append((j, copy))

            @pl.when(j != mine)
            def _():
                copy.start()
        for j, copy in copies:
            @pl.when(j != mine)
            def _():
                copy.wait_send()
                pltpu.make_async_remote_copy(
                    src_ref=src_of(j), dst_ref=dst.at[j], send_sem=send_sem.at[0],
                    recv_sem=sems.at[j], device_id=groups[axis][j], device_id_type=MESH_ID,
                ).wait_recv()

    one(flat_ref.at[1 - core], got_pipe, recv_pipe.at[0], partner)
    own[...] = flat_ref[core] + got_pipe[...]

    ny = len(groups["y"])
    got_y[my_y] = own[my_y]
    spread("y", my_y, lambda j: own.at[j], got_y, recv_y)
    part[...] = tree_sum([got_y[k] for k in range(ny)])

    got_z[my_z] = part[...]
    spread("z", my_z, lambda j: part, got_z, recv_z)
    part[...] = tree_sum([got_z[k] for k in range(len(groups["z"]))])

    got_x[my_x] = part[...]
    spread("x", my_x, lambda j: part, got_x, recv_x)
    part[...] = tree_sum([got_x[k] for k in range(len(groups["x"]))])

    got_back[my_y] = part[...]
    spread("y", my_y, lambda j: part, got_back, recv_back)

    one(got_back, got_end, recv_end.at[0], partner)
    out_ref[core] = got_back[...]
    out_ref[1 - core] = got_end[...]


def all_reduce(flat):
    halves, ny, rows, lanes = flat.shape
    nz, nx = lax.axis_size("z"), lax.axis_size("x")
    chunk = (rows, lanes)
    sends = 1 + ny + nz + nx + ny + 1
    vmem = pl.BlockSpec(memory_space=pltpu.VMEM)
    return pl.pallas_call(
        reduce_kernel,
        out_shape=jax.ShapeDtypeStruct(flat.shape, flat.dtype),
        in_specs=[vmem],
        out_specs=vmem,
        scratch_shapes=[
            pltpu.VMEM((ny,) + chunk, flat.dtype),
            pltpu.VMEM(chunk, flat.dtype),
            pltpu.VMEM((ny,) + chunk, flat.dtype),
            pltpu.VMEM((ny,) + chunk, flat.dtype),
            pltpu.VMEM((ny,) + chunk, flat.dtype),
            pltpu.VMEM((nz,) + chunk, flat.dtype),
            pltpu.VMEM((nx,) + chunk, flat.dtype),
            pltpu.VMEM((ny,) + chunk, flat.dtype),
            pltpu.VMEM((ny,) + chunk, flat.dtype),
            pltpu.SemaphoreType.DMA((sends,)),
            pltpu.SemaphoreType.DMA((1,)),
            pltpu.SemaphoreType.DMA((ny,)),
            pltpu.SemaphoreType.DMA((nz,)),
            pltpu.SemaphoreType.DMA((nx,)),
            pltpu.SemaphoreType.DMA((ny,)),
            pltpu.SemaphoreType.DMA((1,)),
        ],
        compiler_params=pltpu.CompilerParams(collective_id=1, has_side_effects=True),
    )(flat)


def shards(endpoints, row_counts, layer_order, depth_weight, point_weight, point_bias):
    held = endpoints[0]
    height = held.shape[1]
    breadth = held.shape[2]
    channels = held.shape[3]
    layers = layer_order.shape[0]
    core = lax.axis_index("pipe")

    edges = jnp.stack([held[:, :, :X_HALO], held[:, :, breadth - X_HALO :]])
    body, lo, hi = exchange(held, edges)
    mine = select_row(held, core)
    x_in = jnp.where(core == 0, mine, body)
    g_in = jnp.where(core == 0, body, mine)
    x_wide = jnp.concatenate([lo[0], x_in, hi[0]], axis=1)
    g_wide = jnp.concatenate([lo[1][:, X_HALO - G_HALO :], g_in, hi[1][:, :G_HALO]], axis=1)

    live = (jnp.arange(height)[:, None, None] < select_row(row_counts, core)).astype(jnp.float32)

    weights = []
    for p in range(layers):
        w = layer_order[p]
        weights.append(
            (select_row(depth_weight, w), select_row(point_weight, w), select_row(point_bias, w))
        )

    activation = (x_wide.astype(jnp.float32) * live).astype(jnp.bfloat16)
    acts, mixes, preacts = [], [], []
    for p in range(layers):
        depth, point, offset_vec = weights[p]
        acts.append(activation)
        mixed = conv_forward(pad_rows(activation), depth).astype(jnp.bfloat16)
        rows, span = mixed.shape[0], mixed.shape[1]
        preact = jnp.dot(
            mixed.reshape(rows * span, channels), point, preferred_element_type=jnp.float32
        ).reshape(rows, span, channels) + offset_vec
        mixes.append(mixed)
        preacts.append(preact)
        activation = (
            (activation[:, 1:-1].astype(jnp.float32) + gelu_pair(preact)[0]) * live
        ).astype(jnp.bfloat16)
    final_halo = X_HALO - layers
    outcome = activation[:, final_halo : final_halo + breadth]

    cotangent = g_wide
    depth_terms, point_terms, bias_terms = [None] * layers, [None] * layers, [None] * layers
    for p in range(layers - 1, -1, -1):
        depth, point, _ = weights[p]
        halo_c = (cotangent.shape[1] - breadth) // 2
        halo_p = (preacts[p].shape[1] - breadth) // 2
        shift = halo_p - halo_c
        span = cotangent.shape[1]
        preact = preacts[p][:, shift : shift + span]
        masked = cotangent.astype(jnp.float32) * live
        gated = (masked * gelu_pair(preact)[1]).astype(jnp.bfloat16)
        back_mix = lax.dot_general(
            gated.reshape(height * span, channels),
            point,
            (((1,), (1,)), ((), ())),
            preferred_element_type=jnp.float32,
        ).reshape(height, span, channels).astype(jnp.bfloat16)

        gate_in = gated[:, halo_c : halo_c + breadth].reshape(height * breadth, channels)
        mix_in = mixes[p][:, halo_p : halo_p + breadth].reshape(height * breadth, channels)
        point_terms[p] = lax.dot_general(
            mix_in, gate_in, (((0,), (0,)), ((), ())), preferred_element_type=jnp.float32
        )
        bias_terms[p] = jnp.sum(gate_in.astype(jnp.float32), axis=0)
        back_in = back_mix[:, halo_c : halo_c + breadth].astype(jnp.float32)
        padded = pad_rows(acts[p])
        halo_a = (acts[p].shape[1] - breadth) // 2
        rows_k = []
        for i in range(3):
            row_k = []
            for j in range(3):
                start = halo_a - 1 + j
                row_k.append(
                    jnp.sum(
                        back_in * padded[i : i + height, start : start + breadth].astype(jnp.float32),
                        axis=(0, 1),
                    )
                )
            rows_k.append(jnp.stack(row_k))
        depth_terms[p] = jnp.stack(rows_k)

        earlier = conv_backward(pad_rows(back_mix), depth)
        cotangent = ((masked[:, 1:-1] + earlier) * live).astype(jnp.bfloat16)
    input_grad = cotangent

    got_outcome = lax.ppermute(outcome, "pipe", [(0, 1)])
    got_grad = lax.ppermute(input_grad, "pipe", [(1, 0)])
    first = jnp.where(core == 0, input_grad, got_outcome)
    second = jnp.where(core == 0, got_grad, outcome)
    result = jnp.stack([first, second])[None]

    pieces = (jnp.stack(depth_terms), jnp.stack(point_terms), jnp.stack(bias_terms))
    flat = jnp.concatenate([piece.reshape(layers, -1) for piece in pieces], axis=1)
    ny = lax.axis_size("y")
    size = flat.size
    rows = -(-size // (2 * ny * 128))
    rows = -(-rows // 8) * 8
    packed = jnp.pad(flat.reshape(-1), (0, 2 * ny * rows * 128 - size)).reshape(2, ny, rows, 128)
    flat = all_reduce(packed).reshape(-1)[:size].reshape(flat.shape)
    factor = 1.0 / math.sqrt(held.shape[0] * height * breadth * blk_count())
    by_layer = []
    for w in range(layers):
        picked = jnp.zeros_like(flat[0])
        for p in range(layers):
            picked = picked + jnp.where(layer_order[p] == w, flat[p], 0.0)
        by_layer.append(picked)
    flat = jnp.stack(by_layer) * factor
    ordered, at = [], 0
    for piece in pieces:
        width = piece[0].size
        ordered.append(flat[:, at : at + width].reshape(piece.shape))
        at += width
    return (result, ordered[0], ordered[1], ordered[2])


def solution(mesh):
    devices = mesh.devices
    blk = devices.shape[0]
    y_size = 4 if blk % 4 == 0 else 1
    rest = blk // y_size
    z_size = 8 if rest % 8 == 0 else rest
    x_size = rest // z_size
    torus = Mesh(devices.reshape(x_size, z_size, y_size, devices.shape[1]), BLK_AXES + ("pipe",))
    spec = P("pipe", None, None, BLK_AXES, None)
    in_specs = (spec, P(), P(), P(), P(), P())
    out_specs = (spec, P(), P(), P())
    return jax.shard_map(shards, mesh=torus, in_specs=in_specs, out_specs=out_specs, check_vma=False)
```

```python
import math

import jax
import jax.numpy as jnp
from jax import lax
from jax.experimental import pallas as pl
from jax.experimental.pallas import tpu as pltpu
from jax.sharding import Mesh, PartitionSpec as P

MESH_ID = pl.DeviceIdType.MESH

root_half = 0.7071067811865476
density_norm = 0.3989422804014327

X_HALO = 8
G_HALO = 4


BLK_AXES = ("x", "z", "y")


def blk_count():
    count = 1
    for axis in BLK_AXES:
        count *= lax.axis_size(axis)
    return count


def gelu_pair(preact):
    normal_cdf = 0.5 * (1.0 + lax.erf(preact * root_half))
    normal_pdf = density_norm * jnp.exp(-0.5 * preact * preact)
    return (preact * normal_cdf, normal_cdf + preact * normal_pdf)


def select_row(table, chosen):
    return lax.dynamic_index_in_dim(table, chosen, 0, keepdims=False)


def pad_rows(x):
    return jnp.pad(x, ((1, 1), (0, 0), (0, 0)))


def conv_forward(padded, depth):
    height = padded.shape[0] - 2
    breadth = padded.shape[1] - 2
    acc = jnp.zeros((height, breadth, padded.shape[2]), jnp.float32)
    for i in range(3):
        for j in range(3):
            acc = acc + depth[i, j] * padded[i : i + height, j : j + breadth].astype(jnp.float32)
    return acc


def conv_backward(spread, depth):
    height = spread.shape[0] - 2
    breadth = spread.shape[1] - 2
    acc = jnp.zeros((height, breadth, spread.shape[2]), jnp.float32)
    for i in range(3):
        for j in range(3):
            acc = acc + depth[i, j] * spread[
                2 - i : 2 - i + height, 2 - j : 2 - j + breadth
            ].astype(jnp.float32)
    return acc


def torus_coords(b):
    y_size, z_size = lax.axis_size("y"), lax.axis_size("z")
    return (b // (y_size * z_size), lax.rem(b // y_size, z_size), lax.rem(b, y_size))


def exchange_kernel(held_ref, edges_ref, body_out, lo_out, hi_out, body, lo, hi, send_sem, recv_sem):
    core = lax.axis_index("pipe")
    count = blk_count()
    here = (lax.axis_index("x") * lax.axis_size("z") + lax.axis_index("z")) * lax.axis_size("y") + lax.axis_index("y")
    right = torus_coords(lax.rem(here + 1, count))
    left = torus_coords(lax.rem(here + count - 1, count))
    mine = torus_coords(here)
    partner = mine + (1 - core,)
    targets = [partner] + [right + (m,) for m in range(2)] + [left + (m,) for m in range(2)]

    barrier = pltpu.get_barrier_semaphore()
    for target in targets:
        pl.semaphore_signal(barrier, inc=1, device_id=target, device_id_type=MESH_ID)
    pl.semaphore_wait(barrier, len(targets))

    copies = [
        pltpu.make_async_remote_copy(
            src_ref=held_ref.at[1 - core], dst_ref=body,
            send_sem=send_sem.at[0], recv_sem=recv_sem.at[0],
            device_id=partner, device_id_type=MESH_ID,
        )
    ]
    for m in range(2):
        copies.append(pltpu.make_async_remote_copy(
            src_ref=edges_ref.at[1, m], dst_ref=lo.at[core],
            send_sem=send_sem.at[1 + m], recv_sem=recv_sem.at[1 + core],
            device_id=right + (m,), device_id_type=MESH_ID,
        ))
        copies.append(pltpu.make_async_remote_copy(
            src_ref=edges_ref.at[0, m], dst_ref=hi.at[core],
            send_sem=send_sem.at[3 + m], recv_sem=recv_sem.at[3 + core],
            device_id=left + (m,), device_id_type=MESH_ID,
        ))
    for copy in copies:
        copy.start()
    copies[0].wait_recv()
    for k in range(2):
        pltpu.make_async_remote_copy(
            src_ref=edges_ref.at[1, k], dst_ref=lo.at[k],
            send_sem=send_sem.at[1 + k], recv_sem=recv_sem.at[1 + k],
            device_id=right + (k,), device_id_type=MESH_ID,
        ).wait_recv()
        pltpu.make_async_remote_copy(
            src_ref=edges_ref.at[0, k], dst_ref=hi.at[k],
            send_sem=send_sem.at[3 + k], recv_sem=recv_sem.at[3 + k],
            device_id=left + (k,), device_id_type=MESH_ID,
        ).wait_recv()
    for copy in copies:
        copy.wait_send()
    body_out[...] = body[...]
    lo_out[...] = lo[...]
    hi_out[...] = hi[...]


def exchange(held, edges):
    grid_shape = held.shape[1:]
    strip_shape = edges.shape[2:]
    vmem = pl.BlockSpec(memory_space=pltpu.VMEM)
    return pl.pallas_call(
        exchange_kernel,
        out_shape=(
            jax.ShapeDtypeStruct(grid_shape, held.dtype),
            jax.ShapeDtypeStruct((2,) + strip_shape, held.dtype),
            jax.ShapeDtypeStruct((2,) + strip_shape, held.dtype),
        ),
        in_specs=[vmem, vmem],
        out_specs=(vmem, vmem, vmem),
        scratch_shapes=[
            pltpu.VMEM(grid_shape, held.dtype),
            pltpu.VMEM((2,) + strip_shape, held.dtype),
            pltpu.VMEM((2,) + strip_shape, held.dtype),
            pltpu.SemaphoreType.DMA((5,)),
            pltpu.SemaphoreType.DMA((5,)),
        ],
        compiler_params=pltpu.CompilerParams(collective_id=0, has_side_effects=True),
    )(held, edges)


def group_members(axis):
    here = [lax.axis_index(name) for name in BLK_AXES] + [lax.axis_index("pipe")]
    slot = BLK_AXES.index(axis)
    return [tuple(here[:slot]) + (j,) + tuple(here[slot + 1 :]) for j in range(lax.axis_size(axis))]


def tree_sum(values):
    while len(values) > 1:
        values = [values[k] + values[k + 1] for k in range(0, len(values), 2)]
    return values[0]


def reduce_kernel(flat_ref, out_ref, own, part, whole, got_pipe, got_y, got_z, got_x, got_back, got_end,
                  send_sem, recv_pipe, recv_y, recv_z, recv_x, recv_back, recv_end):
    core = lax.axis_index("pipe")
    here = tuple(lax.axis_index(name) for name in BLK_AXES)
    partner = here + (1 - core,)
    my_y, my_z, my_x = (lax.axis_index(name) for name in ("y", "z", "x"))
    groups = {axis: group_members(axis) for axis in ("y", "z", "x")}

    barrier = pltpu.get_barrier_semaphore()
    pl.semaphore_signal(barrier, inc=1, device_id=partner, device_id_type=MESH_ID)
    count = 1
    for axis, mine in (("y", my_y), ("z", my_z), ("x", my_x)):
        for j, member in enumerate(groups[axis]):
            @pl.when(j != mine)
            def _():
                pl.semaphore_signal(barrier, inc=1, device_id=member, device_id_type=MESH_ID)
        count += len(groups[axis]) - 1
    pl.semaphore_wait(barrier, count)

    sends = iter(range(send_sem.shape[0]))

    def one(src, dst, sem, target):
        copy = pltpu.make_async_remote_copy(
            src_ref=src, dst_ref=dst, send_sem=send_sem.at[next(sends)], recv_sem=sem,
            device_id=target, device_id_type=MESH_ID,
        )
        copy.start()
        copy.wait()

    def spread(axis, mine, src_of, dst, sems):
        copies = []
        for j, member in enumerate(groups[axis]):
            copy = pltpu.make_async_remote_copy(
                src_ref=src_of(j), dst_ref=dst.at[mine], send_sem=send_sem.at[next(sends)],
                recv_sem=sems.at[mine], device_id=member, device_id_type=MESH_ID,
            )
            copies.append((j, copy))

            @pl.when(j != mine)
            def _():
                copy.start()
        for j, copy in copies:
            @pl.when(j != mine)
            def _():
                copy.wait_send()
                pltpu.make_async_remote_copy(
                    src_ref=src_of(j), dst_ref=dst.at[j], send_sem=send_sem.at[0],
                    recv_sem=sems.at[j], device_id=groups[axis][j], device_id_type=MESH_ID,
                ).wait_recv()

    one(flat_ref.at[1 - core], got_pipe, recv_pipe.at[0], partner)
    own[...] = flat_ref[core] + got_pipe[...]

    ny = len(groups["y"])
    got_y[my_y] = own[my_y]
    spread("y", my_y, lambda j: own.at[j], got_y, recv_y)
    part[...] = tree_sum([got_y[k] for k in range(ny)])

    got_z[my_z] = part[...]
    spread("z", my_z, lambda j: part, got_z, recv_z)
    part[...] = tree_sum([got_z[k] for k in range(len(groups["z"]))])

    got_x[my_x] = part[...]
    spread("x", my_x, lambda j: part, got_x, recv_x)
    part[...] = tree_sum([got_x[k] for k in range(len(groups["x"]))])

    got_back[my_y] = part[...]
    spread("y", my_y, lambda j: part, got_back, recv_back)

    one(got_back, got_end, recv_end.at[0], partner)
    out_ref[core] = got_back[...]
    out_ref[1 - core] = got_end[...]


def all_reduce(flat):
    halves, ny, rows, lanes = flat.shape
    nz, nx = lax.axis_size("z"), lax.axis_size("x")
    chunk = (rows, lanes)
    sends = 1 + ny + nz + nx + ny + 1
    vmem = pl.BlockSpec(memory_space=pltpu.VMEM)
    return pl.pallas_call(
        reduce_kernel,
        out_shape=jax.ShapeDtypeStruct(flat.shape, flat.dtype),
        in_specs=[vmem],
        out_specs=vmem,
        scratch_shapes=[
            pltpu.VMEM((ny,) + chunk, flat.dtype),
            pltpu.VMEM(chunk, flat.dtype),
            pltpu.VMEM((ny,) + chunk, flat.dtype),
            pltpu.VMEM((ny,) + chunk, flat.dtype),
            pltpu.VMEM((ny,) + chunk, flat.dtype),
            pltpu.VMEM((nz,) + chunk, flat.dtype),
            pltpu.VMEM((nx,) + chunk, flat.dtype),
            pltpu.VMEM((ny,) + chunk, flat.dtype),
            pltpu.VMEM((ny,) + chunk, flat.dtype),
            pltpu.SemaphoreType.DMA((sends,)),
            pltpu.SemaphoreType.DMA((1,)),
            pltpu.SemaphoreType.DMA((ny,)),
            pltpu.SemaphoreType.DMA((nz,)),
            pltpu.SemaphoreType.DMA((nx,)),
            pltpu.SemaphoreType.DMA((ny,)),
            pltpu.SemaphoreType.DMA((1,)),
        ],
        compiler_params=pltpu.CompilerParams(collective_id=1, has_side_effects=True),
    )(flat)


def shards(endpoints, row_counts, layer_order, depth_weight, point_weight, point_bias):
    held = endpoints[0]
    height = held.shape[1]
    breadth = held.shape[2]
    channels = held.shape[3]
    layers = layer_order.shape[0]
    core = lax.axis_index("pipe")

    edges = jnp.stack([held[:, :, :X_HALO], held[:, :, breadth - X_HALO :]])
    body, lo, hi = exchange(held, edges)
    mine = select_row(held, core)
    x_in = jnp.where(core == 0, mine, body)
    g_in = jnp.where(core == 0, body, mine)
    x_wide = jnp.concatenate([lo[0], x_in, hi[0]], axis=1)
    g_wide = jnp.concatenate([lo[1][:, X_HALO - G_HALO :], g_in, hi[1][:, :G_HALO]], axis=1)

    live = (jnp.arange(height)[:, None, None] < select_row(row_counts, core)).astype(jnp.float32)

    weights = []
    for p in range(layers):
        w = layer_order[p]
        weights.append(
            (select_row(depth_weight, w), select_row(point_weight, w), select_row(point_bias, w))
        )

    activation = (x_wide.astype(jnp.float32) * live).astype(jnp.bfloat16)
    acts, mixes, preacts = [], [], []
    for p in range(layers):
        depth, point, offset_vec = weights[p]
        acts.append(activation)
        mixed = conv_forward(pad_rows(activation), depth).astype(jnp.bfloat16)
        rows, span = mixed.shape[0], mixed.shape[1]
        preact = jnp.dot(
            mixed.reshape(rows * span, channels), point, preferred_element_type=jnp.float32
        ).reshape(rows, span, channels) + offset_vec
        mixes.append(mixed)
        preacts.append(preact)
        activation = (
            (activation[:, 1:-1].astype(jnp.float32) + gelu_pair(preact)[0]) * live
        ).astype(jnp.bfloat16)
    final_halo = X_HALO - layers
    outcome = activation[:, final_halo : final_halo + breadth]

    cotangent = g_wide
    depth_terms, point_terms, bias_terms = [None] * layers, [None] * layers, [None] * layers
    for p in range(layers - 1, -1, -1):
        depth, point, _ = weights[p]
        halo_c = (cotangent.shape[1] - breadth) // 2
        halo_p = (preacts[p].shape[1] - breadth) // 2
        shift = halo_p - halo_c
        span = cotangent.shape[1]
        preact = preacts[p][:, shift : shift + span]
        masked = cotangent.astype(jnp.float32) * live
        gated = (masked * gelu_pair(preact)[1]).astype(jnp.bfloat16)
        back_mix = lax.dot_general(
            gated.reshape(height * span, channels),
            point,
            (((1,), (1,)), ((), ())),
            preferred_element_type=jnp.float32,
        ).reshape(height, span, channels).astype(jnp.bfloat16)

        gate_in = gated[:, halo_c : halo_c + breadth].reshape(height * breadth, channels)
        mix_in = mixes[p][:, halo_p : halo_p + breadth].reshape(height * breadth, channels)
        point_terms[p] = lax.dot_general(
            mix_in, gate_in, (((0,), (0,)), ((), ())), preferred_element_type=jnp.float32
        )
        bias_terms[p] = jnp.sum(gate_in.astype(jnp.float32), axis=0)
        back_in = back_mix[:, halo_c : halo_c + breadth].astype(jnp.float32)
        padded = pad_rows(acts[p])
        halo_a = (acts[p].shape[1] - breadth) // 2
        rows_k = []
        for i in range(3):
            row_k = []
            for j in range(3):
                start = halo_a - 1 + j
                row_k.append(
                    jnp.sum(
                        back_in * padded[i : i + height, start : start + breadth].astype(jnp.float32),
                        axis=(0, 1),
                    )
                )
            rows_k.append(jnp.stack(row_k))
        depth_terms[p] = jnp.stack(rows_k)

        earlier = conv_backward(pad_rows(back_mix), depth)
        cotangent = ((masked[:, 1:-1] + earlier) * live).astype(jnp.bfloat16)
    input_grad = cotangent

    got_outcome = lax.ppermute(outcome, "pipe", [(0, 1)])
    got_grad = lax.ppermute(input_grad, "pipe", [(1, 0)])
    first = jnp.where(core == 0, input_grad, got_outcome)
    second = jnp.where(core == 0, got_grad, outcome)
    result = jnp.stack([first, second])[None]

    pieces = (jnp.stack(depth_terms), jnp.stack(point_terms), jnp.stack(bias_terms))
    flat = jnp.concatenate([piece.reshape(layers, -1) for piece in pieces], axis=1)
    ny = lax.axis_size("y")
    size = flat.size
    rows = -(-size // (2 * ny * 128))
    rows = -(-rows // 8) * 8
    packed = jnp.pad(flat.reshape(-1), (0, 2 * ny * rows * 128 - size)).reshape(2, ny, rows, 128)
    flat = all_reduce(packed).reshape(-1)[:size].reshape(flat.shape)
    factor = 1.0 / math.sqrt(held.shape[0] * height * breadth * blk_count())
    chosen = layer_order[None, :] == jnp.arange(layers, dtype=layer_order.dtype)[:, None]
    flat = jnp.sum(jnp.where(chosen[:, :, None], flat[None, :, :], 0.0), axis=1) * factor
    ordered, at = [], 0
    for piece in pieces:
        width = piece[0].size
        ordered.append(flat[:, at : at + width].reshape(piece.shape))
        at += width
    return (result, ordered[0], ordered[1], ordered[2])


def solution(mesh):
    devices = mesh.devices
    blk = devices.shape[0]
    y_size = 4 if blk % 4 == 0 else 1
    rest = blk // y_size
    z_size = 8 if rest % 8 == 0 else rest
    x_size = rest // z_size
    torus = Mesh(devices.reshape(x_size, z_size, y_size, devices.shape[1]), BLK_AXES + ("pipe",))
    spec = P("pipe", None, None, BLK_AXES, None)
    in_specs = (spec, P(), P(), P(), P(), P())
    out_specs = (spec, P(), P(), P())
    return jax.shard_map(shards, mesh=torus, in_specs=in_specs, out_specs=out_specs, check_vma=False)
```

```python
import math

import jax
import jax.numpy as jnp
from jax import lax
from jax.experimental import pallas as pl
from jax.experimental.pallas import tpu as pltpu
from jax.sharding import Mesh, PartitionSpec as P

MESH_ID = pl.DeviceIdType.MESH

root_half = 0.7071067811865476
density_norm = 0.3989422804014327

X_HALO = 8
G_HALO = 4


BLK_AXES = ("x", "z", "y")


def blk_count():
    count = 1
    for axis in BLK_AXES:
        count *= lax.axis_size(axis)
    return count


def gelu_pair(preact):
    normal_cdf = 0.5 * (1.0 + lax.erf(preact * root_half))
    normal_pdf = density_norm * jnp.exp(-0.5 * preact * preact)
    return (preact * normal_cdf, normal_cdf + preact * normal_pdf)


def select_row(table, chosen):
    return lax.dynamic_index_in_dim(table, chosen, 0, keepdims=False)


def pad_rows(x):
    return jnp.pad(x, ((1, 1), (0, 0), (0, 0)))


def conv_forward(padded, depth):
    height = padded.shape[0] - 2
    breadth = padded.shape[1] - 2
    acc = jnp.zeros((height, breadth, padded.shape[2]), jnp.float32)
    for i in range(3):
        for j in range(3):
            acc = acc + depth[i, j] * padded[i : i + height, j : j + breadth].astype(jnp.float32)
    return acc


def conv_backward(spread, depth):
    height = spread.shape[0] - 2
    breadth = spread.shape[1] - 2
    acc = jnp.zeros((height, breadth, spread.shape[2]), jnp.float32)
    for i in range(3):
        for j in range(3):
            acc = acc + depth[i, j] * spread[
                2 - i : 2 - i + height, 2 - j : 2 - j + breadth
            ].astype(jnp.float32)
    return acc


def torus_coords(b):
    y_size, z_size = lax.axis_size("y"), lax.axis_size("z")
    return (b // (y_size * z_size), lax.rem(b // y_size, z_size), lax.rem(b, y_size))


def exchange_kernel(held_ref, edges_ref, body_out, lo_out, hi_out, body, lo, hi, send_sem, recv_sem):
    core = lax.axis_index("pipe")
    count = blk_count()
    here = (lax.axis_index("x") * lax.axis_size("z") + lax.axis_index("z")) * lax.axis_size("y") + lax.axis_index("y")
    right = torus_coords(lax.rem(here + 1, count))
    left = torus_coords(lax.rem(here + count - 1, count))
    mine = torus_coords(here)
    partner = mine + (1 - core,)
    targets = [partner] + [right + (m,) for m in range(2)] + [left + (m,) for m in range(2)]

    barrier = pltpu.get_barrier_semaphore()
    for target in targets:
        pl.semaphore_signal(barrier, inc=1, device_id=target, device_id_type=MESH_ID)
    pl.semaphore_wait(barrier, len(targets))

    copies = [
        pltpu.make_async_remote_copy(
            src_ref=held_ref.at[1 - core], dst_ref=body,
            send_sem=send_sem.at[0], recv_sem=recv_sem.at[0],
            device_id=partner, device_id_type=MESH_ID,
        )
    ]
    for m in range(2):
        copies.append(pltpu.make_async_remote_copy(
            src_ref=edges_ref.at[1, m], dst_ref=lo.at[core],
            send_sem=send_sem.at[1 + m], recv_sem=recv_sem.at[1 + core],
            device_id=right + (m,), device_id_type=MESH_ID,
        ))
        copies.append(pltpu.make_async_remote_copy(
            src_ref=edges_ref.at[0, m], dst_ref=hi.at[core],
            send_sem=send_sem.at[3 + m], recv_sem=recv_sem.at[3 + core],
            device_id=left + (m,), device_id_type=MESH_ID,
        ))
    for copy in copies:
        copy.start()
    copies[0].wait_recv()
    for k in range(2):
        pltpu.make_async_remote_copy(
            src_ref=edges_ref.at[1, k], dst_ref=lo.at[k],
            send_sem=send_sem.at[1 + k], recv_sem=recv_sem.at[1 + k],
            device_id=right + (k,), device_id_type=MESH_ID,
        ).wait_recv()
        pltpu.make_async_remote_copy(
            src_ref=edges_ref.at[0, k], dst_ref=hi.at[k],
            send_sem=send_sem.at[3 + k], recv_sem=recv_sem.at[3 + k],
            device_id=left + (k,), device_id_type=MESH_ID,
        ).wait_recv()
    for copy in copies:
        copy.wait_send()
    body_out[...] = body[...]
    lo_out[...] = lo[...]
    hi_out[...] = hi[...]


def exchange(held, edges):
    grid_shape = held.shape[1:]
    strip_shape = edges.shape[2:]
    vmem = pl.BlockSpec(memory_space=pltpu.VMEM)
    return pl.pallas_call(
        exchange_kernel,
        out_shape=(
            jax.ShapeDtypeStruct(grid_shape, held.dtype),
            jax.ShapeDtypeStruct((2,) + strip_shape, held.dtype),
            jax.ShapeDtypeStruct((2,) + strip_shape, held.dtype),
        ),
        in_specs=[vmem, vmem],
        out_specs=(vmem, vmem, vmem),
        scratch_shapes=[
            pltpu.VMEM(grid_shape, held.dtype),
            pltpu.VMEM((2,) + strip_shape, held.dtype),
            pltpu.VMEM((2,) + strip_shape, held.dtype),
            pltpu.SemaphoreType.DMA((5,)),
            pltpu.SemaphoreType.DMA((5,)),
        ],
        compiler_params=pltpu.CompilerParams(collective_id=0, has_side_effects=True),
    )(held, edges)


def group_members(axis):
    here = [lax.axis_index(name) for name in BLK_AXES] + [lax.axis_index("pipe")]
    slot = BLK_AXES.index(axis)
    return [tuple(here[:slot]) + (j,) + tuple(here[slot + 1 :]) for j in range(lax.axis_size(axis))]


def tree_sum(values):
    while len(values) > 1:
        values = [values[k] + values[k + 1] for k in range(0, len(values), 2)]
    return values[0]


def reduce_kernel(flat_ref, out_ref, own, part, whole, got_pipe, got_y, got_z, got_x, got_back, got_end,
                  send_sem, recv_pipe, recv_y, recv_z, recv_x, recv_back, recv_end):
    core = lax.axis_index("pipe")
    here = tuple(lax.axis_index(name) for name in BLK_AXES)
    partner = here + (1 - core,)
    my_y, my_z, my_x = (lax.axis_index(name) for name in ("y", "z", "x"))
    groups = {axis: group_members(axis) for axis in ("y", "z", "x")}

    barrier = pltpu.get_barrier_semaphore()
    pl.semaphore_signal(barrier, inc=1, device_id=partner, device_id_type=MESH_ID)
    count = 1
    for axis, mine in (("y", my_y), ("z", my_z), ("x", my_x)):
        for j, member in enumerate(groups[axis]):
            @pl.when(j != mine)
            def _():
                pl.semaphore_signal(barrier, inc=1, device_id=member, device_id_type=MESH_ID)
        count += len(groups[axis]) - 1
    pl.semaphore_wait(barrier, count)

    sends = iter(range(send_sem.shape[0]))

    def one(src, dst, sem, target):
        copy = pltpu.make_async_remote_copy(
            src_ref=src, dst_ref=dst, send_sem=send_sem.at[next(sends)], recv_sem=sem,
            device_id=target, device_id_type=MESH_ID,
        )
        copy.start()
        copy.wait()

    def spread(axis, mine, src_of, dst, sems):
        copies = []
        for j, member in enumerate(groups[axis]):
            copy = pltpu.make_async_remote_copy(
                src_ref=src_of(j), dst_ref=dst.at[mine], send_sem=send_sem.at[next(sends)],
                recv_sem=sems.at[mine], device_id=member, device_id_type=MESH_ID,
            )
            copies.append((j, copy))

            @pl.when(j != mine)
            def _():
                copy.start()
        for j, copy in copies:
            @pl.when(j != mine)
            def _():
                copy.wait_send()
                pltpu.make_async_remote_copy(
                    src_ref=src_of(j), dst_ref=dst.at[j], send_sem=send_sem.at[0],
                    recv_sem=sems.at[j], device_id=groups[axis][j], device_id_type=MESH_ID,
                ).wait_recv()

    one(flat_ref.at[1 - core], got_pipe, recv_pipe.at[0], partner)
    own[...] = flat_ref[core] + got_pipe[...]

    ny = len(groups["y"])
    got_y[my_y] = own[my_y]
    spread("y", my_y, lambda j: own.at[j], got_y, recv_y)
    part[...] = tree_sum([got_y[k] for k in range(ny)])

    got_z[my_z] = part[...]
    spread("z", my_z, lambda j: part, got_z, recv_z)
    part[...] = tree_sum([got_z[k] for k in range(len(groups["z"]))])

    got_x[my_x] = part[...]
    spread("x", my_x, lambda j: part, got_x, recv_x)
    part[...] = tree_sum([got_x[k] for k in range(len(groups["x"]))])

    got_back[my_y] = part[...]
    spread("y", my_y, lambda j: part, got_back, recv_back)

    one(got_back, got_end, recv_end.at[0], partner)
    out_ref[core] = got_back[...]
    out_ref[1 - core] = got_end[...]


def all_reduce(flat):
    halves, ny, rows, lanes = flat.shape
    nz, nx = lax.axis_size("z"), lax.axis_size("x")
    chunk = (rows, lanes)
    sends = 1 + ny + nz + nx + ny + 1
    vmem = pl.BlockSpec(memory_space=pltpu.VMEM)
    return pl.pallas_call(
        reduce_kernel,
        out_shape=jax.ShapeDtypeStruct(flat.shape, flat.dtype),
        in_specs=[vmem],
        out_specs=vmem,
        scratch_shapes=[
            pltpu.VMEM((ny,) + chunk, flat.dtype),
            pltpu.VMEM(chunk, flat.dtype),
            pltpu.VMEM((ny,) + chunk, flat.dtype),
            pltpu.VMEM((ny,) + chunk, flat.dtype),
            pltpu.VMEM((ny,) + chunk, flat.dtype),
            pltpu.VMEM((nz,) + chunk, flat.dtype),
            pltpu.VMEM((nx,) + chunk, flat.dtype),
            pltpu.VMEM((ny,) + chunk, flat.dtype),
            pltpu.VMEM((ny,) + chunk, flat.dtype),
            pltpu.SemaphoreType.DMA((sends,)),
            pltpu.SemaphoreType.DMA((1,)),
            pltpu.SemaphoreType.DMA((ny,)),
            pltpu.SemaphoreType.DMA((nz,)),
            pltpu.SemaphoreType.DMA((nx,)),
            pltpu.SemaphoreType.DMA((ny,)),
            pltpu.SemaphoreType.DMA((1,)),
        ],
        compiler_params=pltpu.CompilerParams(collective_id=1, has_side_effects=True),
    )(flat)


def shards(endpoints, row_counts, layer_order, depth_weight, point_weight, point_bias):
    held = endpoints[0]
    height = held.shape[1]
    breadth = held.shape[2]
    channels = held.shape[3]
    layers = layer_order.shape[0]
    core = lax.axis_index("pipe")

    edges = jnp.stack([held[:, :, :X_HALO], held[:, :, breadth - X_HALO :]])
    body, lo, hi = exchange(held, edges)
    mine = select_row(held, core)
    x_in = jnp.where(core == 0, mine, body)
    g_in = jnp.where(core == 0, body, mine)
    x_wide = jnp.concatenate([lo[0], x_in, hi[0]], axis=1)
    g_wide = jnp.concatenate([lo[1][:, X_HALO - G_HALO :], g_in, hi[1][:, :G_HALO]], axis=1)

    counts = jnp.where(core == 0, row_counts[0:1], row_counts[1:2])
    live = (jnp.arange(height)[:, None, None] < counts[None, None, :]).astype(jnp.float32)

    placed = layer_order[:, None] == jnp.arange(layers, dtype=layer_order.dtype)[None, :]

    def pick(table):
        mask = placed.reshape(placed.shape + (1,) * (table.ndim - 1))
        return jnp.sum(jnp.where(mask, table[None], jnp.zeros((), table.dtype)), axis=1, dtype=table.dtype)

    by_position = [pick(table) for table in (depth_weight, point_weight, point_bias)]
    weights = [tuple(table[p] for table in by_position) for p in range(layers)]

    activation = (x_wide.astype(jnp.float32) * live).astype(jnp.bfloat16)
    acts, mixes, preacts = [], [], []
    for p in range(layers):
        depth, point, offset_vec = weights[p]
        acts.append(activation)
        mixed = conv_forward(pad_rows(activation), depth).astype(jnp.bfloat16)
        rows, span = mixed.shape[0], mixed.shape[1]
        preact = jnp.dot(
            mixed.reshape(rows * span, channels), point, preferred_element_type=jnp.float32
        ).reshape(rows, span, channels) + offset_vec
        mixes.append(mixed)
        preacts.append(preact)
        activation = (
            (activation[:, 1:-1].astype(jnp.float32) + gelu_pair(preact)[0]) * live
        ).astype(jnp.bfloat16)
    final_halo = X_HALO - layers
    outcome = activation[:, final_halo : final_halo + breadth]

    cotangent = g_wide
    depth_terms, point_terms, bias_terms = [None] * layers, [None] * layers, [None] * layers
    for p in range(layers - 1, -1, -1):
        depth, point, _ = weights[p]
        halo_c = (cotangent.shape[1] - breadth) // 2
        halo_p = (preacts[p].shape[1] - breadth) // 2
        shift = halo_p - halo_c
        span = cotangent.shape[1]
        preact = preacts[p][:, shift : shift + span]
        masked = cotangent.astype(jnp.float32) * live
        gated = (masked * gelu_pair(preact)[1]).astype(jnp.bfloat16)
        back_mix = lax.dot_general(
            gated.reshape(height * span, channels),
            point,
            (((1,), (1,)), ((), ())),
            preferred_element_type=jnp.float32,
        ).reshape(height, span, channels).astype(jnp.bfloat16)

        gate_in = gated[:, halo_c : halo_c + breadth].reshape(height * breadth, channels)
        mix_in = mixes[p][:, halo_p : halo_p + breadth].reshape(height * breadth, channels)
        point_terms[p] = lax.dot_general(
            mix_in, gate_in, (((0,), (0,)), ((), ())), preferred_element_type=jnp.float32
        )
        bias_terms[p] = jnp.sum(gate_in.astype(jnp.float32), axis=0)
        back_in = back_mix[:, halo_c : halo_c + breadth].astype(jnp.float32)
        padded = pad_rows(acts[p])
        halo_a = (acts[p].shape[1] - breadth) // 2
        rows_k = []
        for i in range(3):
            row_k = []
            for j in range(3):
                start = halo_a - 1 + j
                row_k.append(
                    jnp.sum(
                        back_in * padded[i : i + height, start : start + breadth].astype(jnp.float32),
                        axis=(0, 1),
                    )
                )
            rows_k.append(jnp.stack(row_k))
        depth_terms[p] = jnp.stack(rows_k)

        earlier = conv_backward(pad_rows(back_mix), depth)
        cotangent = ((masked[:, 1:-1] + earlier) * live).astype(jnp.bfloat16)
    input_grad = cotangent

    got_outcome = lax.ppermute(outcome, "pipe", [(0, 1)])
    got_grad = lax.ppermute(input_grad, "pipe", [(1, 0)])
    first = jnp.where(core == 0, input_grad, got_outcome)
    second = jnp.where(core == 0, got_grad, outcome)
    result = jnp.stack([first, second])[None]

    pieces = (jnp.stack(depth_terms), jnp.stack(point_terms), jnp.stack(bias_terms))
    flat = jnp.concatenate([piece.reshape(layers, -1) for piece in pieces], axis=1)
    ny = lax.axis_size("y")
    size = flat.size
    rows = -(-size // (2 * ny * 128))
    rows = -(-rows // 8) * 8
    packed = jnp.pad(flat.reshape(-1), (0, 2 * ny * rows * 128 - size)).reshape(2, ny, rows, 128)
    flat = all_reduce(packed).reshape(-1)[:size].reshape(flat.shape)
    factor = 1.0 / math.sqrt(held.shape[0] * height * breadth * blk_count())
    chosen = layer_order[None, :] == jnp.arange(layers, dtype=layer_order.dtype)[:, None]
    flat = jnp.sum(jnp.where(chosen[:, :, None], flat[None, :, :], 0.0), axis=1) * factor
    ordered, at = [], 0
    for piece in pieces:
        width = piece[0].size
        ordered.append(flat[:, at : at + width].reshape(piece.shape))
        at += width
    return (result, ordered[0], ordered[1], ordered[2])


def solution(mesh):
    devices = mesh.devices
    blk = devices.shape[0]
    y_size = 4 if blk % 4 == 0 else 1
    rest = blk // y_size
    z_size = 8 if rest % 8 == 0 else rest
    x_size = rest // z_size
    torus = Mesh(devices.reshape(x_size, z_size, y_size, devices.shape[1]), BLK_AXES + ("pipe",))
    spec = P("pipe", None, None, BLK_AXES, None)
    in_specs = (spec, P(), P(), P(), P(), P())
    out_specs = (spec, P(), P(), P())
    return jax.shard_map(shards, mesh=torus, in_specs=in_specs, out_specs=out_specs, check_vma=False)
```

```python
import math

import jax
import jax.numpy as jnp
from jax import lax
from jax.experimental import pallas as pl
from jax.experimental.pallas import tpu as pltpu
from jax.sharding import Mesh, PartitionSpec as P

MESH_ID = pl.DeviceIdType.MESH

root_half = 0.7071067811865476
density_norm = 0.3989422804014327

X_HALO = 8
G_HALO = 4


BLK_AXES = ("x", "z", "y")


def blk_count():
    count = 1
    for axis in BLK_AXES:
        count *= lax.axis_size(axis)
    return count


def gelu_pair(preact):
    normal_cdf = 0.5 * (1.0 + lax.erf(preact * root_half))
    normal_pdf = density_norm * jnp.exp(-0.5 * preact * preact)
    return (preact * normal_cdf, normal_cdf + preact * normal_pdf)


def select_row(table, chosen):
    return lax.dynamic_index_in_dim(table, chosen, 0, keepdims=False)


def pad_rows(x):
    return jnp.pad(x, ((1, 1), (0, 0), (0, 0)))


def conv_forward(padded, depth):
    height = padded.shape[0] - 2
    breadth = padded.shape[1] - 2
    acc = jnp.zeros((height, breadth, padded.shape[2]), jnp.float32)
    for i in range(3):
        for j in range(3):
            acc = acc + depth[i, j] * padded[i : i + height, j : j + breadth].astype(jnp.float32)
    return acc


def conv_backward(spread, depth):
    height = spread.shape[0] - 2
    breadth = spread.shape[1] - 2
    acc = jnp.zeros((height, breadth, spread.shape[2]), jnp.float32)
    for i in range(3):
        for j in range(3):
            acc = acc + depth[i, j] * spread[
                2 - i : 2 - i + height, 2 - j : 2 - j + breadth
            ].astype(jnp.float32)
    return acc


def torus_coords(b):
    y_size, z_size = lax.axis_size("y"), lax.axis_size("z")
    return (b // (y_size * z_size), lax.rem(b // y_size, z_size), lax.rem(b, y_size))


def exchange_kernel(held_ref, edges_ref, body_out, lo_out, hi_out, body, lo, hi, send_sem, recv_sem):
    core = lax.axis_index("pipe")
    count = blk_count()
    here = (lax.axis_index("x") * lax.axis_size("z") + lax.axis_index("z")) * lax.axis_size("y") + lax.axis_index("y")
    right = torus_coords(lax.rem(here + 1, count))
    left = torus_coords(lax.rem(here + count - 1, count))
    mine = torus_coords(here)
    partner = mine + (1 - core,)
    targets = [partner] + [right + (m,) for m in range(2)] + [left + (m,) for m in range(2)]

    barrier = pltpu.get_barrier_semaphore()
    for target in targets:
        pl.semaphore_signal(barrier, inc=1, device_id=target, device_id_type=MESH_ID)
    pl.semaphore_wait(barrier, len(targets))

    copies = [
        pltpu.make_async_remote_copy(
            src_ref=held_ref.at[1 - core], dst_ref=body,
            send_sem=send_sem.at[0], recv_sem=recv_sem.at[0],
            device_id=partner, device_id_type=MESH_ID,
        )
    ]
    for m in range(2):
        copies.append(pltpu.make_async_remote_copy(
            src_ref=edges_ref.at[1, m], dst_ref=lo.at[core],
            send_sem=send_sem.at[1 + m], recv_sem=recv_sem.at[1 + core],
            device_id=right + (m,), device_id_type=MESH_ID,
        ))
        copies.append(pltpu.make_async_remote_copy(
            src_ref=edges_ref.at[0, m], dst_ref=hi.at[core],
            send_sem=send_sem.at[3 + m], recv_sem=recv_sem.at[3 + core],
            device_id=left + (m,), device_id_type=MESH_ID,
        ))
    for copy in copies:
        copy.start()
    copies[0].wait_recv()
    for k in range(2):
        pltpu.make_async_remote_copy(
            src_ref=edges_ref.at[1, k], dst_ref=lo.at[k],
            send_sem=send_sem.at[1 + k], recv_sem=recv_sem.at[1 + k],
            device_id=right + (k,), device_id_type=MESH_ID,
        ).wait_recv()
        pltpu.make_async_remote_copy(
            src_ref=edges_ref.at[0, k], dst_ref=hi.at[k],
            send_sem=send_sem.at[3 + k], recv_sem=recv_sem.at[3 + k],
            device_id=left + (k,), device_id_type=MESH_ID,
        ).wait_recv()
    for copy in copies:
        copy.wait_send()
    body_out[...] = body[...]
    lo_out[...] = lo[...]
    hi_out[...] = hi[...]


def exchange(held, edges):
    grid_shape = held.shape[1:]
    strip_shape = edges.shape[2:]
    vmem = pl.BlockSpec(memory_space=pltpu.VMEM)
    return pl.pallas_call(
        exchange_kernel,
        out_shape=(
            jax.ShapeDtypeStruct(grid_shape, held.dtype),
            jax.ShapeDtypeStruct((2,) + strip_shape, held.dtype),
            jax.ShapeDtypeStruct((2,) + strip_shape, held.dtype),
        ),
        in_specs=[vmem, vmem],
        out_specs=(vmem, vmem, vmem),
        scratch_shapes=[
            pltpu.VMEM(grid_shape, held.dtype),
            pltpu.VMEM((2,) + strip_shape, held.dtype),
            pltpu.VMEM((2,) + strip_shape, held.dtype),
            pltpu.SemaphoreType.DMA((5,)),
            pltpu.SemaphoreType.DMA((5,)),
        ],
        compiler_params=pltpu.CompilerParams(collective_id=0, has_side_effects=True),
    )(held, edges)


def group_members(axis):
    here = [lax.axis_index(name) for name in BLK_AXES] + [lax.axis_index("pipe")]
    slot = BLK_AXES.index(axis)
    return [tuple(here[:slot]) + (j,) + tuple(here[slot + 1 :]) for j in range(lax.axis_size(axis))]


def tree_sum(values):
    while len(values) > 1:
        values = [values[k] + values[k + 1] for k in range(0, len(values), 2)]
    return values[0]


def reduce_kernel(flat_ref, out_ref, own, part, whole, got_pipe, got_y, got_z, got_x, got_back, got_end,
                  send_sem, recv_pipe, recv_y, recv_z, recv_x, recv_back, recv_end):
    core = lax.axis_index("pipe")
    here = tuple(lax.axis_index(name) for name in BLK_AXES)
    partner = here + (1 - core,)
    my_y, my_z, my_x = (lax.axis_index(name) for name in ("y", "z", "x"))
    groups = {axis: group_members(axis) for axis in ("y", "z", "x")}

    barrier = pltpu.get_barrier_semaphore()
    pl.semaphore_signal(barrier, inc=1, device_id=partner, device_id_type=MESH_ID)
    count = 1
    for axis, mine in (("y", my_y), ("z", my_z), ("x", my_x)):
        for j, member in enumerate(groups[axis]):
            @pl.when(j != mine)
            def _():
                pl.semaphore_signal(barrier, inc=1, device_id=member, device_id_type=MESH_ID)
        count += len(groups[axis]) - 1
    pl.semaphore_wait(barrier, count)

    sends = iter(range(send_sem.shape[0]))

    def one(src, dst, sem, target):
        copy = pltpu.make_async_remote_copy(
            src_ref=src, dst_ref=dst, send_sem=send_sem.at[next(sends)], recv_sem=sem,
            device_id=target, device_id_type=MESH_ID,
        )
        copy.start()
        copy.wait()

    def spread(axis, mine, src_of, dst, sems):
        copies = []
        for j, member in enumerate(groups[axis]):
            copy = pltpu.make_async_remote_copy(
                src_ref=src_of(j), dst_ref=dst.at[mine], send_sem=send_sem.at[next(sends)],
                recv_sem=sems.at[mine], device_id=member, device_id_type=MESH_ID,
            )
            copies.append((j, copy))

            @pl.when(j != mine)
            def _():
                copy.start()
        for j, copy in copies:
            @pl.when(j != mine)
            def _():
                copy.wait_send()
                pltpu.make_async_remote_copy(
                    src_ref=src_of(j), dst_ref=dst.at[j], send_sem=send_sem.at[0],
                    recv_sem=sems.at[j], device_id=groups[axis][j], device_id_type=MESH_ID,
                ).wait_recv()

    one(flat_ref.at[1 - core], got_pipe, recv_pipe.at[0], partner)
    own[...] = flat_ref[core] + got_pipe[...]

    ny = len(groups["y"])
    got_y[my_y] = own[my_y]
    spread("y", my_y, lambda j: own.at[j], got_y, recv_y)
    part[...] = tree_sum([got_y[k] for k in range(ny)])

    got_z[my_z] = part[...]
    spread("z", my_z, lambda j: part, got_z, recv_z)
    part[...] = tree_sum([got_z[k] for k in range(len(groups["z"]))])

    got_x[my_x] = part[...]
    spread("x", my_x, lambda j: part, got_x, recv_x)
    part[...] = tree_sum([got_x[k] for k in range(len(groups["x"]))])

    got_back[my_y] = part[...]
    spread("y", my_y, lambda j: part, got_back, recv_back)

    one(got_back, got_end, recv_end.at[0], partner)
    out_ref[core] = got_back[...]
    out_ref[1 - core] = got_end[...]


def all_reduce(flat):
    halves, ny, rows, lanes = flat.shape
    nz, nx = lax.axis_size("z"), lax.axis_size("x")
    chunk = (rows, lanes)
    sends = 1 + ny + nz + nx + ny + 1
    vmem = pl.BlockSpec(memory_space=pltpu.VMEM)
    return pl.pallas_call(
        reduce_kernel,
        out_shape=jax.ShapeDtypeStruct(flat.shape, flat.dtype),
        in_specs=[vmem],
        out_specs=vmem,
        scratch_shapes=[
            pltpu.VMEM((ny,) + chunk, flat.dtype),
            pltpu.VMEM(chunk, flat.dtype),
            pltpu.VMEM((ny,) + chunk, flat.dtype),
            pltpu.VMEM((ny,) + chunk, flat.dtype),
            pltpu.VMEM((ny,) + chunk, flat.dtype),
            pltpu.VMEM((nz,) + chunk, flat.dtype),
            pltpu.VMEM((nx,) + chunk, flat.dtype),
            pltpu.VMEM((ny,) + chunk, flat.dtype),
            pltpu.VMEM((ny,) + chunk, flat.dtype),
            pltpu.SemaphoreType.DMA((sends,)),
            pltpu.SemaphoreType.DMA((1,)),
            pltpu.SemaphoreType.DMA((ny,)),
            pltpu.SemaphoreType.DMA((nz,)),
            pltpu.SemaphoreType.DMA((nx,)),
            pltpu.SemaphoreType.DMA((ny,)),
            pltpu.SemaphoreType.DMA((1,)),
        ],
        compiler_params=pltpu.CompilerParams(collective_id=1, has_side_effects=True),
    )(flat)


def shards(endpoints, row_counts, layer_order, depth_weight, point_weight, point_bias):
    held = endpoints[0]
    height = held.shape[1]
    breadth = held.shape[2]
    channels = held.shape[3]
    layers = layer_order.shape[0]
    core = lax.axis_index("pipe")

    edges = jnp.stack([held[:, :, :X_HALO], held[:, :, breadth - X_HALO :]])
    body, lo, hi = exchange(held, edges)
    mine = select_row(held, core)
    x_in = jnp.where(core == 0, mine, body)
    g_in = jnp.where(core == 0, body, mine)
    x_wide = jnp.concatenate([lo[0], x_in, hi[0]], axis=1)
    g_wide = jnp.concatenate([lo[1][:, X_HALO - G_HALO :], g_in, hi[1][:, :G_HALO]], axis=1)

    counts = jnp.where(core == 0, row_counts[0:1], row_counts[1:2])
    live = (jnp.arange(height)[:, None, None] < counts[None, None, :]).astype(jnp.float32)

    placed = layer_order[:, None] == jnp.arange(layers, dtype=layer_order.dtype)[None, :]

    def pick(table):
        mask = placed.reshape(placed.shape + (1,) * (table.ndim - 1))
        return jnp.sum(jnp.where(mask, table[None], jnp.zeros((), table.dtype)), axis=1, dtype=table.dtype)

    by_position = [pick(table) for table in (depth_weight, point_weight, point_bias)]
    weights = [tuple(table[p] for table in by_position) for p in range(layers)]

    activation = (x_wide.astype(jnp.float32) * live).astype(jnp.bfloat16)
    acts, mixes, preacts = [], [], []
    for p in range(layers):
        depth, point, offset_vec = weights[p]
        acts.append(activation)
        mixed = conv_forward(pad_rows(activation), depth).astype(jnp.bfloat16)
        rows, span = mixed.shape[0], mixed.shape[1]
        preact = jnp.dot(
            mixed.reshape(rows * span, channels), point, preferred_element_type=jnp.float32
        ).reshape(rows, span, channels) + offset_vec
        mixes.append(mixed)
        preacts.append(preact)
        activation = (
            (activation[:, 1:-1].astype(jnp.float32) + gelu_pair(preact)[0]) * live
        ).astype(jnp.bfloat16)
    final_halo = X_HALO - layers
    outcome = activation[:, final_halo : final_halo + breadth]

    cotangent = g_wide
    depth_terms, point_terms, bias_terms = [None] * layers, [None] * layers, [None] * layers
    for p in range(layers - 1, -1, -1):
        depth, point, _ = weights[p]
        halo_c = (cotangent.shape[1] - breadth) // 2
        halo_p = (preacts[p].shape[1] - breadth) // 2
        shift = halo_p - halo_c
        span = cotangent.shape[1]
        preact = preacts[p][:, shift : shift + span]
        masked = cotangent.astype(jnp.float32) * live
        gated = (masked * gelu_pair(preact)[1]).astype(jnp.bfloat16)
        back_mix = lax.dot_general(
            gated.reshape(height * span, channels),
            point,
            (((1,), (1,)), ((), ())),
            preferred_element_type=jnp.float32,
        ).reshape(height, span, channels).astype(jnp.bfloat16)

        gate_in = gated[:, halo_c : halo_c + breadth].reshape(height * breadth, channels)
        mix_in = mixes[p][:, halo_p : halo_p + breadth].reshape(height * breadth, channels)
        point_terms[p] = lax.dot_general(
            mix_in, gate_in, (((0,), (0,)), ((), ())), preferred_element_type=jnp.float32
        )
        bias_terms[p] = jnp.sum(gate_in.astype(jnp.float32), axis=0)
        back_in = back_mix[:, halo_c : halo_c + breadth].astype(jnp.float32)
        padded = pad_rows(acts[p])
        halo_a = (acts[p].shape[1] - breadth) // 2
        rows_k = []
        for i in range(3):
            row_k = []
            for j in range(3):
                start = halo_a - 1 + j
                row_k.append(
                    jnp.sum(
                        back_in * padded[i : i + height, start : start + breadth].astype(jnp.float32),
                        axis=(0, 1),
                    )
                )
            rows_k.append(jnp.stack(row_k))
        depth_terms[p] = jnp.stack(rows_k)

        earlier = conv_backward(pad_rows(back_mix), depth)
        cotangent = ((masked[:, 1:-1] + earlier) * live).astype(jnp.bfloat16)
    input_grad = cotangent

    got_outcome = lax.ppermute(outcome, "pipe", [(0, 1)])
    got_grad = lax.ppermute(input_grad, "pipe", [(1, 0)])
    first = jnp.where(core == 0, input_grad, got_outcome)
    second = jnp.where(core == 0, got_grad, outcome)
    result = jnp.stack([first, second])[None]

    pieces = (jnp.stack(depth_terms), jnp.stack(point_terms), jnp.stack(bias_terms))
    flat = jnp.concatenate([piece.reshape(layers, -1) for piece in pieces], axis=1)
    ny = lax.axis_size("y")
    size = flat.size
    rows = -(-size // (2 * ny * 128))
    rows = -(-rows // 8) * 8
    packed = jnp.pad(flat.reshape(-1), (0, 2 * ny * rows * 128 - size)).reshape(2, ny, rows, 128)
    result, packed = lax.optimization_barrier((result, packed))
    flat = all_reduce(packed).reshape(-1)[:size].reshape(flat.shape)
    factor = 1.0 / math.sqrt(held.shape[0] * height * breadth * blk_count())
    chosen = layer_order[None, :] == jnp.arange(layers, dtype=layer_order.dtype)[:, None]
    flat = jnp.sum(jnp.where(chosen[:, :, None], flat[None, :, :], 0.0), axis=1) * factor
    ordered, at = [], 0
    for piece in pieces:
        width = piece[0].size
        ordered.append(flat[:, at : at + width].reshape(piece.shape))
        at += width
    return (result, ordered[0], ordered[1], ordered[2])


def solution(mesh):
    devices = mesh.devices
    blk = devices.shape[0]
    y_size = 4 if blk % 4 == 0 else 1
    rest = blk // y_size
    z_size = 8 if rest % 8 == 0 else rest
    x_size = rest // z_size
    torus = Mesh(devices.reshape(x_size, z_size, y_size, devices.shape[1]), BLK_AXES + ("pipe",))
    spec = P("pipe", None, None, BLK_AXES, None)
    in_specs = (spec, P(), P(), P(), P(), P())
    out_specs = (spec, P(), P(), P())
    return jax.shard_map(shards, mesh=torus, in_specs=in_specs, out_specs=out_specs, check_vma=False)
```

```python
import math

import jax
import jax.numpy as jnp
from jax import lax
from jax.experimental import pallas as pl
from jax.experimental.pallas import tpu as pltpu
from jax.sharding import Mesh, PartitionSpec as P

MESH_ID = pl.DeviceIdType.MESH

root_half = 0.7071067811865476
density_norm = 0.3989422804014327

X_HALO = 8
G_HALO = 4


BLK_AXES = ("x", "z", "y")


def blk_count():
    count = 1
    for axis in BLK_AXES:
        count *= lax.axis_size(axis)
    return count


def gelu_pair(preact):
    normal_cdf = 0.5 * (1.0 + lax.erf(preact * root_half))
    normal_pdf = density_norm * jnp.exp(-0.5 * preact * preact)
    return (preact * normal_cdf, normal_cdf + preact * normal_pdf)


def select_row(table, chosen):
    return lax.dynamic_index_in_dim(table, chosen, 0, keepdims=False)


def pad_rows(x):
    return jnp.pad(x, ((1, 1), (0, 0), (0, 0)))


def conv_forward(padded, depth):
    height = padded.shape[0] - 2
    breadth = padded.shape[1] - 2
    acc = jnp.zeros((height, breadth, padded.shape[2]), jnp.float32)
    for i in range(3):
        for j in range(3):
            acc = acc + depth[i, j] * padded[i : i + height, j : j + breadth].astype(jnp.float32)
    return acc


def conv_backward(spread, depth):
    height = spread.shape[0] - 2
    breadth = spread.shape[1] - 2
    acc = jnp.zeros((height, breadth, spread.shape[2]), jnp.float32)
    for i in range(3):
        for j in range(3):
            acc = acc + depth[i, j] * spread[
                2 - i : 2 - i + height, 2 - j : 2 - j + breadth
            ].astype(jnp.float32)
    return acc


def torus_coords(b):
    y_size, z_size = lax.axis_size("y"), lax.axis_size("z")
    return (b // (y_size * z_size), lax.rem(b // y_size, z_size), lax.rem(b, y_size))


def exchange_kernel(held_ref, edges_ref, body_out, lo_out, hi_out, body, lo, hi, send_sem, recv_sem):
    core = lax.axis_index("pipe")
    count = blk_count()
    here = (lax.axis_index("x") * lax.axis_size("z") + lax.axis_index("z")) * lax.axis_size("y") + lax.axis_index("y")
    right = torus_coords(lax.rem(here + 1, count))
    left = torus_coords(lax.rem(here + count - 1, count))
    mine = torus_coords(here)
    partner = mine + (1 - core,)
    targets = [partner] + [right + (m,) for m in range(2)] + [left + (m,) for m in range(2)]

    barrier = pltpu.get_barrier_semaphore()
    for target in targets:
        pl.semaphore_signal(barrier, inc=1, device_id=target, device_id_type=MESH_ID)
    pl.semaphore_wait(barrier, len(targets))

    copies = [
        pltpu.make_async_remote_copy(
            src_ref=held_ref.at[1 - core], dst_ref=body,
            send_sem=send_sem.at[0], recv_sem=recv_sem.at[0],
            device_id=partner, device_id_type=MESH_ID,
        )
    ]
    for m in range(2):
        copies.append(pltpu.make_async_remote_copy(
            src_ref=edges_ref.at[1, m], dst_ref=lo.at[core],
            send_sem=send_sem.at[1 + m], recv_sem=recv_sem.at[1 + core],
            device_id=right + (m,), device_id_type=MESH_ID,
        ))
        copies.append(pltpu.make_async_remote_copy(
            src_ref=edges_ref.at[0, m], dst_ref=hi.at[core],
            send_sem=send_sem.at[3 + m], recv_sem=recv_sem.at[3 + core],
            device_id=left + (m,), device_id_type=MESH_ID,
        ))
    for copy in copies:
        copy.start()
    copies[0].wait_recv()
    for k in range(2):
        pltpu.make_async_remote_copy(
            src_ref=edges_ref.at[1, k], dst_ref=lo.at[k],
            send_sem=send_sem.at[1 + k], recv_sem=recv_sem.at[1 + k],
            device_id=right + (k,), device_id_type=MESH_ID,
        ).wait_recv()
        pltpu.make_async_remote_copy(
            src_ref=edges_ref.at[0, k], dst_ref=hi.at[k],
            send_sem=send_sem.at[3 + k], recv_sem=recv_sem.at[3 + k],
            device_id=left + (k,), device_id_type=MESH_ID,
        ).wait_recv()
    for copy in copies:
        copy.wait_send()
    body_out[...] = body[...]
    lo_out[...] = lo[...]
    hi_out[...] = hi[...]


def exchange(held, edges):
    grid_shape = held.shape[1:]
    strip_shape = edges.shape[2:]
    vmem = pl.BlockSpec(memory_space=pltpu.VMEM)
    return pl.pallas_call(
        exchange_kernel,
        out_shape=(
            jax.ShapeDtypeStruct(grid_shape, held.dtype),
            jax.ShapeDtypeStruct((2,) + strip_shape, held.dtype),
            jax.ShapeDtypeStruct((2,) + strip_shape, held.dtype),
        ),
        in_specs=[vmem, vmem],
        out_specs=(vmem, vmem, vmem),
        scratch_shapes=[
            pltpu.VMEM(grid_shape, held.dtype),
            pltpu.VMEM((2,) + strip_shape, held.dtype),
            pltpu.VMEM((2,) + strip_shape, held.dtype),
            pltpu.SemaphoreType.DMA((5,)),
            pltpu.SemaphoreType.DMA((5,)),
        ],
        compiler_params=pltpu.CompilerParams(collective_id=0, has_side_effects=True),
    )(held, edges)


def group_members(axis):
    here = [lax.axis_index(name) for name in BLK_AXES] + [lax.axis_index("pipe")]
    slot = BLK_AXES.index(axis)
    return [tuple(here[:slot]) + (j,) + tuple(here[slot + 1 :]) for j in range(lax.axis_size(axis))]


def tree_sum(values):
    while len(values) > 1:
        values = [values[k] + values[k + 1] for k in range(0, len(values), 2)]
    return values[0]


def reduce_kernel(flat_ref, out_ref, part, got_a, got_z, got_x, got_b,
                  send_sem, recv_a, recv_z, recv_x, recv_b):
    core = lax.axis_index("pipe")
    my_y, my_z, my_x = (lax.axis_index(name) for name in ("y", "z", "x"))
    ny = lax.axis_size("y")
    row = [lax.axis_index(name) for name in BLK_AXES]
    groups = {
        "py": [(row[0], row[1], j, h) for h in range(2) for j in range(ny)],
        "z": group_members("z"),
        "x": group_members("x"),
    }
    places = {"py": core * ny + my_y, "z": my_z, "x": my_x}

    barrier = pltpu.get_barrier_semaphore()
    count = 0
    for axis in ("py", "z", "x"):
        for j, member in enumerate(groups[axis]):
            @pl.when(j != places[axis])
            def _():
                pl.semaphore_signal(barrier, inc=1, device_id=member, device_id_type=MESH_ID)
        count += len(groups[axis]) - 1
    pl.semaphore_wait(barrier, count)

    sends = iter(range(send_sem.shape[0]))

    def spread(axis, src_of, dst, sems):
        mine = places[axis]
        copies = []
        for j, member in enumerate(groups[axis]):
            copy = pltpu.make_async_remote_copy(
                src_ref=src_of(j), dst_ref=dst.at[mine], send_sem=send_sem.at[next(sends)],
                recv_sem=sems.at[mine], device_id=member, device_id_type=MESH_ID,
            )
            copies.append((j, copy))

            @pl.when(j != mine)
            def _():
                copy.start()
        for j, copy in copies:
            @pl.when(j != mine)
            def _():
                copy.wait_send()
                pltpu.make_async_remote_copy(
                    src_ref=src_of(j), dst_ref=dst.at[j], send_sem=send_sem.at[0],
                    recv_sem=sems.at[j], device_id=groups[axis][j], device_id_type=MESH_ID,
                ).wait_recv()

    got_a[places["py"]] = flat_ref[places["py"]]
    spread("py", lambda j: flat_ref.at[j], got_a, recv_a)
    part[...] = tree_sum([got_a[k] for k in range(len(groups["py"]))])

    got_z[my_z] = part[...]
    spread("z", lambda j: part, got_z, recv_z)
    part[...] = tree_sum([got_z[k] for k in range(len(groups["z"]))])

    got_x[my_x] = part[...]
    spread("x", lambda j: part, got_x, recv_x)
    part[...] = tree_sum([got_x[k] for k in range(len(groups["x"]))])

    got_b[places["py"]] = part[...]
    spread("py", lambda j: part, got_b, recv_b)
    out_ref[...] = got_b[...]


def all_reduce(flat):
    chunks, rows, lanes = flat.shape
    nz, nx = lax.axis_size("z"), lax.axis_size("x")
    chunk = (rows, lanes)
    sends = chunks + nz + nx + chunks
    vmem = pl.BlockSpec(memory_space=pltpu.VMEM)
    return pl.pallas_call(
        reduce_kernel,
        out_shape=jax.ShapeDtypeStruct(flat.shape, flat.dtype),
        in_specs=[vmem],
        out_specs=vmem,
        scratch_shapes=[
            pltpu.VMEM(chunk, flat.dtype),
            pltpu.VMEM((chunks,) + chunk, flat.dtype),
            pltpu.VMEM((nz,) + chunk, flat.dtype),
            pltpu.VMEM((nx,) + chunk, flat.dtype),
            pltpu.VMEM((chunks,) + chunk, flat.dtype),
            pltpu.SemaphoreType.DMA((sends,)),
            pltpu.SemaphoreType.DMA((chunks,)),
            pltpu.SemaphoreType.DMA((nz,)),
            pltpu.SemaphoreType.DMA((nx,)),
            pltpu.SemaphoreType.DMA((chunks,)),
        ],
        compiler_params=pltpu.CompilerParams(collective_id=1, has_side_effects=True),
    )(flat)


def shards(endpoints, row_counts, layer_order, depth_weight, point_weight, point_bias):
    held = endpoints[0]
    height = held.shape[1]
    breadth = held.shape[2]
    channels = held.shape[3]
    layers = layer_order.shape[0]
    core = lax.axis_index("pipe")

    edges = jnp.stack([held[:, :, :X_HALO], held[:, :, breadth - X_HALO :]])
    body, lo, hi = exchange(held, edges)
    mine = select_row(held, core)
    x_in = jnp.where(core == 0, mine, body)
    g_in = jnp.where(core == 0, body, mine)
    x_wide = jnp.concatenate([lo[0], x_in, hi[0]], axis=1)
    g_wide = jnp.concatenate([lo[1][:, X_HALO - G_HALO :], g_in, hi[1][:, :G_HALO]], axis=1)

    counts = jnp.where(core == 0, row_counts[0:1], row_counts[1:2])
    live = (jnp.arange(height)[:, None, None] < counts[None, None, :]).astype(jnp.float32)

    placed = layer_order[:, None] == jnp.arange(layers, dtype=layer_order.dtype)[None, :]

    def pick(table):
        mask = placed.reshape(placed.shape + (1,) * (table.ndim - 1))
        return jnp.sum(jnp.where(mask, table[None], jnp.zeros((), table.dtype)), axis=1, dtype=table.dtype)

    by_position = [pick(table) for table in (depth_weight, point_weight, point_bias)]
    weights = [tuple(table[p] for table in by_position) for p in range(layers)]

    activation = (x_wide.astype(jnp.float32) * live).astype(jnp.bfloat16)
    acts, mixes, preacts = [], [], []
    for p in range(layers):
        depth, point, offset_vec = weights[p]
        acts.append(activation)
        mixed = conv_forward(pad_rows(activation), depth).astype(jnp.bfloat16)
        rows, span = mixed.shape[0], mixed.shape[1]
        preact = jnp.dot(
            mixed.reshape(rows * span, channels), point, preferred_element_type=jnp.float32
        ).reshape(rows, span, channels) + offset_vec
        mixes.append(mixed)
        preacts.append(preact)
        activation = (
            (activation[:, 1:-1].astype(jnp.float32) + gelu_pair(preact)[0]) * live
        ).astype(jnp.bfloat16)
    final_halo = X_HALO - layers
    outcome = activation[:, final_halo : final_halo + breadth]

    cotangent = g_wide
    depth_terms, point_terms, bias_terms = [None] * layers, [None] * layers, [None] * layers
    for p in range(layers - 1, -1, -1):
        depth, point, _ = weights[p]
        halo_c = (cotangent.shape[1] - breadth) // 2
        halo_p = (preacts[p].shape[1] - breadth) // 2
        shift = halo_p - halo_c
        span = cotangent.shape[1]
        preact = preacts[p][:, shift : shift + span]
        masked = cotangent.astype(jnp.float32) * live
        gated = (masked * gelu_pair(preact)[1]).astype(jnp.bfloat16)
        back_mix = lax.dot_general(
            gated.reshape(height * span, channels),
            point,
            (((1,), (1,)), ((), ())),
            preferred_element_type=jnp.float32,
        ).reshape(height, span, channels).astype(jnp.bfloat16)

        gate_in = gated[:, halo_c : halo_c + breadth].reshape(height * breadth, channels)
        mix_in = mixes[p][:, halo_p : halo_p + breadth].reshape(height * breadth, channels)
        point_terms[p] = lax.dot_general(
            mix_in, gate_in, (((0,), (0,)), ((), ())), preferred_element_type=jnp.float32
        )
        bias_terms[p] = jnp.sum(gate_in.astype(jnp.float32), axis=0)
        back_in = back_mix[:, halo_c : halo_c + breadth].astype(jnp.float32)
        padded = pad_rows(acts[p])
        halo_a = (acts[p].shape[1] - breadth) // 2
        rows_k = []
        for i in range(3):
            row_k = []
            for j in range(3):
                start = halo_a - 1 + j
                row_k.append(
                    jnp.sum(
                        back_in * padded[i : i + height, start : start + breadth].astype(jnp.float32),
                        axis=(0, 1),
                    )
                )
            rows_k.append(jnp.stack(row_k))
        depth_terms[p] = jnp.stack(rows_k)

        earlier = conv_backward(pad_rows(back_mix), depth)
        cotangent = ((masked[:, 1:-1] + earlier) * live).astype(jnp.bfloat16)
    input_grad = cotangent

    got_outcome = lax.ppermute(outcome, "pipe", [(0, 1)])
    got_grad = lax.ppermute(input_grad, "pipe", [(1, 0)])
    first = jnp.where(core == 0, input_grad, got_outcome)
    second = jnp.where(core == 0, got_grad, outcome)
    result = jnp.stack([first, second])[None]

    pieces = (jnp.stack(depth_terms), jnp.stack(point_terms), jnp.stack(bias_terms))
    flat = jnp.concatenate([piece.reshape(layers, -1) for piece in pieces], axis=1)
    ny = lax.axis_size("y")
    size = flat.size
    rows = -(-size // (2 * ny * 128))
    rows = -(-rows // 8) * 8
    packed = jnp.pad(flat.reshape(-1), (0, 2 * ny * rows * 128 - size)).reshape(2 * ny, rows, 128)
    flat = all_reduce(packed).reshape(-1)[:size].reshape(flat.shape)
    factor = 1.0 / math.sqrt(held.shape[0] * height * breadth * blk_count())
    chosen = layer_order[None, :] == jnp.arange(layers, dtype=layer_order.dtype)[:, None]
    flat = jnp.sum(jnp.where(chosen[:, :, None], flat[None, :, :], 0.0), axis=1) * factor
    ordered, at = [], 0
    for piece in pieces:
        width = piece[0].size
        ordered.append(flat[:, at : at + width].reshape(piece.shape))
        at += width
    return (result, ordered[0], ordered[1], ordered[2])


def solution(mesh):
    devices = mesh.devices
    blk = devices.shape[0]
    y_size = 4 if blk % 4 == 0 else 1
    rest = blk // y_size
    z_size = 8 if rest % 8 == 0 else rest
    x_size = rest // z_size
    torus = Mesh(devices.reshape(x_size, z_size, y_size, devices.shape[1]), BLK_AXES + ("pipe",))
    spec = P("pipe", None, None, BLK_AXES, None)
    in_specs = (spec, P(), P(), P(), P(), P())
    out_specs = (spec, P(), P(), P())
    return jax.shard_map(shards, mesh=torus, in_specs=in_specs, out_specs=out_specs, check_vma=False)
```

```python
import math

import jax
import jax.numpy as jnp
from jax import lax
from jax.experimental import pallas as pl
from jax.experimental.pallas import tpu as pltpu
from jax.sharding import Mesh, PartitionSpec as P

MESH_ID = pl.DeviceIdType.MESH

root_half = 0.7071067811865476
density_norm = 0.3989422804014327

X_HALO = 8
G_HALO = 4


BLK_AXES = ("x", "z", "y")


def blk_count():
    count = 1
    for axis in BLK_AXES:
        count *= lax.axis_size(axis)
    return count


def gelu_pair(preact):
    normal_cdf = 0.5 * (1.0 + lax.erf(preact * root_half))
    normal_pdf = density_norm * jnp.exp(-0.5 * preact * preact)
    return (preact * normal_cdf, normal_cdf + preact * normal_pdf)


def select_row(table, chosen):
    return lax.dynamic_index_in_dim(table, chosen, 0, keepdims=False)


def pad_rows(x):
    return jnp.pad(x, ((1, 1), (0, 0), (0, 0)))


def conv_forward(padded, depth):
    height = padded.shape[0] - 2
    breadth = padded.shape[1] - 2
    acc = jnp.zeros((height, breadth, padded.shape[2]), jnp.float32)
    for i in range(3):
        for j in range(3):
            acc = acc + depth[i, j] * padded[i : i + height, j : j + breadth].astype(jnp.float32)
    return acc


def conv_backward(spread, depth):
    height = spread.shape[0] - 2
    breadth = spread.shape[1] - 2
    acc = jnp.zeros((height, breadth, spread.shape[2]), jnp.float32)
    for i in range(3):
        for j in range(3):
            acc = acc + depth[i, j] * spread[
                2 - i : 2 - i + height, 2 - j : 2 - j + breadth
            ].astype(jnp.float32)
    return acc


def torus_coords(b):
    y_size, z_size = lax.axis_size("y"), lax.axis_size("z")
    return (b // (y_size * z_size), lax.rem(b // y_size, z_size), lax.rem(b, y_size))


def exchange_kernel(held_ref, edges_ref, body_out, lo_out, hi_out, body, lo, hi, send_sem, recv_sem):
    core = lax.axis_index("pipe")
    count = blk_count()
    here = (lax.axis_index("x") * lax.axis_size("z") + lax.axis_index("z")) * lax.axis_size("y") + lax.axis_index("y")
    right = torus_coords(lax.rem(here + 1, count))
    left = torus_coords(lax.rem(here + count - 1, count))
    mine = torus_coords(here)
    partner = mine + (1 - core,)
    targets = [partner] + [right + (m,) for m in range(2)] + [left + (m,) for m in range(2)]

    barrier = pltpu.get_barrier_semaphore()
    for target in targets:
        pl.semaphore_signal(barrier, inc=1, device_id=target, device_id_type=MESH_ID)
    pl.semaphore_wait(barrier, len(targets))

    copies = [
        pltpu.make_async_remote_copy(
            src_ref=held_ref.at[1 - core], dst_ref=body,
            send_sem=send_sem.at[0], recv_sem=recv_sem.at[0],
            device_id=partner, device_id_type=MESH_ID,
        )
    ]
    for m in range(2):
        copies.append(pltpu.make_async_remote_copy(
            src_ref=edges_ref.at[1, m], dst_ref=lo.at[core],
            send_sem=send_sem.at[1 + m], recv_sem=recv_sem.at[1 + core],
            device_id=right + (m,), device_id_type=MESH_ID,
        ))
        copies.append(pltpu.make_async_remote_copy(
            src_ref=edges_ref.at[0, m], dst_ref=hi.at[core],
            send_sem=send_sem.at[3 + m], recv_sem=recv_sem.at[3 + core],
            device_id=left + (m,), device_id_type=MESH_ID,
        ))
    for copy in copies:
        copy.start()
    copies[0].wait_recv()
    for k in range(2):
        pltpu.make_async_remote_copy(
            src_ref=edges_ref.at[1, k], dst_ref=lo.at[k],
            send_sem=send_sem.at[1 + k], recv_sem=recv_sem.at[1 + k],
            device_id=right + (k,), device_id_type=MESH_ID,
        ).wait_recv()
        pltpu.make_async_remote_copy(
            src_ref=edges_ref.at[0, k], dst_ref=hi.at[k],
            send_sem=send_sem.at[3 + k], recv_sem=recv_sem.at[3 + k],
            device_id=left + (k,), device_id_type=MESH_ID,
        ).wait_recv()
    for copy in copies:
        copy.wait_send()
    body_out[...] = body[...]
    lo_out[...] = lo[...]
    hi_out[...] = hi[...]


def exchange(held, edges):
    grid_shape = held.shape[1:]
    strip_shape = edges.shape[2:]
    vmem = pl.BlockSpec(memory_space=pltpu.VMEM)
    return pl.pallas_call(
        exchange_kernel,
        out_shape=(
            jax.ShapeDtypeStruct(grid_shape, held.dtype),
            jax.ShapeDtypeStruct((2,) + strip_shape, held.dtype),
            jax.ShapeDtypeStruct((2,) + strip_shape, held.dtype),
        ),
        in_specs=[vmem, vmem],
        out_specs=(vmem, vmem, vmem),
        scratch_shapes=[
            pltpu.VMEM(grid_shape, held.dtype),
            pltpu.VMEM((2,) + strip_shape, held.dtype),
            pltpu.VMEM((2,) + strip_shape, held.dtype),
            pltpu.SemaphoreType.DMA((5,)),
            pltpu.SemaphoreType.DMA((5,)),
        ],
        compiler_params=pltpu.CompilerParams(collective_id=0, has_side_effects=True),
    )(held, edges)


def group_members(axis):
    here = [lax.axis_index(name) for name in BLK_AXES] + [lax.axis_index("pipe")]
    slot = BLK_AXES.index(axis)
    return [tuple(here[:slot]) + (j,) + tuple(here[slot + 1 :]) for j in range(lax.axis_size(axis))]


def tree_sum(values):
    while len(values) > 1:
        values = [values[k] + values[k + 1] for k in range(0, len(values), 2)]
    return values[0]


def reduce_kernel(flat_ref, out_ref, part, got_a, got_z, got_b,
                  send_sem, recv_a, recv_z, recv_b):
    core = lax.axis_index("pipe")
    my_y, my_z, my_x = (lax.axis_index(name) for name in ("y", "z", "x"))
    ny, nx = lax.axis_size("y"), lax.axis_size("x")
    row = [lax.axis_index(name) for name in BLK_AXES]
    groups = {
        "py": [(i, row[1], j, h) for h in range(2) for i in range(nx) for j in range(ny)],
        "z": group_members("z"),
    }
    places = {"py": (core * nx + my_x) * ny + my_y, "z": my_z}

    barrier = pltpu.get_barrier_semaphore()
    count = 0
    for axis in ("py", "z"):
        for j, member in enumerate(groups[axis]):
            @pl.when(j != places[axis])
            def _():
                pl.semaphore_signal(barrier, inc=1, device_id=member, device_id_type=MESH_ID)
        count += len(groups[axis]) - 1
    pl.semaphore_wait(barrier, count)

    sends = iter(range(send_sem.shape[0]))

    def spread(axis, src_of, dst, sems):
        mine = places[axis]
        copies = []
        for j, member in enumerate(groups[axis]):
            copy = pltpu.make_async_remote_copy(
                src_ref=src_of(j), dst_ref=dst.at[mine], send_sem=send_sem.at[next(sends)],
                recv_sem=sems.at[mine], device_id=member, device_id_type=MESH_ID,
            )
            copies.append((j, copy))

            @pl.when(j != mine)
            def _():
                copy.start()
        for j, copy in copies:
            @pl.when(j != mine)
            def _():
                copy.wait_send()
                pltpu.make_async_remote_copy(
                    src_ref=src_of(j), dst_ref=dst.at[j], send_sem=send_sem.at[0],
                    recv_sem=sems.at[j], device_id=groups[axis][j], device_id_type=MESH_ID,
                ).wait_recv()

    got_a[places["py"]] = flat_ref[places["py"]]
    spread("py", lambda j: flat_ref.at[j], got_a, recv_a)
    part[...] = tree_sum([got_a[k] for k in range(len(groups["py"]))])

    got_z[my_z] = part[...]
    spread("z", lambda j: part, got_z, recv_z)
    part[...] = tree_sum([got_z[k] for k in range(len(groups["z"]))])

    got_b[places["py"]] = part[...]
    spread("py", lambda j: part, got_b, recv_b)
    out_ref[...] = got_b[...]


def all_reduce(flat):
    chunks, rows, lanes = flat.shape
    nz = lax.axis_size("z")
    chunk = (rows, lanes)
    sends = chunks + nz + chunks
    vmem = pl.BlockSpec(memory_space=pltpu.VMEM)
    return pl.pallas_call(
        reduce_kernel,
        out_shape=jax.ShapeDtypeStruct(flat.shape, flat.dtype),
        in_specs=[vmem],
        out_specs=vmem,
        scratch_shapes=[
            pltpu.VMEM(chunk, flat.dtype),
            pltpu.VMEM((chunks,) + chunk, flat.dtype),
            pltpu.VMEM((nz,) + chunk, flat.dtype),
            pltpu.VMEM((chunks,) + chunk, flat.dtype),
            pltpu.SemaphoreType.DMA((sends,)),
            pltpu.SemaphoreType.DMA((chunks,)),
            pltpu.SemaphoreType.DMA((nz,)),
            pltpu.SemaphoreType.DMA((chunks,)),
        ],
        compiler_params=pltpu.CompilerParams(collective_id=1, has_side_effects=True),
    )(flat)


def shards(endpoints, row_counts, layer_order, depth_weight, point_weight, point_bias):
    held = endpoints[0]
    height = held.shape[1]
    breadth = held.shape[2]
    channels = held.shape[3]
    layers = layer_order.shape[0]
    core = lax.axis_index("pipe")

    edges = jnp.stack([held[:, :, :X_HALO], held[:, :, breadth - X_HALO :]])
    body, lo, hi = exchange(held, edges)
    mine = select_row(held, core)
    x_in = jnp.where(core == 0, mine, body)
    g_in = jnp.where(core == 0, body, mine)
    x_wide = jnp.concatenate([lo[0], x_in, hi[0]], axis=1)
    g_wide = jnp.concatenate([lo[1][:, X_HALO - G_HALO :], g_in, hi[1][:, :G_HALO]], axis=1)

    counts = jnp.where(core == 0, row_counts[0:1], row_counts[1:2])
    live = (jnp.arange(height)[:, None, None] < counts[None, None, :]).astype(jnp.float32)

    placed = layer_order[:, None] == jnp.arange(layers, dtype=layer_order.dtype)[None, :]

    def pick(table):
        mask = placed.reshape(placed.shape + (1,) * (table.ndim - 1))
        return jnp.sum(jnp.where(mask, table[None], jnp.zeros((), table.dtype)), axis=1, dtype=table.dtype)

    by_position = [pick(table) for table in (depth_weight, point_weight, point_bias)]
    weights = [tuple(table[p] for table in by_position) for p in range(layers)]

    activation = (x_wide.astype(jnp.float32) * live).astype(jnp.bfloat16)
    acts, mixes, preacts = [], [], []
    for p in range(layers):
        depth, point, offset_vec = weights[p]
        acts.append(activation)
        mixed = conv_forward(pad_rows(activation), depth).astype(jnp.bfloat16)
        rows, span = mixed.shape[0], mixed.shape[1]
        preact = jnp.dot(
            mixed.reshape(rows * span, channels), point, preferred_element_type=jnp.float32
        ).reshape(rows, span, channels) + offset_vec
        mixes.append(mixed)
        preacts.append(preact)
        activation = (
            (activation[:, 1:-1].astype(jnp.float32) + gelu_pair(preact)[0]) * live
        ).astype(jnp.bfloat16)
    final_halo = X_HALO - layers
    outcome = activation[:, final_halo : final_halo + breadth]

    cotangent = g_wide
    depth_terms, point_terms, bias_terms = [None] * layers, [None] * layers, [None] * layers
    for p in range(layers - 1, -1, -1):
        depth, point, _ = weights[p]
        halo_c = (cotangent.shape[1] - breadth) // 2
        halo_p = (preacts[p].shape[1] - breadth) // 2
        shift = halo_p - halo_c
        span = cotangent.shape[1]
        preact = preacts[p][:, shift : shift + span]
        masked = cotangent.astype(jnp.float32) * live
        gated = (masked * gelu_pair(preact)[1]).astype(jnp.bfloat16)
        back_mix = lax.dot_general(
            gated.reshape(height * span, channels),
            point,
            (((1,), (1,)), ((), ())),
            preferred_element_type=jnp.float32,
        ).reshape(height, span, channels).astype(jnp.bfloat16)

        gate_in = gated[:, halo_c : halo_c + breadth].reshape(height * breadth, channels)
        mix_in = mixes[p][:, halo_p : halo_p + breadth].reshape(height * breadth, channels)
        point_terms[p] = lax.dot_general(
            mix_in, gate_in, (((0,), (0,)), ((), ())), preferred_element_type=jnp.float32
        )
        bias_terms[p] = jnp.sum(gate_in.astype(jnp.float32), axis=0)
        back_in = back_mix[:, halo_c : halo_c + breadth].astype(jnp.float32)
        padded = pad_rows(acts[p])
        halo_a = (acts[p].shape[1] - breadth) // 2
        rows_k = []
        for i in range(3):
            row_k = []
            for j in range(3):
                start = halo_a - 1 + j
                row_k.append(
                    jnp.sum(
                        back_in * padded[i : i + height, start : start + breadth].astype(jnp.float32),
                        axis=(0, 1),
                    )
                )
            rows_k.append(jnp.stack(row_k))
        depth_terms[p] = jnp.stack(rows_k)

        earlier = conv_backward(pad_rows(back_mix), depth)
        cotangent = ((masked[:, 1:-1] + earlier) * live).astype(jnp.bfloat16)
    input_grad = cotangent

    got_outcome = lax.ppermute(outcome, "pipe", [(0, 1)])
    got_grad = lax.ppermute(input_grad, "pipe", [(1, 0)])
    first = jnp.where(core == 0, input_grad, got_outcome)
    second = jnp.where(core == 0, got_grad, outcome)
    result = jnp.stack([first, second])[None]

    pieces = (jnp.stack(depth_terms), jnp.stack(point_terms), jnp.stack(bias_terms))
    flat = jnp.concatenate([piece.reshape(layers, -1) for piece in pieces], axis=1)
    chunks = 2 * lax.axis_size("y") * lax.axis_size("x")
    size = flat.size
    rows = -(-size // (chunks * 128))
    rows = -(-rows // 8) * 8
    packed = jnp.pad(flat.reshape(-1), (0, chunks * rows * 128 - size)).reshape(chunks, rows, 128)
    flat = all_reduce(packed).reshape(-1)[:size].reshape(flat.shape)
    factor = 1.0 / math.sqrt(held.shape[0] * height * breadth * blk_count())
    chosen = layer_order[None, :] == jnp.arange(layers, dtype=layer_order.dtype)[:, None]
    flat = jnp.sum(jnp.where(chosen[:, :, None], flat[None, :, :], 0.0), axis=1) * factor
    ordered, at = [], 0
    for piece in pieces:
        width = piece[0].size
        ordered.append(flat[:, at : at + width].reshape(piece.shape))
        at += width
    return (result, ordered[0], ordered[1], ordered[2])


def solution(mesh):
    devices = mesh.devices
    blk = devices.shape[0]
    y_size = 4 if blk % 4 == 0 else 1
    rest = blk // y_size
    z_size = 8 if rest % 8 == 0 else rest
    x_size = rest // z_size
    torus = Mesh(devices.reshape(x_size, z_size, y_size, devices.shape[1]), BLK_AXES + ("pipe",))
    spec = P("pipe", None, None, BLK_AXES, None)
    in_specs = (spec, P(), P(), P(), P(), P())
    out_specs = (spec, P(), P(), P())
    return jax.shard_map(shards, mesh=torus, in_specs=in_specs, out_specs=out_specs, check_vma=False)
```

```python
import math

import jax
import jax.numpy as jnp
from jax import lax
from jax.experimental import pallas as pl
from jax.experimental.pallas import tpu as pltpu
from jax.sharding import Mesh, PartitionSpec as P

MESH_ID = pl.DeviceIdType.MESH

root_half = 0.7071067811865476
density_norm = 0.3989422804014327

X_HALO = 8
G_HALO = 4


BLK_AXES = ("x", "z", "y")


def blk_count():
    count = 1
    for axis in BLK_AXES:
        count *= lax.axis_size(axis)
    return count


def gelu_pair(preact):
    normal_cdf = 0.5 * (1.0 + lax.erf(preact * root_half))
    normal_pdf = density_norm * jnp.exp(-0.5 * preact * preact)
    return (preact * normal_cdf, normal_cdf + preact * normal_pdf)


def select_row(table, chosen):
    return lax.dynamic_index_in_dim(table, chosen, 0, keepdims=False)


def pad_rows(x):
    return jnp.pad(x, ((1, 1), (0, 0), (0, 0)))


def conv_forward(padded, depth):
    height = padded.shape[0] - 2
    breadth = padded.shape[1] - 2
    acc = jnp.zeros((height, breadth, padded.shape[2]), jnp.float32)
    for i in range(3):
        for j in range(3):
            acc = acc + depth[i, j] * padded[i : i + height, j : j + breadth].astype(jnp.float32)
    return acc


def conv_backward(spread, depth):
    height = spread.shape[0] - 2
    breadth = spread.shape[1] - 2
    acc = jnp.zeros((height, breadth, spread.shape[2]), jnp.float32)
    for i in range(3):
        for j in range(3):
            acc = acc + depth[i, j] * spread[
                2 - i : 2 - i + height, 2 - j : 2 - j + breadth
            ].astype(jnp.float32)
    return acc


def torus_coords(b):
    y_size, z_size = lax.axis_size("y"), lax.axis_size("z")
    return (b // (y_size * z_size), lax.rem(b // y_size, z_size), lax.rem(b, y_size))


def exchange_kernel(held_ref, edges_ref, body_out, lo_out, hi_out, body, lo, hi, send_sem, recv_sem):
    core = lax.axis_index("pipe")
    count = blk_count()
    here = (lax.axis_index("x") * lax.axis_size("z") + lax.axis_index("z")) * lax.axis_size("y") + lax.axis_index("y")
    right = torus_coords(lax.rem(here + 1, count))
    left = torus_coords(lax.rem(here + count - 1, count))
    mine = torus_coords(here)
    partner = mine + (1 - core,)
    targets = [partner] + [right + (m,) for m in range(2)] + [left + (m,) for m in range(2)]

    barrier = pltpu.get_barrier_semaphore()
    for target in targets:
        pl.semaphore_signal(barrier, inc=1, device_id=target, device_id_type=MESH_ID)
    pl.semaphore_wait(barrier, len(targets))

    copies = [
        pltpu.make_async_remote_copy(
            src_ref=held_ref.at[1 - core], dst_ref=body,
            send_sem=send_sem.at[0], recv_sem=recv_sem.at[0],
            device_id=partner, device_id_type=MESH_ID,
        )
    ]
    for m in range(2):
        copies.append(pltpu.make_async_remote_copy(
            src_ref=edges_ref.at[1, m], dst_ref=lo.at[core],
            send_sem=send_sem.at[1 + m], recv_sem=recv_sem.at[1 + core],
            device_id=right + (m,), device_id_type=MESH_ID,
        ))
        copies.append(pltpu.make_async_remote_copy(
            src_ref=edges_ref.at[0, m], dst_ref=hi.at[core],
            send_sem=send_sem.at[3 + m], recv_sem=recv_sem.at[3 + core],
            device_id=left + (m,), device_id_type=MESH_ID,
        ))
    for copy in copies:
        copy.start()
    copies[0].wait_recv()
    for k in range(2):
        pltpu.make_async_remote_copy(
            src_ref=edges_ref.at[1, k], dst_ref=lo.at[k],
            send_sem=send_sem.at[1 + k], recv_sem=recv_sem.at[1 + k],
            device_id=right + (k,), device_id_type=MESH_ID,
        ).wait_recv()
        pltpu.make_async_remote_copy(
            src_ref=edges_ref.at[0, k], dst_ref=hi.at[k],
            send_sem=send_sem.at[3 + k], recv_sem=recv_sem.at[3 + k],
            device_id=left + (k,), device_id_type=MESH_ID,
        ).wait_recv()
    for copy in copies:
        copy.wait_send()
    body_out[...] = body[...]
    lo_out[...] = lo[...]
    hi_out[...] = hi[...]


def exchange(held, edges):
    grid_shape = held.shape[1:]
    strip_shape = edges.shape[2:]
    vmem = pl.BlockSpec(memory_space=pltpu.VMEM)
    return pl.pallas_call(
        exchange_kernel,
        out_shape=(
            jax.ShapeDtypeStruct(grid_shape, held.dtype),
            jax.ShapeDtypeStruct((2,) + strip_shape, held.dtype),
            jax.ShapeDtypeStruct((2,) + strip_shape, held.dtype),
        ),
        in_specs=[vmem, vmem],
        out_specs=(vmem, vmem, vmem),
        scratch_shapes=[
            pltpu.VMEM(grid_shape, held.dtype),
            pltpu.VMEM((2,) + strip_shape, held.dtype),
            pltpu.VMEM((2,) + strip_shape, held.dtype),
            pltpu.SemaphoreType.DMA((5,)),
            pltpu.SemaphoreType.DMA((5,)),
        ],
        compiler_params=pltpu.CompilerParams(collective_id=0, has_side_effects=True),
    )(held, edges)


def group_members(axis):
    here = [lax.axis_index(name) for name in BLK_AXES] + [lax.axis_index("pipe")]
    slot = BLK_AXES.index(axis)
    return [tuple(here[:slot]) + (j,) + tuple(here[slot + 1 :]) for j in range(lax.axis_size(axis))]


def tree_sum(values):
    while len(values) > 1:
        values = [values[k] + values[k + 1] for k in range(0, len(values), 2)]
    return values[0]


def reduce_kernel(flat_ref, piece_ref, out_ref, other_ref, part, got_a, got_z, got_b, got_piece,
                  send_sem, recv_a, recv_z, recv_b, piece_send, piece_recv):
    core = lax.axis_index("pipe")
    my_y, my_z, my_x = (lax.axis_index(name) for name in ("y", "z", "x"))
    ny, nx = lax.axis_size("y"), lax.axis_size("x")
    row = [lax.axis_index(name) for name in BLK_AXES]
    groups = {
        "py": [(i, row[1], j, h) for h in range(2) for i in range(nx) for j in range(ny)],
        "z": group_members("z"),
    }
    places = {"py": (core * nx + my_x) * ny + my_y, "z": my_z}

    barrier = pltpu.get_barrier_semaphore()
    count = 0
    for axis in ("py", "z"):
        for j, member in enumerate(groups[axis]):
            @pl.when(j != places[axis])
            def _():
                pl.semaphore_signal(barrier, inc=1, device_id=member, device_id_type=MESH_ID)
        count += len(groups[axis]) - 1
    pl.semaphore_wait(barrier, count)

    sends = iter(range(send_sem.shape[0]))

    handover = pltpu.make_async_remote_copy(
        src_ref=piece_ref, dst_ref=got_piece, send_sem=piece_send.at[0], recv_sem=piece_recv.at[0],
        device_id=tuple(row) + (1 - core,), device_id_type=MESH_ID,
    )
    handover.start()

    def spread(axis, src_of, dst, sems):
        mine = places[axis]
        copies = []
        for j, member in enumerate(groups[axis]):
            copy = pltpu.make_async_remote_copy(
                src_ref=src_of(j), dst_ref=dst.at[mine], send_sem=send_sem.at[next(sends)],
                recv_sem=sems.at[mine], device_id=member, device_id_type=MESH_ID,
            )
            copies.append((j, copy))

            @pl.when(j != mine)
            def _():
                copy.start()
        for j, copy in copies:
            @pl.when(j != mine)
            def _():
                copy.wait_send()
                pltpu.make_async_remote_copy(
                    src_ref=src_of(j), dst_ref=dst.at[j], send_sem=send_sem.at[0],
                    recv_sem=sems.at[j], device_id=groups[axis][j], device_id_type=MESH_ID,
                ).wait_recv()

    got_a[places["py"]] = flat_ref[places["py"]]
    spread("py", lambda j: flat_ref.at[j], got_a, recv_a)
    part[...] = tree_sum([got_a[k] for k in range(len(groups["py"]))])

    got_z[my_z] = part[...]
    spread("z", lambda j: part, got_z, recv_z)
    part[...] = tree_sum([got_z[k] for k in range(len(groups["z"]))])

    got_b[places["py"]] = part[...]
    spread("py", lambda j: part, got_b, recv_b)
    out_ref[...] = got_b[...]
    handover.wait()
    other_ref[...] = got_piece[...]


def all_reduce(flat, piece):
    chunks, rows, lanes = flat.shape
    nz = lax.axis_size("z")
    chunk = (rows, lanes)
    sends = chunks + nz + chunks
    vmem = pl.BlockSpec(memory_space=pltpu.VMEM)
    return pl.pallas_call(
        reduce_kernel,
        out_shape=(
            jax.ShapeDtypeStruct(flat.shape, flat.dtype),
            jax.ShapeDtypeStruct(piece.shape, piece.dtype),
        ),
        in_specs=[vmem, vmem],
        out_specs=(vmem, vmem),
        scratch_shapes=[
            pltpu.VMEM(chunk, flat.dtype),
            pltpu.VMEM((chunks,) + chunk, flat.dtype),
            pltpu.VMEM((nz,) + chunk, flat.dtype),
            pltpu.VMEM((chunks,) + chunk, flat.dtype),
            pltpu.VMEM(piece.shape, piece.dtype),
            pltpu.SemaphoreType.DMA((sends,)),
            pltpu.SemaphoreType.DMA((chunks,)),
            pltpu.SemaphoreType.DMA((nz,)),
            pltpu.SemaphoreType.DMA((chunks,)),
            pltpu.SemaphoreType.DMA((1,)),
            pltpu.SemaphoreType.DMA((1,)),
        ],
        compiler_params=pltpu.CompilerParams(collective_id=1, has_side_effects=True),
    )(flat, piece)


def shards(endpoints, row_counts, layer_order, depth_weight, point_weight, point_bias):
    held = endpoints[0]
    height = held.shape[1]
    breadth = held.shape[2]
    channels = held.shape[3]
    layers = layer_order.shape[0]
    core = lax.axis_index("pipe")

    edges = jnp.stack([held[:, :, :X_HALO], held[:, :, breadth - X_HALO :]])
    body, lo, hi = exchange(held, edges)
    mine = select_row(held, core)
    x_in = jnp.where(core == 0, mine, body)
    g_in = jnp.where(core == 0, body, mine)
    x_wide = jnp.concatenate([lo[0], x_in, hi[0]], axis=1)
    g_wide = jnp.concatenate([lo[1][:, X_HALO - G_HALO :], g_in, hi[1][:, :G_HALO]], axis=1)

    counts = jnp.where(core == 0, row_counts[0:1], row_counts[1:2])
    live = (jnp.arange(height)[:, None, None] < counts[None, None, :]).astype(jnp.float32)

    placed = layer_order[:, None] == jnp.arange(layers, dtype=layer_order.dtype)[None, :]

    def pick(table):
        mask = placed.reshape(placed.shape + (1,) * (table.ndim - 1))
        return jnp.sum(jnp.where(mask, table[None], jnp.zeros((), table.dtype)), axis=1, dtype=table.dtype)

    by_position = [pick(table) for table in (depth_weight, point_weight, point_bias)]
    weights = [tuple(table[p] for table in by_position) for p in range(layers)]

    activation = (x_wide.astype(jnp.float32) * live).astype(jnp.bfloat16)
    acts, mixes, preacts = [], [], []
    for p in range(layers):
        depth, point, offset_vec = weights[p]
        acts.append(activation)
        mixed = conv_forward(pad_rows(activation), depth).astype(jnp.bfloat16)
        rows, span = mixed.shape[0], mixed.shape[1]
        preact = jnp.dot(
            mixed.reshape(rows * span, channels), point, preferred_element_type=jnp.float32
        ).reshape(rows, span, channels) + offset_vec
        mixes.append(mixed)
        preacts.append(preact)
        activation = (
            (activation[:, 1:-1].astype(jnp.float32) + gelu_pair(preact)[0]) * live
        ).astype(jnp.bfloat16)
    final_halo = X_HALO - layers
    outcome = activation[:, final_halo : final_halo + breadth]

    cotangent = g_wide
    depth_terms, point_terms, bias_terms = [None] * layers, [None] * layers, [None] * layers
    for p in range(layers - 1, -1, -1):
        depth, point, _ = weights[p]
        halo_c = (cotangent.shape[1] - breadth) // 2
        halo_p = (preacts[p].shape[1] - breadth) // 2
        shift = halo_p - halo_c
        span = cotangent.shape[1]
        preact = preacts[p][:, shift : shift + span]
        masked = cotangent.astype(jnp.float32) * live
        gated = (masked * gelu_pair(preact)[1]).astype(jnp.bfloat16)
        back_mix = lax.dot_general(
            gated.reshape(height * span, channels),
            point,
            (((1,), (1,)), ((), ())),
            preferred_element_type=jnp.float32,
        ).reshape(height, span, channels).astype(jnp.bfloat16)

        gate_in = gated[:, halo_c : halo_c + breadth].reshape(height * breadth, channels)
        mix_in = mixes[p][:, halo_p : halo_p + breadth].reshape(height * breadth, channels)
        point_terms[p] = lax.dot_general(
            mix_in, gate_in, (((0,), (0,)), ((), ())), preferred_element_type=jnp.float32
        )
        bias_terms[p] = jnp.sum(gate_in.astype(jnp.float32), axis=0)
        back_in = back_mix[:, halo_c : halo_c + breadth].astype(jnp.float32)
        padded = pad_rows(acts[p])
        halo_a = (acts[p].shape[1] - breadth) // 2
        rows_k = []
        for i in range(3):
            row_k = []
            for j in range(3):
                start = halo_a - 1 + j
                row_k.append(
                    jnp.sum(
                        back_in * padded[i : i + height, start : start + breadth].astype(jnp.float32),
                        axis=(0, 1),
                    )
                )
            rows_k.append(jnp.stack(row_k))
        depth_terms[p] = jnp.stack(rows_k)

        earlier = conv_backward(pad_rows(back_mix), depth)
        cotangent = ((masked[:, 1:-1] + earlier) * live).astype(jnp.bfloat16)
    input_grad = cotangent


    pieces = (jnp.stack(depth_terms), jnp.stack(point_terms), jnp.stack(bias_terms))
    flat = jnp.concatenate([piece.reshape(layers, -1) for piece in pieces], axis=1)
    chunks = 2 * lax.axis_size("y") * lax.axis_size("x")
    size = flat.size
    rows = -(-size // (chunks * 128))
    rows = -(-rows // 8) * 8
    packed = jnp.pad(flat.reshape(-1), (0, chunks * rows * 128 - size)).reshape(chunks, rows, 128)
    piece = jnp.where(core == 0, outcome, input_grad)
    reduced, other = all_reduce(packed, piece)
    flat = reduced.reshape(-1)[:size].reshape(flat.shape)
    first = jnp.where(core == 0, input_grad, other)
    second = jnp.where(core == 0, other, outcome)
    result = jnp.stack([first, second])[None]
    factor = 1.0 / math.sqrt(held.shape[0] * height * breadth * blk_count())
    chosen = layer_order[None, :] == jnp.arange(layers, dtype=layer_order.dtype)[:, None]
    flat = jnp.sum(jnp.where(chosen[:, :, None], flat[None, :, :], 0.0), axis=1) * factor
    ordered, at = [], 0
    for piece in pieces:
        width = piece[0].size
        ordered.append(flat[:, at : at + width].reshape(piece.shape))
        at += width
    return (result, ordered[0], ordered[1], ordered[2])


def solution(mesh):
    devices = mesh.devices
    blk = devices.shape[0]
    y_size = 4 if blk % 4 == 0 else 1
    rest = blk // y_size
    z_size = 8 if rest % 8 == 0 else rest
    x_size = rest // z_size
    torus = Mesh(devices.reshape(x_size, z_size, y_size, devices.shape[1]), BLK_AXES + ("pipe",))
    spec = P("pipe", None, None, BLK_AXES, None)
    in_specs = (spec, P(), P(), P(), P(), P())
    out_specs = (spec, P(), P(), P())
    return jax.shard_map(shards, mesh=torus, in_specs=in_specs, out_specs=out_specs, check_vma=False)
```

```python
import math

import jax
import jax.numpy as jnp
from jax import lax
from jax.experimental import pallas as pl
from jax.experimental.pallas import tpu as pltpu
from jax.sharding import Mesh, PartitionSpec as P

MESH_ID = pl.DeviceIdType.MESH

root_half = 0.7071067811865476
density_norm = 0.3989422804014327

X_HALO = 8
G_HALO = 4


BLK_AXES = ("x", "z", "y")


def blk_count():
    count = 1
    for axis in BLK_AXES:
        count *= lax.axis_size(axis)
    return count


def gelu_pair(preact):
    normal_cdf = 0.5 * (1.0 + lax.erf(preact * root_half))
    normal_pdf = density_norm * jnp.exp(-0.5 * preact * preact)
    return (preact * normal_cdf, normal_cdf + preact * normal_pdf)


def select_row(table, chosen):
    return lax.dynamic_index_in_dim(table, chosen, 0, keepdims=False)


def pad_rows(x):
    return jnp.pad(x, ((1, 1), (0, 0), (0, 0)))


def conv_forward(padded, depth):
    height = padded.shape[0] - 2
    breadth = padded.shape[1] - 2
    acc = jnp.zeros((height, breadth, padded.shape[2]), jnp.float32)
    for i in range(3):
        for j in range(3):
            acc = acc + depth[i, j] * padded[i : i + height, j : j + breadth].astype(jnp.float32)
    return acc


def conv_backward(spread, depth):
    height = spread.shape[0] - 2
    breadth = spread.shape[1] - 2
    acc = jnp.zeros((height, breadth, spread.shape[2]), jnp.float32)
    for i in range(3):
        for j in range(3):
            acc = acc + depth[i, j] * spread[
                2 - i : 2 - i + height, 2 - j : 2 - j + breadth
            ].astype(jnp.float32)
    return acc


def torus_coords(b):
    y_size, z_size = lax.axis_size("y"), lax.axis_size("z")
    return (b // (y_size * z_size), lax.rem(b // y_size, z_size), lax.rem(b, y_size))


def exchange_kernel(held_ref, edges_ref, body_out, lo_out, hi_out, body, lo, hi, send_sem, recv_sem):
    core = lax.axis_index("pipe")
    count = blk_count()
    here = (lax.axis_index("x") * lax.axis_size("z") + lax.axis_index("z")) * lax.axis_size("y") + lax.axis_index("y")
    right = torus_coords(lax.rem(here + 1, count))
    left = torus_coords(lax.rem(here + count - 1, count))
    mine = torus_coords(here)
    partner = mine + (1 - core,)
    targets = [partner] + [right + (m,) for m in range(2)] + [left + (m,) for m in range(2)]

    barrier = pltpu.get_barrier_semaphore()
    for target in targets:
        pl.semaphore_signal(barrier, inc=1, device_id=target, device_id_type=MESH_ID)
    pl.semaphore_wait(barrier, len(targets))

    copies = [
        pltpu.make_async_remote_copy(
            src_ref=held_ref.at[1 - core], dst_ref=body,
            send_sem=send_sem.at[0], recv_sem=recv_sem.at[0],
            device_id=partner, device_id_type=MESH_ID,
        )
    ]
    for m in range(2):
        copies.append(pltpu.make_async_remote_copy(
            src_ref=edges_ref.at[1, m], dst_ref=lo.at[core],
            send_sem=send_sem.at[1 + m], recv_sem=recv_sem.at[1 + core],
            device_id=right + (m,), device_id_type=MESH_ID,
        ))
        copies.append(pltpu.make_async_remote_copy(
            src_ref=edges_ref.at[0, m], dst_ref=hi.at[core],
            send_sem=send_sem.at[3 + m], recv_sem=recv_sem.at[3 + core],
            device_id=left + (m,), device_id_type=MESH_ID,
        ))
    for copy in copies:
        copy.start()
    copies[0].wait_recv()
    for k in range(2):
        pltpu.make_async_remote_copy(
            src_ref=edges_ref.at[1, k], dst_ref=lo.at[k],
            send_sem=send_sem.at[1 + k], recv_sem=recv_sem.at[1 + k],
            device_id=right + (k,), device_id_type=MESH_ID,
        ).wait_recv()
        pltpu.make_async_remote_copy(
            src_ref=edges_ref.at[0, k], dst_ref=hi.at[k],
            send_sem=send_sem.at[3 + k], recv_sem=recv_sem.at[3 + k],
            device_id=left + (k,), device_id_type=MESH_ID,
        ).wait_recv()
    for copy in copies:
        copy.wait_send()
    body_out[...] = body[...]
    lo_out[...] = lo[...]
    hi_out[...] = hi[...]


def exchange(held, edges):
    grid_shape = held.shape[1:]
    strip_shape = edges.shape[2:]
    vmem = pl.BlockSpec(memory_space=pltpu.VMEM)
    return pl.pallas_call(
        exchange_kernel,
        out_shape=(
            jax.ShapeDtypeStruct(grid_shape, held.dtype),
            jax.ShapeDtypeStruct((2,) + strip_shape, held.dtype),
            jax.ShapeDtypeStruct((2,) + strip_shape, held.dtype),
        ),
        in_specs=[vmem, vmem],
        out_specs=(vmem, vmem, vmem),
        scratch_shapes=[
            pltpu.VMEM(grid_shape, held.dtype),
            pltpu.VMEM((2,) + strip_shape, held.dtype),
            pltpu.VMEM((2,) + strip_shape, held.dtype),
            pltpu.SemaphoreType.DMA((5,)),
            pltpu.SemaphoreType.DMA((5,)),
        ],
        compiler_params=pltpu.CompilerParams(collective_id=0, has_side_effects=True),
    )(held, edges)


def group_members(axis):
    here = [lax.axis_index(name) for name in BLK_AXES] + [lax.axis_index("pipe")]
    slot = BLK_AXES.index(axis)
    return [tuple(here[:slot]) + (j,) + tuple(here[slot + 1 :]) for j in range(lax.axis_size(axis))]


def tree_sum(values):
    while len(values) > 1:
        values = [values[k] + values[k + 1] for k in range(0, len(values), 2)]
    return values[0]


def reduce_kernel(flat_ref, out_ref, part, got_a, got_z, got_b,
                  send_sem, recv_a, recv_z, recv_b):
    core = lax.axis_index("pipe")
    my_y, my_z, my_x = (lax.axis_index(name) for name in ("y", "z", "x"))
    ny, nx = lax.axis_size("y"), lax.axis_size("x")
    row = [lax.axis_index(name) for name in BLK_AXES]
    groups = {
        "py": [(i, row[1], j, h) for h in range(2) for i in range(nx) for j in range(ny)],
        "z": group_members("z"),
    }
    places = {"py": (core * nx + my_x) * ny + my_y, "z": my_z}

    barrier = pltpu.get_barrier_semaphore()
    count = 0
    for axis in ("py", "z"):
        for j, member in enumerate(groups[axis]):
            @pl.when(j != places[axis])
            def _():
                pl.semaphore_signal(barrier, inc=1, device_id=member, device_id_type=MESH_ID)
        count += len(groups[axis]) - 1
    pl.semaphore_wait(barrier, count)

    sends = iter(range(send_sem.shape[0]))

    def spread(axis, src_of, dst, sems):
        mine = places[axis]
        copies = []
        for j, member in enumerate(groups[axis]):
            copy = pltpu.make_async_remote_copy(
                src_ref=src_of(j), dst_ref=dst.at[mine], send_sem=send_sem.at[next(sends)],
                recv_sem=sems.at[mine], device_id=member, device_id_type=MESH_ID,
            )
            copies.append((j, copy))

            @pl.when(j != mine)
            def _():
                copy.start()
        for j, copy in copies:
            @pl.when(j != mine)
            def _():
                copy.wait_send()
                pltpu.make_async_remote_copy(
                    src_ref=src_of(j), dst_ref=dst.at[j], send_sem=send_sem.at[0],
                    recv_sem=sems.at[j], device_id=groups[axis][j], device_id_type=MESH_ID,
                ).wait_recv()

    got_a[places["py"]] = flat_ref[places["py"]]
    spread("py", lambda j: flat_ref.at[j], got_a, recv_a)
    part[...] = tree_sum([got_a[k] for k in range(len(groups["py"]))])

    got_z[my_z] = part[...]
    spread("z", lambda j: part, got_z, recv_z)
    part[...] = tree_sum([got_z[k] for k in range(len(groups["z"]))])

    got_b[places["py"]] = part[...]
    spread("py", lambda j: part, got_b, recv_b)
    out_ref[...] = got_b[...]


def all_reduce(flat):
    chunks, rows, lanes = flat.shape
    nz = lax.axis_size("z")
    chunk = (rows, lanes)
    sends = chunks + nz + chunks
    vmem = pl.BlockSpec(memory_space=pltpu.VMEM)
    return pl.pallas_call(
        reduce_kernel,
        out_shape=jax.ShapeDtypeStruct(flat.shape, flat.dtype),
        in_specs=[vmem],
        out_specs=vmem,
        scratch_shapes=[
            pltpu.VMEM(chunk, flat.dtype),
            pltpu.VMEM((chunks,) + chunk, flat.dtype),
            pltpu.VMEM((nz,) + chunk, flat.dtype),
            pltpu.VMEM((chunks,) + chunk, flat.dtype),
            pltpu.SemaphoreType.DMA((sends,)),
            pltpu.SemaphoreType.DMA((chunks,)),
            pltpu.SemaphoreType.DMA((nz,)),
            pltpu.SemaphoreType.DMA((chunks,)),
        ],
        compiler_params=pltpu.CompilerParams(collective_id=1, has_side_effects=True),
    )(flat)


def shards(endpoints, row_counts, layer_order, depth_weight, point_weight, point_bias):
    held = endpoints[0]
    height = held.shape[1]
    breadth = held.shape[2]
    channels = held.shape[3]
    layers = layer_order.shape[0]
    core = lax.axis_index("pipe")

    edges = jnp.stack([held[:, :, :X_HALO], held[:, :, breadth - X_HALO :]])
    body, lo, hi = exchange(held, edges)
    mine = select_row(held, core)
    x_in = jnp.where(core == 0, mine, body)
    g_in = jnp.where(core == 0, body, mine)
    x_wide = jnp.concatenate([lo[0], x_in, hi[0]], axis=1)
    g_wide = jnp.concatenate([lo[1][:, X_HALO - G_HALO :], g_in, hi[1][:, :G_HALO]], axis=1)

    both = (jnp.arange(height, dtype=row_counts.dtype)[:, None] < row_counts[None, :]).astype(jnp.float32)
    live = jnp.where(core == 0, both[:, 0], both[:, 1])[:, None, None]

    placed = layer_order[:, None] == jnp.arange(layers, dtype=layer_order.dtype)[None, :]

    def pick(table):
        mask = placed.reshape(placed.shape + (1,) * (table.ndim - 1))
        return jnp.sum(jnp.where(mask, table[None], jnp.zeros((), table.dtype)), axis=1, dtype=table.dtype)

    by_position = [pick(table) for table in (depth_weight, point_weight, point_bias)]
    weights = [tuple(table[p] for table in by_position) for p in range(layers)]

    activation = (x_wide.astype(jnp.float32) * live).astype(jnp.bfloat16)
    acts, mixes, preacts = [], [], []
    for p in range(layers):
        depth, point, offset_vec = weights[p]
        acts.append(activation)
        mixed = conv_forward(pad_rows(activation), depth).astype(jnp.bfloat16)
        rows, span = mixed.shape[0], mixed.shape[1]
        preact = jnp.dot(
            mixed.reshape(rows * span, channels), point, preferred_element_type=jnp.float32
        ).reshape(rows, span, channels) + offset_vec
        mixes.append(mixed)
        preacts.append(preact)
        activation = (
            (activation[:, 1:-1].astype(jnp.float32) + gelu_pair(preact)[0]) * live
        ).astype(jnp.bfloat16)
    final_halo = X_HALO - layers
    outcome = activation[:, final_halo : final_halo + breadth]

    cotangent = g_wide
    depth_terms, point_terms, bias_terms = [None] * layers, [None] * layers, [None] * layers
    for p in range(layers - 1, -1, -1):
        depth, point, _ = weights[p]
        halo_c = (cotangent.shape[1] - breadth) // 2
        halo_p = (preacts[p].shape[1] - breadth) // 2
        shift = halo_p - halo_c
        span = cotangent.shape[1]
        preact = preacts[p][:, shift : shift + span]
        masked = cotangent.astype(jnp.float32) * live
        gated = (masked * gelu_pair(preact)[1]).astype(jnp.bfloat16)
        back_mix = lax.dot_general(
            gated.reshape(height * span, channels),
            point,
            (((1,), (1,)), ((), ())),
            preferred_element_type=jnp.float32,
        ).reshape(height, span, channels).astype(jnp.bfloat16)

        gate_in = gated[:, halo_c : halo_c + breadth].reshape(height * breadth, channels)
        mix_in = mixes[p][:, halo_p : halo_p + breadth].reshape(height * breadth, channels)
        point_terms[p] = lax.dot_general(
            mix_in, gate_in, (((0,), (0,)), ((), ())), preferred_element_type=jnp.float32
        )
        bias_terms[p] = jnp.sum(gate_in.astype(jnp.float32), axis=0)
        back_in = back_mix[:, halo_c : halo_c + breadth].astype(jnp.float32)
        padded = pad_rows(acts[p])
        halo_a = (acts[p].shape[1] - breadth) // 2
        rows_k = []
        for i in range(3):
            row_k = []
            for j in range(3):
                start = halo_a - 1 + j
                row_k.append(
                    jnp.sum(
                        back_in * padded[i : i + height, start : start + breadth].astype(jnp.float32),
                        axis=(0, 1),
                    )
                )
            rows_k.append(jnp.stack(row_k))
        depth_terms[p] = jnp.stack(rows_k)

        earlier = conv_backward(pad_rows(back_mix), depth)
        cotangent = ((masked[:, 1:-1] + earlier) * live).astype(jnp.bfloat16)
    input_grad = cotangent

    got_outcome = lax.ppermute(outcome, "pipe", [(0, 1)])
    got_grad = lax.ppermute(input_grad, "pipe", [(1, 0)])
    first = jnp.where(core == 0, input_grad, got_outcome)
    second = jnp.where(core == 0, got_grad, outcome)
    result = jnp.stack([first, second])[None]

    pieces = (jnp.stack(depth_terms), jnp.stack(point_terms), jnp.stack(bias_terms))
    flat = jnp.concatenate([piece.reshape(layers, -1) for piece in pieces], axis=1)
    chunks = 2 * lax.axis_size("y") * lax.axis_size("x")
    size = flat.size
    rows = -(-size // (chunks * 128))
    rows = -(-rows // 8) * 8
    packed = jnp.pad(flat.reshape(-1), (0, chunks * rows * 128 - size)).reshape(chunks, rows, 128)
    flat = all_reduce(packed).reshape(-1)[:size].reshape(flat.shape)
    factor = 1.0 / math.sqrt(held.shape[0] * height * breadth * blk_count())
    chosen = layer_order[None, :] == jnp.arange(layers, dtype=layer_order.dtype)[:, None]
    flat = jnp.sum(jnp.where(chosen[:, :, None], flat[None, :, :], 0.0), axis=1) * factor
    ordered, at = [], 0
    for piece in pieces:
        width = piece[0].size
        ordered.append(flat[:, at : at + width].reshape(piece.shape))
        at += width
    return (result, ordered[0], ordered[1], ordered[2])


def solution(mesh):
    devices = mesh.devices
    blk = devices.shape[0]
    y_size = 4 if blk % 4 == 0 else 1
    rest = blk // y_size
    z_size = 8 if rest % 8 == 0 else rest
    x_size = rest // z_size
    torus = Mesh(devices.reshape(x_size, z_size, y_size, devices.shape[1]), BLK_AXES + ("pipe",))
    spec = P("pipe", None, None, BLK_AXES, None)
    in_specs = (spec, P(), P(), P(), P(), P())
    out_specs = (spec, P(), P(), P())
    return jax.shard_map(shards, mesh=torus, in_specs=in_specs, out_specs=out_specs, check_vma=False)
```

```python
import math

import jax
import jax.numpy as jnp
from jax import lax
from jax.experimental import pallas as pl
from jax.experimental.pallas import tpu as pltpu
from jax.sharding import Mesh, PartitionSpec as P

MESH_ID = pl.DeviceIdType.MESH

root_half = 0.7071067811865476
density_norm = 0.3989422804014327

X_HALO = 8
G_HALO = 4


BLK_AXES = ("x", "z", "y")


def blk_count():
    count = 1
    for axis in BLK_AXES:
        count *= lax.axis_size(axis)
    return count


def gelu_pair(preact):
    normal_cdf = 0.5 * (1.0 + lax.erf(preact * root_half))
    normal_pdf = density_norm * jnp.exp(-0.5 * preact * preact)
    return (preact * normal_cdf, normal_cdf + preact * normal_pdf)


def select_row(table, chosen):
    return lax.dynamic_index_in_dim(table, chosen, 0, keepdims=False)


def pad_rows(x):
    return jnp.pad(x, ((1, 1), (0, 0), (0, 0)))


def conv_forward(padded, depth):
    height = padded.shape[0] - 2
    breadth = padded.shape[1] - 2
    acc = jnp.zeros((height, breadth, padded.shape[2]), jnp.float32)
    for i in range(3):
        for j in range(3):
            acc = acc + depth[i, j] * padded[i : i + height, j : j + breadth].astype(jnp.float32)
    return acc


def conv_backward(spread, depth):
    height = spread.shape[0] - 2
    breadth = spread.shape[1] - 2
    acc = jnp.zeros((height, breadth, spread.shape[2]), jnp.float32)
    for i in range(3):
        for j in range(3):
            acc = acc + depth[i, j] * spread[
                2 - i : 2 - i + height, 2 - j : 2 - j + breadth
            ].astype(jnp.float32)
    return acc


def torus_coords(b):
    y_size, z_size = lax.axis_size("y"), lax.axis_size("z")
    return (b // (y_size * z_size), lax.rem(b // y_size, z_size), lax.rem(b, y_size))


def exchange_kernel(held_ref, edges_ref, body_out, lo_out, hi_out, body, lo, hi, send_sem, recv_sem):
    core = lax.axis_index("pipe")
    count = blk_count()
    here = (lax.axis_index("x") * lax.axis_size("z") + lax.axis_index("z")) * lax.axis_size("y") + lax.axis_index("y")
    right = torus_coords(lax.rem(here + 1, count))
    left = torus_coords(lax.rem(here + count - 1, count))
    mine = torus_coords(here)
    partner = mine + (1 - core,)
    targets = [partner] + [right + (m,) for m in range(2)] + [left + (m,) for m in range(2)]

    barrier = pltpu.get_barrier_semaphore()
    for target in targets:
        pl.semaphore_signal(barrier, inc=1, device_id=target, device_id_type=MESH_ID)
    pl.semaphore_wait(barrier, len(targets))

    copies = [
        pltpu.make_async_remote_copy(
            src_ref=held_ref.at[1 - core], dst_ref=body,
            send_sem=send_sem.at[0], recv_sem=recv_sem.at[0],
            device_id=partner, device_id_type=MESH_ID,
        )
    ]
    for m in range(2):
        copies.append(pltpu.make_async_remote_copy(
            src_ref=edges_ref.at[1, m], dst_ref=lo.at[core],
            send_sem=send_sem.at[1 + m], recv_sem=recv_sem.at[1 + core],
            device_id=right + (m,), device_id_type=MESH_ID,
        ))
        copies.append(pltpu.make_async_remote_copy(
            src_ref=edges_ref.at[0, m], dst_ref=hi.at[core],
            send_sem=send_sem.at[3 + m], recv_sem=recv_sem.at[3 + core],
            device_id=left + (m,), device_id_type=MESH_ID,
        ))
    for copy in copies:
        copy.start()
    copies[0].wait_recv()
    for k in range(2):
        pltpu.make_async_remote_copy(
            src_ref=edges_ref.at[1, k], dst_ref=lo.at[k],
            send_sem=send_sem.at[1 + k], recv_sem=recv_sem.at[1 + k],
            device_id=right + (k,), device_id_type=MESH_ID,
        ).wait_recv()
        pltpu.make_async_remote_copy(
            src_ref=edges_ref.at[0, k], dst_ref=hi.at[k],
            send_sem=send_sem.at[3 + k], recv_sem=recv_sem.at[3 + k],
            device_id=left + (k,), device_id_type=MESH_ID,
        ).wait_recv()
    for copy in copies:
        copy.wait_send()
    body_out[...] = body[...]
    lo_out[...] = lo[...]
    hi_out[...] = hi[...]


def exchange(held, edges):
    grid_shape = held.shape[1:]
    strip_shape = edges.shape[2:]
    vmem = pl.BlockSpec(memory_space=pltpu.VMEM)
    return pl.pallas_call(
        exchange_kernel,
        out_shape=(
            jax.ShapeDtypeStruct(grid_shape, held.dtype),
            jax.ShapeDtypeStruct((2,) + strip_shape, held.dtype),
            jax.ShapeDtypeStruct((2,) + strip_shape, held.dtype),
        ),
        in_specs=[vmem, vmem],
        out_specs=(vmem, vmem, vmem),
        scratch_shapes=[
            pltpu.VMEM(grid_shape, held.dtype),
            pltpu.VMEM((2,) + strip_shape, held.dtype),
            pltpu.VMEM((2,) + strip_shape, held.dtype),
            pltpu.SemaphoreType.DMA((5,)),
            pltpu.SemaphoreType.DMA((5,)),
        ],
        compiler_params=pltpu.CompilerParams(collective_id=0, has_side_effects=True),
    )(held, edges)


def group_members(axis):
    here = [lax.axis_index(name) for name in BLK_AXES] + [lax.axis_index("pipe")]
    slot = BLK_AXES.index(axis)
    return [tuple(here[:slot]) + (j,) + tuple(here[slot + 1 :]) for j in range(lax.axis_size(axis))]


def tree_sum(values):
    while len(values) > 1:
        values = [values[k] + values[k + 1] for k in range(0, len(values), 2)]
    return values[0]


def reduce_kernel(flat_ref, out_ref, part, got_a, got_z, got_b,
                  send_sem, recv_a, recv_z, recv_b):
    core = lax.axis_index("pipe")
    my_y, my_z, my_x = (lax.axis_index(name) for name in ("y", "z", "x"))
    ny, nx = lax.axis_size("y"), lax.axis_size("x")
    row = [lax.axis_index(name) for name in BLK_AXES]
    groups = {
        "py": [(i, row[1], j, h) for h in range(2) for i in range(nx) for j in range(ny)],
        "z": group_members("z"),
    }
    places = {"py": (core * nx + my_x) * ny + my_y, "z": my_z}

    barrier = pltpu.get_barrier_semaphore()
    count = 0
    for axis in ("py", "z"):
        for j, member in enumerate(groups[axis]):
            @pl.when(j != places[axis])
            def _():
                pl.semaphore_signal(barrier, inc=1, device_id=member, device_id_type=MESH_ID)
        count += len(groups[axis]) - 1
    pl.semaphore_wait(barrier, count)

    sends = iter(range(send_sem.shape[0]))

    def spread(axis, src_of, dst, sems):
        mine = places[axis]
        copies = []
        for j, member in enumerate(groups[axis]):
            copy = pltpu.make_async_remote_copy(
                src_ref=src_of(j), dst_ref=dst.at[mine], send_sem=send_sem.at[next(sends)],
                recv_sem=sems.at[mine], device_id=member, device_id_type=MESH_ID,
            )
            copies.append((j, copy))

            @pl.when(j != mine)
            def _():
                copy.start()
        for j, copy in copies:
            @pl.when(j != mine)
            def _():
                copy.wait_send()
                pltpu.make_async_remote_copy(
                    src_ref=src_of(j), dst_ref=dst.at[j], send_sem=send_sem.at[0],
                    recv_sem=sems.at[j], device_id=groups[axis][j], device_id_type=MESH_ID,
                ).wait_recv()

    got_a[places["py"]] = flat_ref[places["py"]]
    spread("py", lambda j: flat_ref.at[j], got_a, recv_a)
    part[...] = tree_sum([got_a[k] for k in range(len(groups["py"]))])

    got_z[my_z] = part[...]
    spread("z", lambda j: part, got_z, recv_z)
    part[...] = tree_sum([got_z[k] for k in range(len(groups["z"]))])

    got_b[places["py"]] = part[...]
    spread("py", lambda j: part, got_b, recv_b)
    out_ref[...] = got_b[...]


def all_reduce(flat):
    chunks, rows, lanes = flat.shape
    nz = lax.axis_size("z")
    chunk = (rows, lanes)
    sends = chunks + nz + chunks
    vmem = pl.BlockSpec(memory_space=pltpu.VMEM)
    return pl.pallas_call(
        reduce_kernel,
        out_shape=jax.ShapeDtypeStruct(flat.shape, flat.dtype),
        in_specs=[vmem],
        out_specs=vmem,
        scratch_shapes=[
            pltpu.VMEM(chunk, flat.dtype),
            pltpu.VMEM((chunks,) + chunk, flat.dtype),
            pltpu.VMEM((nz,) + chunk, flat.dtype),
            pltpu.VMEM((chunks,) + chunk, flat.dtype),
            pltpu.SemaphoreType.DMA((sends,)),
            pltpu.SemaphoreType.DMA((chunks,)),
            pltpu.SemaphoreType.DMA((nz,)),
            pltpu.SemaphoreType.DMA((chunks,)),
        ],
        compiler_params=pltpu.CompilerParams(collective_id=1, has_side_effects=True),
    )(flat)


def shards(endpoints, row_counts, layer_order, depth_weight, point_weight, point_bias):
    held = endpoints[0]
    height = held.shape[1]
    breadth = held.shape[2]
    channels = held.shape[3]
    layers = layer_order.shape[0]
    core = lax.axis_index("pipe")

    edges = jnp.stack([held[:, :, :X_HALO], held[:, :, breadth - X_HALO :]])
    body, lo, hi = exchange(held, edges)
    x_in = jnp.where(core == 0, held[0], body)
    g_in = jnp.where(core == 0, body, held[1])
    x_wide = jnp.concatenate([lo[0], x_in, hi[0]], axis=1)
    g_wide = jnp.concatenate([lo[1][:, X_HALO - G_HALO :], g_in, hi[1][:, :G_HALO]], axis=1)

    both = (jnp.arange(height, dtype=row_counts.dtype)[:, None] < row_counts[None, :]).astype(jnp.float32)
    live = jnp.where(core == 0, both[:, 0], both[:, 1])[:, None, None]

    placed = layer_order[:, None] == jnp.arange(layers, dtype=layer_order.dtype)[None, :]

    def pick(table):
        mask = placed.reshape(placed.shape + (1,) * (table.ndim - 1))
        return jnp.sum(jnp.where(mask, table[None], jnp.zeros((), table.dtype)), axis=1, dtype=table.dtype)

    by_position = [pick(table) for table in (depth_weight, point_weight, point_bias)]
    weights = [tuple(table[p] for table in by_position) for p in range(layers)]

    activation = (x_wide.astype(jnp.float32) * live).astype(jnp.bfloat16)
    acts, mixes, preacts = [], [], []
    for p in range(layers):
        depth, point, offset_vec = weights[p]
        acts.append(activation)
        mixed = conv_forward(pad_rows(activation), depth).astype(jnp.bfloat16)
        rows, span = mixed.shape[0], mixed.shape[1]
        preact = jnp.dot(
            mixed.reshape(rows * span, channels), point, preferred_element_type=jnp.float32
        ).reshape(rows, span, channels) + offset_vec
        mixes.append(mixed)
        preacts.append(preact)
        activation = (
            (activation[:, 1:-1].astype(jnp.float32) + gelu_pair(preact)[0]) * live
        ).astype(jnp.bfloat16)
    final_halo = X_HALO - layers
    outcome = activation[:, final_halo : final_halo + breadth]

    cotangent = g_wide
    depth_terms, point_terms, bias_terms = [None] * layers, [None] * layers, [None] * layers
    for p in range(layers - 1, -1, -1):
        depth, point, _ = weights[p]
        halo_c = (cotangent.shape[1] - breadth) // 2
        halo_p = (preacts[p].shape[1] - breadth) // 2
        shift = halo_p - halo_c
        span = cotangent.shape[1]
        preact = preacts[p][:, shift : shift + span]
        masked = cotangent.astype(jnp.float32) * live
        gated = (masked * gelu_pair(preact)[1]).astype(jnp.bfloat16)
        back_mix = lax.dot_general(
            gated.reshape(height * span, channels),
            point,
            (((1,), (1,)), ((), ())),
            preferred_element_type=jnp.float32,
        ).reshape(height, span, channels).astype(jnp.bfloat16)

        gate_in = gated[:, halo_c : halo_c + breadth].reshape(height * breadth, channels)
        mix_in = mixes[p][:, halo_p : halo_p + breadth].reshape(height * breadth, channels)
        point_terms[p] = lax.dot_general(
            mix_in, gate_in, (((0,), (0,)), ((), ())), preferred_element_type=jnp.float32
        )
        bias_terms[p] = jnp.sum(gate_in.astype(jnp.float32), axis=0)
        back_in = back_mix[:, halo_c : halo_c + breadth].astype(jnp.float32)
        padded = pad_rows(acts[p])
        halo_a = (acts[p].shape[1] - breadth) // 2
        rows_k = []
        for i in range(3):
            row_k = []
            for j in range(3):
                start = halo_a - 1 + j
                row_k.append(
                    jnp.sum(
                        back_in * padded[i : i + height, start : start + breadth].astype(jnp.float32),
                        axis=(0, 1),
                    )
                )
            rows_k.append(jnp.stack(row_k))
        depth_terms[p] = jnp.stack(rows_k)

        earlier = conv_backward(pad_rows(back_mix), depth)
        cotangent = ((masked[:, 1:-1] + earlier) * live).astype(jnp.bfloat16)
    input_grad = cotangent

    got_outcome = lax.ppermute(outcome, "pipe", [(0, 1)])
    got_grad = lax.ppermute(input_grad, "pipe", [(1, 0)])
    first = jnp.where(core == 0, input_grad, got_outcome)
    second = jnp.where(core == 0, got_grad, outcome)
    result = jnp.stack([first, second])[None]

    pieces = (jnp.stack(depth_terms), jnp.stack(point_terms), jnp.stack(bias_terms))
    flat = jnp.concatenate([piece.reshape(layers, -1) for piece in pieces], axis=1)
    chunks = 2 * lax.axis_size("y") * lax.axis_size("x")
    size = flat.size
    rows = -(-size // (chunks * 128))
    rows = -(-rows // 8) * 8
    packed = jnp.pad(flat.reshape(-1), (0, chunks * rows * 128 - size)).reshape(chunks, rows, 128)
    flat = all_reduce(packed).reshape(-1)[:size].reshape(flat.shape)
    factor = 1.0 / math.sqrt(held.shape[0] * height * breadth * blk_count())
    chosen = layer_order[None, :] == jnp.arange(layers, dtype=layer_order.dtype)[:, None]
    flat = jnp.sum(jnp.where(chosen[:, :, None], flat[None, :, :], 0.0), axis=1) * factor
    ordered, at = [], 0
    for piece in pieces:
        width = piece[0].size
        ordered.append(flat[:, at : at + width].reshape(piece.shape))
        at += width
    return (result, ordered[0], ordered[1], ordered[2])


def solution(mesh):
    devices = mesh.devices
    blk = devices.shape[0]
    y_size = 4 if blk % 4 == 0 else 1
    rest = blk // y_size
    z_size = 8 if rest % 8 == 0 else rest
    x_size = rest // z_size
    torus = Mesh(devices.reshape(x_size, z_size, y_size, devices.shape[1]), BLK_AXES + ("pipe",))
    spec = P("pipe", None, None, BLK_AXES, None)
    in_specs = (spec, P(), P(), P(), P(), P())
    out_specs = (spec, P(), P(), P())
    return jax.shard_map(shards, mesh=torus, in_specs=in_specs, out_specs=out_specs, check_vma=False)
```

```python
import math

import jax
import jax.numpy as jnp
from jax import lax
from jax.experimental import pallas as pl
from jax.experimental.pallas import tpu as pltpu
from jax.sharding import Mesh, PartitionSpec as P

MESH_ID = pl.DeviceIdType.MESH

root_half = 0.7071067811865476
density_norm = 0.3989422804014327

X_HALO = 8
G_HALO = 4


BLK_AXES = ("x", "z", "y")


def blk_count():
    count = 1
    for axis in BLK_AXES:
        count *= lax.axis_size(axis)
    return count


def gelu_pair(preact):
    normal_cdf = 0.5 * (1.0 + lax.erf(preact * root_half))
    normal_pdf = density_norm * jnp.exp(-0.5 * preact * preact)
    return (preact * normal_cdf, normal_cdf + preact * normal_pdf)


def select_row(table, chosen):
    return lax.dynamic_index_in_dim(table, chosen, 0, keepdims=False)


def pad_rows(x):
    return jnp.pad(x, ((1, 1), (0, 0), (0, 0)))


def conv_forward(padded, depth):
    height = padded.shape[0] - 2
    breadth = padded.shape[1] - 2
    acc = jnp.zeros((height, breadth, padded.shape[2]), jnp.float32)
    for i in range(3):
        for j in range(3):
            acc = acc + depth[i, j] * padded[i : i + height, j : j + breadth].astype(jnp.float32)
    return acc


def conv_backward(spread, depth):
    height = spread.shape[0] - 2
    breadth = spread.shape[1] - 2
    acc = jnp.zeros((height, breadth, spread.shape[2]), jnp.float32)
    for i in range(3):
        for j in range(3):
            acc = acc + depth[i, j] * spread[
                2 - i : 2 - i + height, 2 - j : 2 - j + breadth
            ].astype(jnp.float32)
    return acc


def torus_coords(b):
    y_size, z_size = lax.axis_size("y"), lax.axis_size("z")
    return (b // (y_size * z_size), lax.rem(b // y_size, z_size), lax.rem(b, y_size))


def exchange_kernel(held_ref, edges_ref, body_out, lo_out, hi_out, body, lo, hi, send_sem, recv_sem):
    core = lax.axis_index("pipe")
    count = blk_count()
    here = (lax.axis_index("x") * lax.axis_size("z") + lax.axis_index("z")) * lax.axis_size("y") + lax.axis_index("y")
    right = torus_coords(lax.rem(here + 1, count))
    left = torus_coords(lax.rem(here + count - 1, count))
    mine = torus_coords(here)
    partner = mine + (1 - core,)
    targets = [partner] + [right + (m,) for m in range(2)] + [left + (m,) for m in range(2)]

    barrier = pltpu.get_barrier_semaphore()
    for target in targets:
        pl.semaphore_signal(barrier, inc=1, device_id=target, device_id_type=MESH_ID)
    pl.semaphore_wait(barrier, len(targets))

    copies = [
        pltpu.make_async_remote_copy(
            src_ref=held_ref.at[1 - core], dst_ref=body,
            send_sem=send_sem.at[0], recv_sem=recv_sem.at[0],
            device_id=partner, device_id_type=MESH_ID,
        )
    ]
    for m in range(2):
        copies.append(pltpu.make_async_remote_copy(
            src_ref=edges_ref.at[1, m], dst_ref=lo.at[core],
            send_sem=send_sem.at[1 + m], recv_sem=recv_sem.at[1 + core],
            device_id=right + (m,), device_id_type=MESH_ID,
        ))
        copies.append(pltpu.make_async_remote_copy(
            src_ref=edges_ref.at[0, m], dst_ref=hi.at[core],
            send_sem=send_sem.at[3 + m], recv_sem=recv_sem.at[3 + core],
            device_id=left + (m,), device_id_type=MESH_ID,
        ))
    for copy in copies:
        copy.start()
    copies[0].wait_recv()
    for k in range(2):
        pltpu.make_async_remote_copy(
            src_ref=edges_ref.at[1, k], dst_ref=lo.at[k],
            send_sem=send_sem.at[1 + k], recv_sem=recv_sem.at[1 + k],
            device_id=right + (k,), device_id_type=MESH_ID,
        ).wait_recv()
        pltpu.make_async_remote_copy(
            src_ref=edges_ref.at[0, k], dst_ref=hi.at[k],
            send_sem=send_sem.at[3 + k], recv_sem=recv_sem.at[3 + k],
            device_id=left + (k,), device_id_type=MESH_ID,
        ).wait_recv()
    for copy in copies:
        copy.wait_send()
    body_out[...] = body[...]
    lo_out[...] = lo[...]
    hi_out[...] = hi[...]


def exchange(held, edges):
    grid_shape = held.shape[1:]
    strip_shape = edges.shape[2:]
    vmem = pl.BlockSpec(memory_space=pltpu.VMEM)
    return pl.pallas_call(
        exchange_kernel,
        out_shape=(
            jax.ShapeDtypeStruct(grid_shape, held.dtype),
            jax.ShapeDtypeStruct((2,) + strip_shape, held.dtype),
            jax.ShapeDtypeStruct((2,) + strip_shape, held.dtype),
        ),
        in_specs=[vmem, vmem],
        out_specs=(vmem, vmem, vmem),
        scratch_shapes=[
            pltpu.VMEM(grid_shape, held.dtype),
            pltpu.VMEM((2,) + strip_shape, held.dtype),
            pltpu.VMEM((2,) + strip_shape, held.dtype),
            pltpu.SemaphoreType.DMA((5,)),
            pltpu.SemaphoreType.DMA((5,)),
        ],
        compiler_params=pltpu.CompilerParams(collective_id=0, has_side_effects=True),
    )(held, edges)


def group_members(axis):
    here = [lax.axis_index(name) for name in BLK_AXES] + [lax.axis_index("pipe")]
    slot = BLK_AXES.index(axis)
    return [tuple(here[:slot]) + (j,) + tuple(here[slot + 1 :]) for j in range(lax.axis_size(axis))]


def tree_sum(values):
    while len(values) > 1:
        values = [values[k] + values[k + 1] for k in range(0, len(values), 2)]
    return values[0]


def reduce_kernel(flat_ref, out_ref, part, got_a, got_z, got_b,
                  send_sem, recv_a, recv_z, recv_b):
    core = lax.axis_index("pipe")
    my_y, my_z, my_x = (lax.axis_index(name) for name in ("y", "z", "x"))
    ny, nx = lax.axis_size("y"), lax.axis_size("x")
    row = [lax.axis_index(name) for name in BLK_AXES]
    groups = {
        "py": [(i, row[1], j, h) for h in range(2) for i in range(nx) for j in range(ny)],
        "z": group_members("z"),
    }
    places = {"py": (core * nx + my_x) * ny + my_y, "z": my_z}

    barrier = pltpu.get_barrier_semaphore()
    count = 0
    for axis in ("py", "z"):
        for j, member in enumerate(groups[axis]):
            @pl.when(j != places[axis])
            def _():
                pl.semaphore_signal(barrier, inc=1, device_id=member, device_id_type=MESH_ID)
        count += len(groups[axis]) - 1
    pl.semaphore_wait(barrier, count)

    sends = iter(range(send_sem.shape[0]))

    def spread(axis, src_of, dst, sems):
        mine = places[axis]
        copies = []
        for j, member in enumerate(groups[axis]):
            copy = pltpu.make_async_remote_copy(
                src_ref=src_of(j), dst_ref=dst.at[mine], send_sem=send_sem.at[next(sends)],
                recv_sem=sems.at[mine], device_id=member, device_id_type=MESH_ID,
            )
            copies.append((j, copy))

            @pl.when(j != mine)
            def _():
                copy.start()
        for j, copy in copies:
            @pl.when(j != mine)
            def _():
                copy.wait_send()
                pltpu.make_async_remote_copy(
                    src_ref=src_of(j), dst_ref=dst.at[j], send_sem=send_sem.at[0],
                    recv_sem=sems.at[j], device_id=groups[axis][j], device_id_type=MESH_ID,
                ).wait_recv()

    got_a[places["py"]] = flat_ref[places["py"]]
    spread("py", lambda j: flat_ref.at[j], got_a, recv_a)
    part[...] = tree_sum([got_a[k] for k in range(len(groups["py"]))])

    got_z[my_z] = part[...]
    spread("z", lambda j: part, got_z, recv_z)
    part[...] = tree_sum([got_z[k] for k in range(len(groups["z"]))])

    got_b[places["py"]] = part[...]
    spread("py", lambda j: part, got_b, recv_b)
    out_ref[...] = got_b[...]


def all_reduce(flat):
    chunks, rows, lanes = flat.shape
    nz = lax.axis_size("z")
    chunk = (rows, lanes)
    sends = chunks + nz + chunks
    vmem = pl.BlockSpec(memory_space=pltpu.VMEM)
    return pl.pallas_call(
        reduce_kernel,
        out_shape=jax.ShapeDtypeStruct(flat.shape, flat.dtype),
        in_specs=[vmem],
        out_specs=vmem,
        scratch_shapes=[
            pltpu.VMEM(chunk, flat.dtype),
            pltpu.VMEM((chunks,) + chunk, flat.dtype),
            pltpu.VMEM((nz,) + chunk, flat.dtype),
            pltpu.VMEM((chunks,) + chunk, flat.dtype),
            pltpu.SemaphoreType.DMA((sends,)),
            pltpu.SemaphoreType.DMA((chunks,)),
            pltpu.SemaphoreType.DMA((nz,)),
            pltpu.SemaphoreType.DMA((chunks,)),
        ],
        compiler_params=pltpu.CompilerParams(collective_id=1, has_side_effects=True),
    )(flat)


def shards(endpoints, row_counts, layer_order, depth_weight, point_weight, point_bias):
    held = endpoints[0]
    height = held.shape[1]
    breadth = held.shape[2]
    channels = held.shape[3]
    layers = layer_order.shape[0]
    core = lax.axis_index("pipe")

    edges = jnp.stack([held[:, :, :X_HALO], held[:, :, breadth - X_HALO :]])
    body, lo, hi = exchange(held, edges)
    x_in = jnp.where(core == 0, held[0], body)
    g_in = jnp.where(core == 0, body, held[1])
    x_wide = jnp.concatenate([lo[0], x_in, hi[0]], axis=1)
    g_wide = jnp.concatenate([lo[1][:, X_HALO - G_HALO :], g_in, hi[1][:, :G_HALO]], axis=1)

    both = (jnp.arange(height, dtype=row_counts.dtype)[:, None] < row_counts[None, :]).astype(jnp.float32)
    live = jnp.where(core == 0, both[:, 0], both[:, 1])[:, None, None]

    placed = layer_order[:, None] == jnp.arange(layers, dtype=layer_order.dtype)[None, :]

    def pick(table):
        mask = placed.reshape(placed.shape + (1,) * (table.ndim - 1))
        return jnp.sum(jnp.where(mask, table[None], jnp.zeros((), table.dtype)), axis=1, dtype=table.dtype)

    by_position = [pick(table) for table in (depth_weight, point_weight, point_bias)]
    weights = [tuple(table[p] for table in by_position) for p in range(layers)]

    activation = (x_wide.astype(jnp.float32) * live).astype(jnp.bfloat16)
    acts, mixes, preacts = [], [], []
    for p in range(layers):
        depth, point, offset_vec = weights[p]
        acts.append(activation)
        mixed = conv_forward(pad_rows(activation), depth).astype(jnp.bfloat16)
        rows, span = mixed.shape[0], mixed.shape[1]
        preact = jnp.dot(
            mixed.reshape(rows * span, channels), point, preferred_element_type=jnp.float32
        ).reshape(rows, span, channels) + offset_vec
        mixes.append(mixed)
        preacts.append(preact)
        activation = (
            (activation[:, 1:-1].astype(jnp.float32) + gelu_pair(preact)[0]) * live
        ).astype(jnp.bfloat16)
    final_halo = X_HALO - layers
    outcome = activation[:, final_halo : final_halo + breadth]

    cotangent = g_wide
    depth_terms, point_terms, bias_terms = [None] * layers, [None] * layers, [None] * layers
    for p in range(layers - 1, -1, -1):
        depth, point, _ = weights[p]
        halo_c = (cotangent.shape[1] - breadth) // 2
        halo_p = (preacts[p].shape[1] - breadth) // 2
        shift = halo_p - halo_c
        span = cotangent.shape[1]
        preact = preacts[p][:, shift : shift + span]
        masked = cotangent.astype(jnp.float32) * live
        gated = (masked * gelu_pair(preact)[1]).astype(jnp.bfloat16)
        back_mix = lax.dot_general(
            gated.reshape(height * span, channels),
            point,
            (((1,), (1,)), ((), ())),
            preferred_element_type=jnp.float32,
        ).reshape(height, span, channels).astype(jnp.bfloat16)

        gate_in = gated[:, halo_c : halo_c + breadth].reshape(height * breadth, channels)
        mix_in = mixes[p][:, halo_p : halo_p + breadth].reshape(height * breadth, channels)
        point_terms[p] = lax.dot_general(
            mix_in, gate_in, (((0,), (0,)), ((), ())), preferred_element_type=jnp.float32
        )
        bias_terms[p] = jnp.sum(gate_in.astype(jnp.float32), axis=0)
        back_in = back_mix[:, halo_c : halo_c + breadth].astype(jnp.float32)
        padded = pad_rows(acts[p])
        halo_a = (acts[p].shape[1] - breadth) // 2
        rows_k = []
        for i in range(3):
            row_k = []
            for j in range(3):
                start = halo_a - 1 + j
                row_k.append(
                    jnp.sum(
                        back_in * padded[i : i + height, start : start + breadth].astype(jnp.float32),
                        axis=(0, 1),
                    )
                )
            rows_k.append(jnp.stack(row_k))
        depth_terms[p] = jnp.stack(rows_k)

        earlier = conv_backward(pad_rows(back_mix), depth)
        cotangent = ((masked[:, 1:-1] + earlier) * live).astype(jnp.bfloat16)
    input_grad = cotangent

    got_outcome = lax.ppermute(outcome, "pipe", [(0, 1)])
    got_grad = lax.ppermute(input_grad, "pipe", [(1, 0)])
    result = jnp.where(
        core == 0, jnp.stack([input_grad, got_grad]), jnp.stack([got_outcome, outcome])
    )[None]

    pieces = (jnp.stack(depth_terms), jnp.stack(point_terms), jnp.stack(bias_terms))
    flat = jnp.concatenate([piece.reshape(layers, -1) for piece in pieces], axis=1)
    chunks = 2 * lax.axis_size("y") * lax.axis_size("x")
    size = flat.size
    rows = -(-size // (chunks * 128))
    rows = -(-rows // 8) * 8
    packed = jnp.pad(flat.reshape(-1), (0, chunks * rows * 128 - size)).reshape(chunks, rows, 128)
    flat = all_reduce(packed).reshape(-1)[:size].reshape(flat.shape)
    factor = 1.0 / math.sqrt(held.shape[0] * height * breadth * blk_count())
    chosen = layer_order[None, :] == jnp.arange(layers, dtype=layer_order.dtype)[:, None]
    flat = jnp.sum(jnp.where(chosen[:, :, None], flat[None, :, :], 0.0), axis=1) * factor
    ordered, at = [], 0
    for piece in pieces:
        width = piece[0].size
        ordered.append(flat[:, at : at + width].reshape(piece.shape))
        at += width
    return (result, ordered[0], ordered[1], ordered[2])


def solution(mesh):
    devices = mesh.devices
    blk = devices.shape[0]
    y_size = 4 if blk % 4 == 0 else 1
    rest = blk // y_size
    z_size = 8 if rest % 8 == 0 else rest
    x_size = rest // z_size
    torus = Mesh(devices.reshape(x_size, z_size, y_size, devices.shape[1]), BLK_AXES + ("pipe",))
    spec = P("pipe", None, None, BLK_AXES, None)
    in_specs = (spec, P(), P(), P(), P(), P())
    out_specs = (spec, P(), P(), P())
    return jax.shard_map(shards, mesh=torus, in_specs=in_specs, out_specs=out_specs, check_vma=False)
```

```python
import math

import jax
import jax.numpy as jnp
from jax import lax
from jax.experimental import pallas as pl
from jax.experimental.pallas import tpu as pltpu
from jax.sharding import Mesh, PartitionSpec as P

MESH_ID = pl.DeviceIdType.MESH

root_half = 0.7071067811865476
density_norm = 0.3989422804014327

X_HALO = 8
G_HALO = 4


BLK_AXES = ("x", "z", "y")


def blk_count():
    count = 1
    for axis in BLK_AXES:
        count *= lax.axis_size(axis)
    return count


def gelu_pair(preact):
    normal_cdf = 0.5 * (1.0 + lax.erf(preact * root_half))
    normal_pdf = density_norm * jnp.exp(-0.5 * preact * preact)
    return (preact * normal_cdf, normal_cdf + preact * normal_pdf)


def select_row(table, chosen):
    return lax.dynamic_index_in_dim(table, chosen, 0, keepdims=False)


def pad_rows(x):
    return jnp.pad(x, ((1, 1), (0, 0), (0, 0)))


def conv_forward(padded, depth):
    height = padded.shape[0] - 2
    breadth = padded.shape[1] - 2
    acc = jnp.zeros((height, breadth, padded.shape[2]), jnp.float32)
    for i in range(3):
        for j in range(3):
            acc = acc + depth[i, j] * padded[i : i + height, j : j + breadth].astype(jnp.float32)
    return acc


def conv_backward(spread, depth):
    height = spread.shape[0] - 2
    breadth = spread.shape[1] - 2
    acc = jnp.zeros((height, breadth, spread.shape[2]), jnp.float32)
    for i in range(3):
        for j in range(3):
            acc = acc + depth[i, j] * spread[
                2 - i : 2 - i + height, 2 - j : 2 - j + breadth
            ].astype(jnp.float32)
    return acc


def torus_coords(b):
    y_size, z_size = lax.axis_size("y"), lax.axis_size("z")
    return (b // (y_size * z_size), lax.rem(b // y_size, z_size), lax.rem(b, y_size))


def exchange_kernel(held_ref, edges_ref, body_out, lo_out, hi_out, body, lo, hi, send_sem, recv_sem):
    core = lax.axis_index("pipe")
    count = blk_count()
    here = (lax.axis_index("x") * lax.axis_size("z") + lax.axis_index("z")) * lax.axis_size("y") + lax.axis_index("y")
    right = torus_coords(lax.rem(here + 1, count))
    left = torus_coords(lax.rem(here + count - 1, count))
    mine = torus_coords(here)
    partner = mine + (1 - core,)
    targets = [partner] + [right + (m,) for m in range(2)] + [left + (m,) for m in range(2)]

    barrier = pltpu.get_barrier_semaphore()
    for target in targets:
        pl.semaphore_signal(barrier, inc=1, device_id=target, device_id_type=MESH_ID)
    pl.semaphore_wait(barrier, len(targets))

    copies = [
        pltpu.make_async_remote_copy(
            src_ref=held_ref.at[1 - core], dst_ref=body,
            send_sem=send_sem.at[0], recv_sem=recv_sem.at[0],
            device_id=partner, device_id_type=MESH_ID,
        )
    ]
    for m in range(2):
        copies.append(pltpu.make_async_remote_copy(
            src_ref=edges_ref.at[1, m], dst_ref=lo.at[core],
            send_sem=send_sem.at[1 + m], recv_sem=recv_sem.at[1 + core],
            device_id=right + (m,), device_id_type=MESH_ID,
        ))
        copies.append(pltpu.make_async_remote_copy(
            src_ref=edges_ref.at[0, m], dst_ref=hi.at[core],
            send_sem=send_sem.at[3 + m], recv_sem=recv_sem.at[3 + core],
            device_id=left + (m,), device_id_type=MESH_ID,
        ))
    for copy in copies:
        copy.start()
    copies[0].wait_recv()
    for k in range(2):
        pltpu.make_async_remote_copy(
            src_ref=edges_ref.at[1, k], dst_ref=lo.at[k],
            send_sem=send_sem.at[1 + k], recv_sem=recv_sem.at[1 + k],
            device_id=right + (k,), device_id_type=MESH_ID,
        ).wait_recv()
        pltpu.make_async_remote_copy(
            src_ref=edges_ref.at[0, k], dst_ref=hi.at[k],
            send_sem=send_sem.at[3 + k], recv_sem=recv_sem.at[3 + k],
            device_id=left + (k,), device_id_type=MESH_ID,
        ).wait_recv()
    for copy in copies:
        copy.wait_send()
    body_out[...] = body[...]
    lo_out[...] = lo[...]
    hi_out[...] = hi[...]


def exchange(held, edges):
    grid_shape = held.shape[1:]
    strip_shape = edges.shape[2:]
    vmem = pl.BlockSpec(memory_space=pltpu.VMEM)
    return pl.pallas_call(
        exchange_kernel,
        out_shape=(
            jax.ShapeDtypeStruct(grid_shape, held.dtype),
            jax.ShapeDtypeStruct((2,) + strip_shape, held.dtype),
            jax.ShapeDtypeStruct((2,) + strip_shape, held.dtype),
        ),
        in_specs=[vmem, vmem],
        out_specs=(vmem, vmem, vmem),
        scratch_shapes=[
            pltpu.VMEM(grid_shape, held.dtype),
            pltpu.VMEM((2,) + strip_shape, held.dtype),
            pltpu.VMEM((2,) + strip_shape, held.dtype),
            pltpu.SemaphoreType.DMA((5,)),
            pltpu.SemaphoreType.DMA((5,)),
        ],
        compiler_params=pltpu.CompilerParams(collective_id=0, has_side_effects=True),
    )(held, edges)


def group_members(axis):
    here = [lax.axis_index(name) for name in BLK_AXES] + [lax.axis_index("pipe")]
    slot = BLK_AXES.index(axis)
    return [tuple(here[:slot]) + (j,) + tuple(here[slot + 1 :]) for j in range(lax.axis_size(axis))]


def tree_sum(values):
    while len(values) > 1:
        values = [values[k] + values[k + 1] for k in range(0, len(values), 2)]
    return values[0]


def reduce_kernel(flat_ref, out_ref, part, got_a, got_z, got_b,
                  send_sem, recv_a, recv_z, recv_b):
    core = lax.axis_index("pipe")
    my_y, my_z, my_x = (lax.axis_index(name) for name in ("y", "z", "x"))
    ny, nx = lax.axis_size("y"), lax.axis_size("x")
    row = [lax.axis_index(name) for name in BLK_AXES]
    groups = {
        "py": [(i, row[1], j, h) for h in range(2) for i in range(nx) for j in range(ny)],
        "z": group_members("z"),
    }
    places = {"py": (core * nx + my_x) * ny + my_y, "z": my_z}

    barrier = pltpu.get_barrier_semaphore()
    count = 0
    for axis in ("py", "z"):
        for j, member in enumerate(groups[axis]):
            @pl.when(j != places[axis])
            def _():
                pl.semaphore_signal(barrier, inc=1, device_id=member, device_id_type=MESH_ID)
        count += len(groups[axis]) - 1
    pl.semaphore_wait(barrier, count)

    sends = iter(range(send_sem.shape[0]))

    def spread(axis, src_of, dst, sems):
        mine = places[axis]
        copies = []
        for j, member in enumerate(groups[axis]):
            copy = pltpu.make_async_remote_copy(
                src_ref=src_of(j), dst_ref=dst.at[mine], send_sem=send_sem.at[next(sends)],
                recv_sem=sems.at[mine], device_id=member, device_id_type=MESH_ID,
            )
            copies.append((j, copy))

            @pl.when(j != mine)
            def _():
                copy.start()
        for j, copy in copies:
            @pl.when(j != mine)
            def _():
                copy.wait_send()
                pltpu.make_async_remote_copy(
                    src_ref=src_of(j), dst_ref=dst.at[j], send_sem=send_sem.at[0],
                    recv_sem=sems.at[j], device_id=groups[axis][j], device_id_type=MESH_ID,
                ).wait_recv()

    got_a[places["py"]] = flat_ref[places["py"]]
    spread("py", lambda j: flat_ref.at[j], got_a, recv_a)
    part[...] = tree_sum([got_a[k] for k in range(len(groups["py"]))])

    got_z[my_z] = part[...]
    spread("z", lambda j: part, got_z, recv_z)
    part[...] = tree_sum([got_z[k] for k in range(len(groups["z"]))])

    got_b[places["py"]] = part[...]
    spread("py", lambda j: part, got_b, recv_b)
    out_ref[...] = got_b[...]


def all_reduce(flat):
    chunks, rows, lanes = flat.shape
    nz = lax.axis_size("z")
    chunk = (rows, lanes)
    sends = chunks + nz + chunks
    vmem = pl.BlockSpec(memory_space=pltpu.VMEM)
    return pl.pallas_call(
        reduce_kernel,
        out_shape=jax.ShapeDtypeStruct(flat.shape, flat.dtype),
        in_specs=[vmem],
        out_specs=vmem,
        scratch_shapes=[
            pltpu.VMEM(chunk, flat.dtype),
            pltpu.VMEM((chunks,) + chunk, flat.dtype),
            pltpu.VMEM((nz,) + chunk, flat.dtype),
            pltpu.VMEM((chunks,) + chunk, flat.dtype),
            pltpu.SemaphoreType.DMA((sends,)),
            pltpu.SemaphoreType.DMA((chunks,)),
            pltpu.SemaphoreType.DMA((nz,)),
            pltpu.SemaphoreType.DMA((chunks,)),
        ],
        compiler_params=pltpu.CompilerParams(collective_id=1, has_side_effects=True),
    )(flat)


def shards(endpoints, row_counts, layer_order, depth_weight, point_weight, point_bias):
    held = endpoints[0]
    height = held.shape[1]
    breadth = held.shape[2]
    channels = held.shape[3]
    layers = layer_order.shape[0]
    core = lax.axis_index("pipe")

    edges = jnp.stack([held[:, :, :X_HALO], held[:, :, breadth - X_HALO :]])
    body, lo, hi = exchange(held, edges)
    x_wide = jnp.where(
        core == 0,
        jnp.concatenate([lo[0], held[0], hi[0]], axis=1),
        jnp.concatenate([lo[0], body, hi[0]], axis=1),
    )
    g_lo, g_hi = lo[1][:, X_HALO - G_HALO :], hi[1][:, :G_HALO]
    g_wide = jnp.where(
        core == 0,
        jnp.concatenate([g_lo, body, g_hi], axis=1),
        jnp.concatenate([g_lo, held[1], g_hi], axis=1),
    )

    both = (jnp.arange(height, dtype=row_counts.dtype)[:, None] < row_counts[None, :]).astype(jnp.float32)
    live = jnp.where(core == 0, both[:, 0], both[:, 1])[:, None, None]

    placed = layer_order[:, None] == jnp.arange(layers, dtype=layer_order.dtype)[None, :]

    def pick(table):
        mask = placed.reshape(placed.shape + (1,) * (table.ndim - 1))
        return jnp.sum(jnp.where(mask, table[None], jnp.zeros((), table.dtype)), axis=1, dtype=table.dtype)

    by_position = [pick(table) for table in (depth_weight, point_weight, point_bias)]
    weights = [tuple(table[p] for table in by_position) for p in range(layers)]

    activation = (x_wide.astype(jnp.float32) * live).astype(jnp.bfloat16)
    acts, mixes, preacts = [], [], []
    for p in range(layers):
        depth, point, offset_vec = weights[p]
        acts.append(activation)
        mixed = conv_forward(pad_rows(activation), depth).astype(jnp.bfloat16)
        rows, span = mixed.shape[0], mixed.shape[1]
        preact = jnp.dot(
            mixed.reshape(rows * span, channels), point, preferred_element_type=jnp.float32
        ).reshape(rows, span, channels) + offset_vec
        mixes.append(mixed)
        preacts.append(preact)
        activation = (
            (activation[:, 1:-1].astype(jnp.float32) + gelu_pair(preact)[0]) * live
        ).astype(jnp.bfloat16)
    final_halo = X_HALO - layers
    outcome = activation[:, final_halo : final_halo + breadth]

    cotangent = g_wide
    depth_terms, point_terms, bias_terms = [None] * layers, [None] * layers, [None] * layers
    for p in range(layers - 1, -1, -1):
        depth, point, _ = weights[p]
        halo_c = (cotangent.shape[1] - breadth) // 2
        halo_p = (preacts[p].shape[1] - breadth) // 2
        shift = halo_p - halo_c
        span = cotangent.shape[1]
        preact = preacts[p][:, shift : shift + span]
        masked = cotangent.astype(jnp.float32) * live
        gated = (masked * gelu_pair(preact)[1]).astype(jnp.bfloat16)
        back_mix = lax.dot_general(
            gated.reshape(height * span, channels),
            point,
            (((1,), (1,)), ((), ())),
            preferred_element_type=jnp.float32,
        ).reshape(height, span, channels).astype(jnp.bfloat16)

        gate_in = gated[:, halo_c : halo_c + breadth].reshape(height * breadth, channels)
        mix_in = mixes[p][:, halo_p : halo_p + breadth].reshape(height * breadth, channels)
        point_terms[p] = lax.dot_general(
            mix_in, gate_in, (((0,), (0,)), ((), ())), preferred_element_type=jnp.float32
        )
        bias_terms[p] = jnp.sum(gate_in.astype(jnp.float32), axis=0)
        back_in = back_mix[:, halo_c : halo_c + breadth].astype(jnp.float32)
        padded = pad_rows(acts[p])
        halo_a = (acts[p].shape[1] - breadth) // 2
        rows_k = []
        for i in range(3):
            row_k = []
            for j in range(3):
                start = halo_a - 1 + j
                row_k.append(
                    jnp.sum(
                        back_in * padded[i : i + height, start : start + breadth].astype(jnp.float32),
                        axis=(0, 1),
                    )
                )
            rows_k.append(jnp.stack(row_k))
        depth_terms[p] = jnp.stack(rows_k)

        earlier = conv_backward(pad_rows(back_mix), depth)
        cotangent = ((masked[:, 1:-1] + earlier) * live).astype(jnp.bfloat16)
    input_grad = cotangent

    got_outcome = lax.ppermute(outcome, "pipe", [(0, 1)])
    got_grad = lax.ppermute(input_grad, "pipe", [(1, 0)])
    result = jnp.where(
        core == 0, jnp.stack([input_grad, got_grad]), jnp.stack([got_outcome, outcome])
    )[None]

    pieces = (jnp.stack(depth_terms), jnp.stack(point_terms), jnp.stack(bias_terms))
    flat = jnp.concatenate([piece.reshape(layers, -1) for piece in pieces], axis=1)
    chunks = 2 * lax.axis_size("y") * lax.axis_size("x")
    size = flat.size
    rows = -(-size // (chunks * 128))
    rows = -(-rows // 8) * 8
    packed = jnp.pad(flat.reshape(-1), (0, chunks * rows * 128 - size)).reshape(chunks, rows, 128)
    flat = all_reduce(packed).reshape(-1)[:size].reshape(flat.shape)
    factor = 1.0 / math.sqrt(held.shape[0] * height * breadth * blk_count())
    chosen = layer_order[None, :] == jnp.arange(layers, dtype=layer_order.dtype)[:, None]
    flat = jnp.sum(jnp.where(chosen[:, :, None], flat[None, :, :], 0.0), axis=1) * factor
    ordered, at = [], 0
    for piece in pieces:
        width = piece[0].size
        ordered.append(flat[:, at : at + width].reshape(piece.shape))
        at += width
    return (result, ordered[0], ordered[1], ordered[2])


def solution(mesh):
    devices = mesh.devices
    blk = devices.shape[0]
    y_size = 4 if blk % 4 == 0 else 1
    rest = blk // y_size
    z_size = 8 if rest % 8 == 0 else rest
    x_size = rest // z_size
    torus = Mesh(devices.reshape(x_size, z_size, y_size, devices.shape[1]), BLK_AXES + ("pipe",))
    spec = P("pipe", None, None, BLK_AXES, None)
    in_specs = (spec, P(), P(), P(), P(), P())
    out_specs = (spec, P(), P(), P())
    return jax.shard_map(shards, mesh=torus, in_specs=in_specs, out_specs=out_specs, check_vma=False)
```

```python
import math

import jax
import jax.numpy as jnp
from jax import lax
from jax.experimental import pallas as pl
from jax.experimental.pallas import tpu as pltpu
from jax.sharding import Mesh, PartitionSpec as P

MESH_ID = pl.DeviceIdType.MESH

root_half = 0.7071067811865476
density_norm = 0.3989422804014327

X_HALO = 8
G_HALO = 4


BLK_AXES = ("x", "z", "y")


def blk_count():
    count = 1
    for axis in BLK_AXES:
        count *= lax.axis_size(axis)
    return count


def gelu_pair(preact):
    normal_cdf = 0.5 * (1.0 + lax.erf(preact * root_half))
    normal_pdf = density_norm * jnp.exp(-0.5 * preact * preact)
    return (preact * normal_cdf, normal_cdf + preact * normal_pdf)


def select_row(table, chosen):
    return lax.dynamic_index_in_dim(table, chosen, 0, keepdims=False)


def pad_rows(x):
    return jnp.pad(x, ((1, 1), (0, 0), (0, 0)))


def conv_forward(padded, depth):
    height = padded.shape[0] - 2
    breadth = padded.shape[1] - 2
    acc = jnp.zeros((height, breadth, padded.shape[2]), jnp.float32)
    for i in range(3):
        for j in range(3):
            acc = acc + depth[i, j] * padded[i : i + height, j : j + breadth].astype(jnp.float32)
    return acc


def conv_backward(spread, depth):
    height = spread.shape[0] - 2
    breadth = spread.shape[1] - 2
    acc = jnp.zeros((height, breadth, spread.shape[2]), jnp.float32)
    for i in range(3):
        for j in range(3):
            acc = acc + depth[i, j] * spread[
                2 - i : 2 - i + height, 2 - j : 2 - j + breadth
            ].astype(jnp.float32)
    return acc


def torus_coords(b):
    y_size, z_size = lax.axis_size("y"), lax.axis_size("z")
    return (b // (y_size * z_size), lax.rem(b // y_size, z_size), lax.rem(b, y_size))


def exchange_kernel(held_ref, edges_ref, body_out, lo_out, hi_out, body, lo, hi, send_sem, recv_sem):
    core = lax.axis_index("pipe")
    count = blk_count()
    here = (lax.axis_index("x") * lax.axis_size("z") + lax.axis_index("z")) * lax.axis_size("y") + lax.axis_index("y")
    right = torus_coords(lax.rem(here + 1, count))
    left = torus_coords(lax.rem(here + count - 1, count))
    mine = torus_coords(here)
    partner = mine + (1 - core,)
    targets = [partner] + [right + (m,) for m in range(2)] + [left + (m,) for m in range(2)]

    barrier = pltpu.get_barrier_semaphore()
    for target in targets:
        pl.semaphore_signal(barrier, inc=1, device_id=target, device_id_type=MESH_ID)
    pl.semaphore_wait(barrier, len(targets))

    copies = [
        pltpu.make_async_remote_copy(
            src_ref=held_ref.at[1 - core], dst_ref=body,
            send_sem=send_sem.at[0], recv_sem=recv_sem.at[0],
            device_id=partner, device_id_type=MESH_ID,
        )
    ]
    for m in range(2):
        copies.append(pltpu.make_async_remote_copy(
            src_ref=edges_ref.at[1, m], dst_ref=lo.at[core],
            send_sem=send_sem.at[1 + m], recv_sem=recv_sem.at[1 + core],
            device_id=right + (m,), device_id_type=MESH_ID,
        ))
        copies.append(pltpu.make_async_remote_copy(
            src_ref=edges_ref.at[0, m], dst_ref=hi.at[core],
            send_sem=send_sem.at[3 + m], recv_sem=recv_sem.at[3 + core],
            device_id=left + (m,), device_id_type=MESH_ID,
        ))
    for copy in copies:
        copy.start()
    copies[0].wait_recv()
    for k in range(2):
        pltpu.make_async_remote_copy(
            src_ref=edges_ref.at[1, k], dst_ref=lo.at[k],
            send_sem=send_sem.at[1 + k], recv_sem=recv_sem.at[1 + k],
            device_id=right + (k,), device_id_type=MESH_ID,
        ).wait_recv()
        pltpu.make_async_remote_copy(
            src_ref=edges_ref.at[0, k], dst_ref=hi.at[k],
            send_sem=send_sem.at[3 + k], recv_sem=recv_sem.at[3 + k],
            device_id=left + (k,), device_id_type=MESH_ID,
        ).wait_recv()
    for copy in copies:
        copy.wait_send()
    body_out[...] = body[...]
    lo_out[...] = lo[...]
    hi_out[...] = hi[...]


def exchange(held, edges):
    grid_shape = held.shape[1:]
    strip_shape = edges.shape[2:]
    vmem = pl.BlockSpec(memory_space=pltpu.VMEM)
    return pl.pallas_call(
        exchange_kernel,
        out_shape=(
            jax.ShapeDtypeStruct(grid_shape, held.dtype),
            jax.ShapeDtypeStruct((2,) + strip_shape, held.dtype),
            jax.ShapeDtypeStruct((2,) + strip_shape, held.dtype),
        ),
        in_specs=[vmem, vmem],
        out_specs=(vmem, vmem, vmem),
        scratch_shapes=[
            pltpu.VMEM(grid_shape, held.dtype),
            pltpu.VMEM((2,) + strip_shape, held.dtype),
            pltpu.VMEM((2,) + strip_shape, held.dtype),
            pltpu.SemaphoreType.DMA((5,)),
            pltpu.SemaphoreType.DMA((5,)),
        ],
        compiler_params=pltpu.CompilerParams(collective_id=0, has_side_effects=True),
    )(held, edges)


def group_members(axis):
    here = [lax.axis_index(name) for name in BLK_AXES] + [lax.axis_index("pipe")]
    slot = BLK_AXES.index(axis)
    return [tuple(here[:slot]) + (j,) + tuple(here[slot + 1 :]) for j in range(lax.axis_size(axis))]


def tree_sum(values):
    while len(values) > 1:
        values = [values[k] + values[k + 1] for k in range(0, len(values), 2)]
    return values[0]


def reduce_kernel(flat_ref, out_ref, part, got_a, got_z, got_b,
                  send_sem, recv_a, recv_z, recv_b):
    core = lax.axis_index("pipe")
    my_y, my_z, my_x = (lax.axis_index(name) for name in ("y", "z", "x"))
    ny, nx = lax.axis_size("y"), lax.axis_size("x")
    row = [lax.axis_index(name) for name in BLK_AXES]
    groups = {
        "py": [(i, row[1], j, h) for h in range(2) for i in range(nx) for j in range(ny)],
        "z": group_members("z"),
    }
    places = {"py": (core * nx + my_x) * ny + my_y, "z": my_z}

    barrier = pltpu.get_barrier_semaphore()
    count = 0
    for axis in ("py", "z"):
        for j, member in enumerate(groups[axis]):
            @pl.when(j != places[axis])
            def _():
                pl.semaphore_signal(barrier, inc=1, device_id=member, device_id_type=MESH_ID)
        count += len(groups[axis]) - 1
    pl.semaphore_wait(barrier, count)

    sends = iter(range(send_sem.shape[0]))

    def spread(axis, src_of, dst, sems):
        mine = places[axis]
        copies = []
        for j, member in enumerate(groups[axis]):
            copy = pltpu.make_async_remote_copy(
                src_ref=src_of(j), dst_ref=dst.at[mine], send_sem=send_sem.at[next(sends)],
                recv_sem=sems.at[mine], device_id=member, device_id_type=MESH_ID,
            )
            copies.append((j, copy))

            @pl.when(j != mine)
            def _():
                copy.start()
        for j, copy in copies:
            @pl.when(j != mine)
            def _():
                copy.wait_send()
                pltpu.make_async_remote_copy(
                    src_ref=src_of(j), dst_ref=dst.at[j], send_sem=send_sem.at[0],
                    recv_sem=sems.at[j], device_id=groups[axis][j], device_id_type=MESH_ID,
                ).wait_recv()

    got_a[places["py"]] = flat_ref[places["py"]]
    spread("py", lambda j: flat_ref.at[j], got_a, recv_a)
    part[...] = tree_sum([got_a[k] for k in range(len(groups["py"]))])

    got_z[my_z] = part[...]
    spread("z", lambda j: part, got_z, recv_z)
    part[...] = tree_sum([got_z[k] for k in range(len(groups["z"]))])

    got_b[places["py"]] = part[...]
    spread("py", lambda j: part, got_b, recv_b)
    out_ref[...] = got_b[...]


def all_reduce(flat):
    chunks, rows, lanes = flat.shape
    nz = lax.axis_size("z")
    chunk = (rows, lanes)
    sends = chunks + nz + chunks
    vmem = pl.BlockSpec(memory_space=pltpu.VMEM)
    return pl.pallas_call(
        reduce_kernel,
        out_shape=jax.ShapeDtypeStruct(flat.shape, flat.dtype),
        in_specs=[vmem],
        out_specs=vmem,
        scratch_shapes=[
            pltpu.VMEM(chunk, flat.dtype),
            pltpu.VMEM((chunks,) + chunk, flat.dtype),
            pltpu.VMEM((nz,) + chunk, flat.dtype),
            pltpu.VMEM((chunks,) + chunk, flat.dtype),
            pltpu.SemaphoreType.DMA((sends,)),
            pltpu.SemaphoreType.DMA((chunks,)),
            pltpu.SemaphoreType.DMA((nz,)),
            pltpu.SemaphoreType.DMA((chunks,)),
        ],
        compiler_params=pltpu.CompilerParams(collective_id=1, has_side_effects=True),
    )(flat)


def shards(endpoints, row_counts, layer_order, depth_weight, point_weight, point_bias):
    held = endpoints[0]
    height = held.shape[1]
    breadth = held.shape[2]
    channels = held.shape[3]
    layers = layer_order.shape[0]
    core = lax.axis_index("pipe")

    edges = jnp.stack([held[:, :, :X_HALO], held[:, :, breadth - X_HALO :]])
    body, lo, hi = exchange(held, edges)
    x_in = jnp.where(core == 0, held[0], body)
    g_in = jnp.where(core == 0, body, held[1])
    x_wide = jnp.concatenate([lo[0], x_in, hi[0]], axis=1)
    g_wide = jnp.concatenate([lo[1][:, X_HALO - G_HALO :], g_in, hi[1][:, :G_HALO]], axis=1)

    both = (jnp.arange(height, dtype=row_counts.dtype)[:, None] < row_counts[None, :]).astype(jnp.float32)
    live = jnp.where(core == 0, both[:, 0], both[:, 1])[:, None, None]

    placed = layer_order[:, None] == jnp.arange(layers, dtype=layer_order.dtype)[None, :]

    def pick(table):
        mask = placed.reshape(placed.shape + (1,) * (table.ndim - 1))
        return jnp.sum(jnp.where(mask, table[None], jnp.zeros((), table.dtype)), axis=1, dtype=table.dtype)

    by_position = [pick(table) for table in (depth_weight, point_weight, point_bias)]
    weights = [tuple(table[p] for table in by_position) for p in range(layers)]

    activation = (x_wide.astype(jnp.float32) * live).astype(jnp.bfloat16)
    acts, mixes, preacts = [], [], []
    for p in range(layers):
        depth, point, offset_vec = weights[p]
        acts.append(activation)
        mixed = conv_forward(pad_rows(activation), depth).astype(jnp.bfloat16)
        rows, span = mixed.shape[0], mixed.shape[1]
        preact = jnp.dot(
            mixed.reshape(rows * span, channels), point, preferred_element_type=jnp.float32
        ).reshape(rows, span, channels) + offset_vec
        mixes.append(mixed)
        preacts.append(preact)
        activation = (
            (activation[:, 1:-1].astype(jnp.float32) + gelu_pair(preact)[0]) * live
        ).astype(jnp.bfloat16)
    final_halo = X_HALO - layers
    outcome = activation[:, final_halo : final_halo + breadth]

    cotangent = g_wide
    depth_terms, point_terms, bias_terms = [None] * layers, [None] * layers, [None] * layers
    for p in range(layers - 1, -1, -1):
        depth, point, _ = weights[p]
        halo_c = (cotangent.shape[1] - breadth) // 2
        halo_p = (preacts[p].shape[1] - breadth) // 2
        shift = halo_p - halo_c
        span = cotangent.shape[1]
        preact = preacts[p][:, shift : shift + span]
        masked = cotangent.astype(jnp.float32) * live
        gated = (masked * gelu_pair(preact)[1]).astype(jnp.bfloat16)
        back_mix = lax.dot_general(
            gated.reshape(height * span, channels),
            point,
            (((1,), (1,)), ((), ())),
            preferred_element_type=jnp.float32,
        ).reshape(height, span, channels).astype(jnp.bfloat16)

        gate_in = gated[:, halo_c : halo_c + breadth].reshape(height * breadth, channels)
        mix_in = mixes[p][:, halo_p : halo_p + breadth].reshape(height * breadth, channels)
        point_terms[p] = lax.dot_general(
            mix_in, gate_in, (((0,), (0,)), ((), ())), preferred_element_type=jnp.float32
        )
        bias_terms[p] = jnp.sum(gate_in.astype(jnp.float32), axis=0)
        back_in = back_mix[:, halo_c : halo_c + breadth].astype(jnp.float32)
        padded = pad_rows(acts[p])
        halo_a = (acts[p].shape[1] - breadth) // 2
        rows_k = []
        for i in range(3):
            row_k = []
            for j in range(3):
                start = halo_a - 1 + j
                row_k.append(
                    jnp.sum(
                        back_in * padded[i : i + height, start : start + breadth].astype(jnp.float32),
                        axis=(0, 1),
                    )
                )
            rows_k.append(jnp.stack(row_k))
        depth_terms[p] = jnp.stack(rows_k)

        earlier = conv_backward(pad_rows(back_mix), depth)
        cotangent = ((masked[:, 1:-1] + earlier) * live).astype(jnp.bfloat16)
    input_grad = cotangent

    got_outcome = lax.ppermute(outcome, "pipe", [(0, 1)])
    got_grad = lax.ppermute(input_grad, "pipe", [(1, 0)])
    result = jnp.where(
        core == 0, jnp.stack([input_grad, got_grad]), jnp.stack([got_outcome, outcome])
    )[None]

    pieces = (jnp.stack(depth_terms), jnp.stack(point_terms), jnp.stack(bias_terms))
    flat = jnp.concatenate([piece.reshape(layers, -1) for piece in pieces], axis=1)
    chosen = layer_order[None, :] == jnp.arange(layers, dtype=layer_order.dtype)[:, None]
    flat = jnp.sum(jnp.where(chosen[:, :, None], flat[None, :, :], 0.0), axis=1)
    chunks = 2 * lax.axis_size("y") * lax.axis_size("x")
    size = flat.size
    rows = -(-size // (chunks * 128))
    rows = -(-rows // 8) * 8
    packed = jnp.pad(flat.reshape(-1), (0, chunks * rows * 128 - size)).reshape(chunks, rows, 128)
    flat = all_reduce(packed).reshape(-1)[:size].reshape(flat.shape)
    factor = 1.0 / math.sqrt(held.shape[0] * height * breadth * blk_count())
    flat = flat * factor
    ordered, at = [], 0
    for piece in pieces:
        width = piece[0].size
        ordered.append(flat[:, at : at + width].reshape(piece.shape))
        at += width
    return (result, ordered[0], ordered[1], ordered[2])


def solution(mesh):
    devices = mesh.devices
    blk = devices.shape[0]
    y_size = 4 if blk % 4 == 0 else 1
    rest = blk // y_size
    z_size = 8 if rest % 8 == 0 else rest
    x_size = rest // z_size
    torus = Mesh(devices.reshape(x_size, z_size, y_size, devices.shape[1]), BLK_AXES + ("pipe",))
    spec = P("pipe", None, None, BLK_AXES, None)
    in_specs = (spec, P(), P(), P(), P(), P())
    out_specs = (spec, P(), P(), P())
    return jax.shard_map(shards, mesh=torus, in_specs=in_specs, out_specs=out_specs, check_vma=False)
```
